256 devices in a mesh: seq: 64 (over y_lo, x, z), head: 4 (over y_hi, core).
Axes of the slice: x: 4, y: 4 (y_hi: 2, y_lo: 2; y = y_hi * 2 + y_lo), z: 8, core: 2. Of those that a mesh axis runs over, the one named last changes fastest.
Arguments:
- linear_query_rows: bfloat16 [8192, 64, 128], P('seq', 'head'), may hold values from -6 to 6
- lin_keys: bfloat16 [8192, 64, 128], P('seq', 'head'), may hold values from -0.5 to 0.5
- linear_value_rows: bfloat16 [8192, 64, 128], P('seq', 'head'), may hold values from -6 to 6
- log_decay: float32 [64, 8192], P('head', 'seq'), may hold values from -1 to 0, as said below
- norm_gain: bfloat16 [64, 128], P('head'), may hold values from 0.5 to 1.5
- soft_queries: bfloat16 [8192, 64, 128], P('seq', 'head'), may hold values from -200 to 200
- soft_keys: bfloat16 [8192, 8, 128], P('seq', 'head'), may hold values from -5 to 5
- soft_values: bfloat16 [8192, 8, 128], P('seq', 'head'), may hold values from -6 to 6
- window_start: int32 [64], P('seq'), may hold values from 0 to 62, as said below
Outputs:
- lin_out: bfloat16 [8192, 64, 128], P('seq', 'head')
- soft_out: bfloat16 [8192, 64, 128], P('seq', 'head')
The draws below stay inside these ranges and needn't reach their ends.
Inputs may be any that keep to these rules, and one draw needn't show every extreme that they name: window_start[b] lies between b - 3 and b and is never negative; the last block's entry is 60 and the next-to-last block's entry is 62. `log_decay`: decay logarithms are negative.
All inputs are finite; a program needn't handle non-finite values.
Results may differ from the reference program's by a relative error of at most 0.013.
Values may be sent and summed in bfloat16 or wider, within the bound.
A program may use at most 192 MiB of HBM per device.

```python
import math
import jax
import jax.numpy as jnp
from jax import lax

DH = 128
HEADS = 64
KV_HEADS = 8
TOK_DEV = 128
REACH = 3
NBLK = 64
SEQUENCE_TOKENS = 8192


def draw_log_decay(key, part):
    parallel_lanes = jax.random.split(key, 6)
    fast_share = 0.5
    selector = jax.random.uniform(parallel_lanes[0], (HEADS,))
    fast_heads = selector < fast_share
    slow_rate = jnp.exp(jax.random.uniform(parallel_lanes[1], (HEADS,), minval=math.log(0.05), maxval=math.log(0.5))) / SEQUENCE_TOKENS
    fast_rate = jnp.exp(jax.random.uniform(parallel_lanes[2], (HEADS,), minval=math.log(1.0 / 50.0), maxval=math.log(1.0 / 30.0)))
    head_decay_rate = jnp.where(fast_heads, fast_rate, slow_rate)
    block_factor = jnp.exp(jax.random.uniform(parallel_lanes[3], (HEADS, NBLK), minval=math.log(0.5), maxval=0.0))
    processor_multiplier = jnp.repeat(block_factor, TOK_DEV, axis=1)
    random_perturbation = jnp.exp(jax.random.uniform(parallel_lanes[4], (HEADS, SEQUENCE_TOKENS), minval=-0.35, maxval=0.35))
    token_locations = jnp.arange(SEQUENCE_TOKENS, dtype=jnp.int32)
    spike_location = jax.random.randint(parallel_lanes[5], (3,), 0, SEQUENCE_TOKENS)
    spike_penalty = jax.random.uniform(jax.random.fold_in(key, 7), (3,), minval=0.2, maxval=0.333)
    spike_components = jnp.where(token_locations[None, :] == spike_location[:, None], jnp.log1p(-spike_penalty)[:, None], 0.0)
    spike_total_sum = jnp.sum(spike_components, axis=0)
    final_output = -head_decay_rate[:, None] * processor_multiplier * random_perturbation + spike_total_sum[None, :]
    return final_output.astype(jnp.float32)


def draw_pair(key):
    base_keys = jnp.clip(jax.random.normal(jax.random.fold_in(key, 11), (SEQUENCE_TOKENS, KV_HEADS, DH)), -4.0, 4.0)
    keys_out = base_keys
    queries_out = jnp.clip(jax.random.normal(jax.random.fold_in(key, 12), (SEQUENCE_TOKENS, HEADS, DH)), -4.0, 4.0)
    return (keys_out, queries_out)


def draw_soft_keys(key, part):
    return draw_pair(key)[0].astype(jnp.bfloat16)


def draw_soft_queries(key, part):
    return draw_pair(key)[1].astype(jnp.bfloat16)


def draw_window_start(key, part):
    blocks = jnp.arange(NBLK, dtype=jnp.int32)
    backward = jax.random.randint(key, (NBLK,), 0, REACH + 1)
    starts = jnp.maximum(blocks - backward, 0)
    starts = jnp.where(blocks == NBLK - 2, NBLK - 2, starts)
    return jnp.where(blocks == NBLK - 1, NBLK - 1 - REACH, starts).astype(jnp.int32)


def steps_of(stream_key, dims, shards, smallest, top_value):
    def one(axis_at, blocks):
        heights = jax.random.uniform(jax.random.fold_in(jax.random.fold_in(stream_key, 6), axis_at), (blocks,), jnp.float32, smallest / len(shards), top_value / len(shards))
        return jnp.repeat(jnp.exp(heights), dims[axis_at] // blocks).reshape((-1,) + (1,) * (len(dims) - axis_at - 1))

    level = one(*shards[0])
    for cut in shards[1:]:
        level = level * one(*cut)
    return level


def normal_values(rng, dims, width, reach, cuts=(), held_as=jnp.bfloat16):
    values = jax.random.normal(rng, dims, jnp.float32) * width
    if len(cuts) > 0:
        values = steps_of(rng, dims, cuts, -0.22, 0.18) * values
    return jnp.clip(values, min=-reach, max=reach).astype(held_as)


def setup_inputs(seed: int = 0) -> dict:
    streams_of = jax.random.split(jax.random.key(seed), 10)
    return {
        "linear_query_rows": normal_values(streams_of[0], (SEQUENCE_TOKENS, HEADS, DH), 1.0, 6.0, ((0, 64), (1, 4))),
        "lin_keys": normal_values(streams_of[1], (SEQUENCE_TOKENS, HEADS, DH), DH ** -0.5, 0.5, ((0, 64), (1, 4))),
        "linear_value_rows": normal_values(streams_of[2], (SEQUENCE_TOKENS, HEADS, DH), 1.0, 6.0, ((0, 64), (1, 4))),
        "log_decay": draw_log_decay(jax.random.fold_in(streams_of[9], 71), 0),
        "norm_gain": jnp.clip(1.0 + 0.1 * jax.random.normal(streams_of[4], (HEADS, DH), jnp.float32), 0.5, 1.5).astype(jnp.bfloat16),
        "soft_queries": draw_soft_queries(jax.random.fold_in(streams_of[9], 71), 0),
        "soft_keys": draw_soft_keys(jax.random.fold_in(streams_of[9], 71), 0),
        "soft_values": normal_values(streams_of[7], (SEQUENCE_TOKENS, KV_HEADS, DH), 1.0, 6.0, ((0, 64), (1, 4))),
        "window_start": draw_window_start(jax.random.fold_in(streams_of[9], 71), 0),
    }


def lightning(linear_query_rows, lin_keys, linear_value_rows, log_decay):
    block_count = SEQUENCE_TOKENS // TOK_DEV
    query_blocks = linear_query_rows.reshape(block_count, TOK_DEV, HEADS, DH)
    key_blocks = lin_keys.reshape(block_count, TOK_DEV, HEADS, DH)
    value_blocks = linear_value_rows.reshape(block_count, TOK_DEV, HEADS, DH)
    decay_blocks = log_decay.reshape(HEADS, block_count, TOK_DEV).transpose(1, 0, 2)
    token_locations = jnp.arange(TOK_DEV, dtype=jnp.int32)
    lower_mask = token_locations[:, None] >= token_locations[None, :]

    def one_block(preceding_state, inputs):
        query_rows, key_rows, value_rows, decays = inputs
        cumulated = jnp.cumsum(decays, axis=1)
        attention_logits = jnp.einsum('thd,shd->hts', query_rows.astype(jnp.float32), key_rows.astype(jnp.float32))
        gap = jnp.where(lower_mask[None], cumulated[:, :, None] - cumulated[:, None, :], -jnp.inf)
        weights = (attention_logits * jnp.exp(gap)).astype(jnp.bfloat16)
        local_part = jnp.einsum('hts,shd->thd', weights.astype(jnp.float32), value_rows.astype(jnp.float32))
        carried_over_state = jnp.einsum('nwg,wgq->nwq', query_rows.astype(jnp.float32), preceding_state, precision=lax.Precision.HIGHEST)
        mixed = local_part + jnp.exp(cumulated).T[:, :, None] * carried_over_state
        tail = jnp.exp(cumulated[:, -1:] - cumulated)
        key_product = key_rows.astype(jnp.float32) * tail.T[:, :, None]
        recurrent_state = jnp.einsum('egz,egc->gzc', key_product, value_rows.astype(jnp.float32), precision=lax.Precision.HIGHEST)
        fresh = jnp.exp(cumulated[:, -1])[:, None, None] * preceding_state + recurrent_state
        return (fresh, mixed)
    start_state = jnp.zeros((HEADS, DH, DH), jnp.float32)
    unused, mixed_all = lax.scan(one_block, start_state, (query_blocks, key_blocks, value_blocks, decay_blocks))
    return mixed_all.reshape(SEQUENCE_TOKENS, HEADS, DH)

def softmax_layer(soft_queries, soft_keys, soft_values, window_start):
    group = HEADS // KV_HEADS
    score_scale = float(DH) ** (-0.5)
    padding = jnp.zeros((REACH * TOK_DEV, KV_HEADS, DH), jnp.bfloat16)
    padded_keys = jnp.concatenate([padding, soft_keys], axis=0)
    padded_values = jnp.concatenate([padding, soft_values], axis=0)
    span = (REACH + 1) * TOK_DEV
    key_index = jnp.arange(span, dtype=jnp.int32)
    query_index = jnp.arange(TOK_DEV, dtype=jnp.int32)

    def one_block(block_index):
        start = (block_index * TOK_DEV).astype(jnp.int32)
        query_rows = lax.dynamic_slice_in_dim(soft_queries, start, TOK_DEV, 0).reshape(TOK_DEV, KV_HEADS, group, DH)
        key_rows = lax.dynamic_slice_in_dim(padded_keys, start, span, 0)
        value_rows = lax.dynamic_slice_in_dim(padded_values, start, span, 0)
        attention_logits = jnp.einsum('cphm,npm->phcn', query_rows.astype(jnp.float32), key_rows.astype(jnp.float32)) * score_scale
        key_block = block_index - REACH + key_index // TOK_DEV
        key_local = key_index % TOK_DEV
        earlier = key_block[None, :] < block_index
        causal = key_local[None, :] <= query_index[:, None]
        visible = (earlier | causal) & (key_block[None, :] >= window_start[block_index])
        masked = jnp.where(visible[None, None], attention_logits, -jnp.inf)
        top = lax.optimization_barrier(jnp.max(masked, axis=-1))
        exps = jnp.exp(masked - top[..., None])
        total = lax.optimization_barrier(jnp.sum(exps, axis=-1))
        attention_probabilities = exps.astype(jnp.bfloat16)
        summed_total = jnp.einsum('nuwz,zny->wnuy', attention_probabilities.astype(jnp.float32), value_rows.astype(jnp.float32))
        final_output = summed_total / total.transpose(2, 0, 1)[..., None]
        return final_output.reshape(TOK_DEV, HEADS, DH).astype(jnp.bfloat16)
    blocks = lax.map(one_block, jnp.arange(NBLK, dtype=jnp.int32))
    return blocks.reshape(SEQUENCE_TOKENS, HEADS, DH)

def reference(linear_query_rows, lin_keys, linear_value_rows, log_decay, norm_gain, soft_queries, soft_keys, soft_values, window_start):
    mixed = lightning(linear_query_rows, lin_keys, linear_value_rows, log_decay)
    mean_square = lax.optimization_barrier(jnp.sum(mixed * mixed, axis=(1, 2))) / (HEADS * DH)
    lin_out = (mixed * lax.rsqrt(mean_square + 1e-06)[:, None, None] * norm_gain.astype(jnp.float32)).astype(jnp.bfloat16)
    soft_out = softmax_layer(soft_queries, soft_keys, soft_values, window_start)
    return (lin_out, soft_out)
```

```python
import jax
import jax.numpy as jnp
from jax import lax
from jax.sharding import PartitionSpec as P

DH = 128
HEADS = 64
REACH = 3


def exclusive_scan(element, axis, combine):
    length, here = (lax.axis_size(axis), lax.axis_index(axis))
    received = from_behind(element, axis, 1)
    before = received
    total = combine(received, element)
    shift = 2
    while shift < length:
        received = from_behind(total, axis, shift)
        before = combine(received, before)
        if 2 * shift < length:
            total = combine(received, total)
        shift *= 2
    return before


def from_behind(value, axis, steps):
    count = lax.axis_size(axis)
    first, last = (max(0, -steps), min(count, count - steps))
    return lax.ppermute(value, axis, [(source, source + steps) for source in range(first, last)])


def combine_states(earlier, later):
    return (earlier[0] * later[0], later[0][:, None, None] * earlier[1] + later[1])


def split_parts(matrix):
    upper = matrix.astype(jnp.bfloat16)
    lower = (matrix - upper.astype(jnp.float32)).astype(jnp.bfloat16)
    return (upper, lower)


def attend(carried_over_state, query_rows, key_rows, value_rows, visible, score_scale):
    running_max, running_sum, accumulated = carried_over_state
    attention_logits = (
        jnp.einsum("cphm,npm->phcn", query_rows, key_rows, preferred_element_type=jnp.float32)
        * score_scale
    )
    masked = jnp.where(visible, attention_logits, -jnp.inf)
    new_max = jnp.maximum(running_max, jnp.max(masked, axis=-1))
    power_exponent = jnp.exp(masked - new_max[..., None])
    fading = jnp.exp(running_max - new_max)
    new_sum = running_sum * fading + jnp.sum(power_exponent, axis=-1)
    product = jnp.einsum(
        "qyjl,lqu->qyju",
        power_exponent.astype(jnp.bfloat16),
        value_rows,
        preferred_element_type=jnp.float32,
    )
    return (new_max, new_sum, accumulated * fading[..., None] + product)


def body(
    linear_query_rows,
    lin_keys,
    linear_value_rows,
    log_decay,
    norm_gain,
    soft_queries,
    soft_keys,
    soft_values,
    window_start,
):
    row_count, heads_here, head_width = linear_query_rows.shape
    cumulated = jnp.cumsum(log_decay, axis=1)
    token_locations = jnp.arange(row_count, dtype=jnp.int32)
    lower_mask = token_locations[:, None] >= token_locations[None, :]
    tail = jnp.exp(cumulated[:, -1:] - cumulated)
    key_product = lin_keys.astype(jnp.float32) * tail.T[:, :, None]
    key_product_upper, key_product_lower = split_parts(key_product)
    recurrent_state = jnp.einsum(
        "egz,egc->gzc", key_product_upper, linear_value_rows, preferred_element_type=jnp.float32
    )
    recurrent_state = recurrent_state + jnp.einsum(
        "egz,egc->gzc", key_product_lower, linear_value_rows, preferred_element_type=jnp.float32
    )
    falling = jnp.exp(cumulated[:, -1])
    preceding_state = exclusive_scan((falling, recurrent_state), "seq", combine_states)[1]
    lin_scores = jnp.einsum(
        "thd,shd->hts", linear_query_rows, lin_keys, preferred_element_type=jnp.float32
    )
    gap = jnp.where(lower_mask[None], cumulated[:, :, None] - cumulated[:, None, :], -jnp.inf)
    lin_weights = (lin_scores * jnp.exp(gap)).astype(jnp.bfloat16)
    local_part = jnp.einsum(
        "hts,shd->thd", lin_weights, linear_value_rows, preferred_element_type=jnp.float32
    )
    preceding_upper, preceding_lower = split_parts(preceding_state)
    carried_part = jnp.einsum(
        "nwg,wgq->nwq", linear_query_rows, preceding_upper, preferred_element_type=jnp.float32
    )
    carried_part = carried_part + jnp.einsum(
        "nwg,wgq->nwq", linear_query_rows, preceding_lower, preferred_element_type=jnp.float32
    )
    mixed = local_part + jnp.exp(cumulated).T[:, :, None] * carried_part
    squares = lax.psum(jnp.sum(mixed * mixed, axis=(1, 2)), "head")
    lin_out = (
        mixed
        * lax.rsqrt(squares / (HEADS * DH) + 1e-06)[:, None, None]
        * norm_gain.astype(jnp.float32)
    ).astype(jnp.bfloat16)
    kv_here = soft_keys.shape[1]
    group = heads_here // kv_here
    score_scale = float(head_width) ** (-0.5)
    query_rows = soft_queries.reshape(row_count, kv_here, group, head_width)
    block_index = lax.axis_index("seq")
    first_block = window_start[0]
    previous = [from_behind((soft_keys, soft_values), "seq", back) for back in range(REACH, 0, -1)]
    all_keys = jnp.concatenate([p[0] for p in previous] + [soft_keys], axis=0)
    all_values = jnp.concatenate([p[1] for p in previous] + [soft_values], axis=0)
    key_index = jnp.arange((REACH + 1) * row_count, dtype=jnp.int32)
    key_block = block_index - REACH + key_index // row_count
    causal = (key_index % row_count)[None, :] <= token_locations[:, None]
    visible = ((key_block[None, :] < block_index) | causal) & (key_block[None, :] >= first_block)
    logits = (
        jnp.einsum("cphm,npm->phcn", query_rows, all_keys, preferred_element_type=jnp.float32)
        * score_scale
    )
    masked = jnp.where(visible, logits, -jnp.inf)
    top = jnp.max(masked, axis=-1)
    exps = jnp.exp(masked - top[..., None])
    total = jnp.sum(exps, axis=-1)
    summed = jnp.einsum(
        "qyjl,lqu->qyju", exps.astype(jnp.bfloat16), all_values, preferred_element_type=jnp.float32
    )
    carried_over_state = (top, total, summed)
    final_output = carried_over_state[2] / carried_over_state[1][..., None]
    soft_out = (
        final_output.transpose(2, 0, 1, 3)
        .reshape(row_count, heads_here, head_width)
        .astype(jnp.bfloat16)
    )
    return (lin_out, soft_out)


def solution(mesh):
    placed = (
        P("seq", "head", None),
        P("seq", "head", None),
        P("seq", "head", None),
        P("head", "seq"),
        P("head", None),
        P("seq", "head", None),
        P("seq", "head", None),
        P("seq", "head", None),
        P("seq"),
    )
    return jax.shard_map(
        body,
        mesh=mesh,
        in_specs=placed,
        out_specs=(P("seq", "head", None), P("seq", "head", None)),
        check_vma=False,
    )
```

```python
import jax
import jax.numpy as jnp
from jax import lax
from jax.sharding import PartitionSpec as P

DH = 128
HEADS = 64
REACH = 3


def exclusive_scan(element, axis, combine):
    length = lax.axis_size(axis)

    def send(value, shift):
        fall, state = from_behind((value[0], value[1].astype(jnp.bfloat16)), axis, shift)
        return (fall, state.astype(jnp.float32))

    received = send(element, 1)
    before = received
    total = combine(received, element)
    shift = 2
    while shift < length:
        received = send(total, shift)
        before = combine(received, before)
        if 2 * shift < length:
            total = combine(received, total)
        shift *= 2
    return before


def from_behind(value, axis, steps):
    count = lax.axis_size(axis)
    first, last = (max(0, -steps), min(count, count - steps))
    return lax.ppermute(value, axis, [(source, source + steps) for source in range(first, last)])


def combine_states(earlier, later):
    return (earlier[0] * later[0], later[0][:, None, None] * earlier[1] + later[1])


def split_parts(matrix):
    upper = matrix.astype(jnp.bfloat16)
    lower = (matrix - upper.astype(jnp.float32)).astype(jnp.bfloat16)
    return (upper, lower)


def attend(carried_over_state, query_rows, key_rows, value_rows, visible, score_scale):
    running_max, running_sum, accumulated = carried_over_state
    attention_logits = (
        jnp.einsum("cphm,npm->phcn", query_rows, key_rows, preferred_element_type=jnp.float32)
        * score_scale
    )
    masked = jnp.where(visible, attention_logits, -jnp.inf)
    new_max = jnp.maximum(running_max, jnp.max(masked, axis=-1))
    power_exponent = jnp.exp(masked - new_max[..., None])
    fading = jnp.exp(running_max - new_max)
    new_sum = running_sum * fading + jnp.sum(power_exponent, axis=-1)
    product = jnp.einsum(
        "qyjl,lqu->qyju",
        power_exponent.astype(jnp.bfloat16),
        value_rows,
        preferred_element_type=jnp.float32,
    )
    return (new_max, new_sum, accumulated * fading[..., None] + product)


def body(
    linear_query_rows,
    lin_keys,
    linear_value_rows,
    log_decay,
    norm_gain,
    soft_queries,
    soft_keys,
    soft_values,
    window_start,
):
    row_count, heads_here, head_width = linear_query_rows.shape
    cumulated = jnp.cumsum(log_decay, axis=1)
    token_locations = jnp.arange(row_count, dtype=jnp.int32)
    lower_mask = token_locations[:, None] >= token_locations[None, :]
    tail = jnp.exp(cumulated[:, -1:] - cumulated)
    key_product = lin_keys.astype(jnp.float32) * tail.T[:, :, None]
    key_product_upper, key_product_lower = split_parts(key_product)
    recurrent_state = jnp.einsum(
        "egz,egc->gzc", key_product_upper, linear_value_rows, preferred_element_type=jnp.float32
    )
    recurrent_state = recurrent_state + jnp.einsum(
        "egz,egc->gzc", key_product_lower, linear_value_rows, preferred_element_type=jnp.float32
    )
    falling = jnp.exp(cumulated[:, -1])
    preceding_state = exclusive_scan((falling, recurrent_state), "seq", combine_states)[1]
    lin_scores = jnp.einsum(
        "thd,shd->hts", linear_query_rows, lin_keys, preferred_element_type=jnp.float32
    )
    gap = jnp.where(lower_mask[None], cumulated[:, :, None] - cumulated[:, None, :], -jnp.inf)
    lin_weights = (lin_scores * jnp.exp(gap)).astype(jnp.bfloat16)
    local_part = jnp.einsum(
        "hts,shd->thd", lin_weights, linear_value_rows, preferred_element_type=jnp.float32
    )
    preceding_upper, preceding_lower = split_parts(preceding_state)
    carried_part = jnp.einsum(
        "nwg,wgq->nwq", linear_query_rows, preceding_upper, preferred_element_type=jnp.float32
    )
    carried_part = carried_part + jnp.einsum(
        "nwg,wgq->nwq", linear_query_rows, preceding_lower, preferred_element_type=jnp.float32
    )
    mixed = local_part + jnp.exp(cumulated).T[:, :, None] * carried_part
    squares = lax.psum(jnp.sum(mixed * mixed, axis=(1, 2)), "head")
    lin_out = (
        mixed
        * lax.rsqrt(squares / (HEADS * DH) + 1e-06)[:, None, None]
        * norm_gain.astype(jnp.float32)
    ).astype(jnp.bfloat16)
    kv_here = soft_keys.shape[1]
    group = heads_here // kv_here
    score_scale = float(head_width) ** (-0.5)
    query_rows = soft_queries.reshape(row_count, kv_here, group, head_width)
    block_index = lax.axis_index("seq")
    first_block = window_start[0]
    previous = [from_behind((soft_keys, soft_values), "seq", back) for back in range(REACH, 0, -1)]
    all_keys = jnp.concatenate([p[0] for p in previous] + [soft_keys], axis=0)
    all_values = jnp.concatenate([p[1] for p in previous] + [soft_values], axis=0)
    key_index = jnp.arange((REACH + 1) * row_count, dtype=jnp.int32)
    key_block = block_index - REACH + key_index // row_count
    causal = (key_index % row_count)[None, :] <= token_locations[:, None]
    visible = ((key_block[None, :] < block_index) | causal) & (key_block[None, :] >= first_block)
    logits = (
        jnp.einsum("cphm,npm->phcn", query_rows, all_keys, preferred_element_type=jnp.float32)
        * score_scale
    )
    masked = jnp.where(visible, logits, -jnp.inf)
    top = jnp.max(masked, axis=-1)
    exps = jnp.exp(masked - top[..., None])
    total = jnp.sum(exps, axis=-1)
    summed = jnp.einsum(
        "qyjl,lqu->qyju", exps.astype(jnp.bfloat16), all_values, preferred_element_type=jnp.float32
    )
    carried_over_state = (top, total, summed)
    final_output = carried_over_state[2] / carried_over_state[1][..., None]
    soft_out = (
        final_output.transpose(2, 0, 1, 3)
        .reshape(row_count, heads_here, head_width)
        .astype(jnp.bfloat16)
    )
    return (lin_out, soft_out)


def solution(mesh):
    placed = (
        P("seq", "head", None),
        P("seq", "head", None),
        P("seq", "head", None),
        P("head", "seq"),
        P("head", None),
        P("seq", "head", None),
        P("seq", "head", None),
        P("seq", "head", None),
        P("seq"),
    )
    return jax.shard_map(
        body,
        mesh=mesh,
        in_specs=placed,
        out_specs=(P("seq", "head", None), P("seq", "head", None)),
        check_vma=False,
    )
```

```python
import functools

import jax
import jax.numpy as jnp
from jax import lax
from jax.experimental import pallas as pl
from jax.experimental.pallas import tpu as pltpu
from jax.sharding import PartitionSpec as P

MESH = pl.DeviceIdType.MESH

DH = 128
HEADS = 64
REACH = 3


def scan_kernel(
    rounds,
    chunks,
    fall_ref,
    state_ref,
    sent0_ref,
    out_ref,
    whole,
    whole_fall,
    out_fall,
    got,
    got_fall,
    outgoing,
    outgoing_fall,
    send_sem,
    recv_sem,
    fsend_sem,
    frecv_sem,
):
    me = lax.axis_index("seq")
    head = lax.axis_index("head")
    length = 2**rounds
    width = state_ref.shape[0] // chunks

    def receives(k):
        return (me - 2**k + length) // length

    def can_send(k):
        return 1 - (me + 2**k) // length

    barrier = pltpu.get_barrier_semaphore()
    partners = 0
    for k in range(rounds):
        ahead, behind = can_send(k), receives(k)
        partners = partners + ahead + behind

        @pl.when(ahead == 1)
        def _():
            pl.semaphore_signal(barrier, inc=1, device_id=(me + 2**k, head), device_id_type=MESH)

        @pl.when(behind == 1)
        def _():
            pl.semaphore_signal(barrier, inc=1, device_id=(me - 2**k, head), device_id_type=MESH)

    pl.semaphore_wait(barrier, partners)

    def state_copy(k, c, source, device):
        rows = pl.ds(c * width, width)
        return pltpu.make_async_remote_copy(
            src_ref=source.at[rows],
            dst_ref=got.at[k, rows],
            send_sem=send_sem.at[k, c],
            recv_sem=recv_sem.at[k, c],
            device_id=(device, head),
            device_id_type=MESH,
        )

    def fall_copy(k, device):
        return pltpu.make_async_remote_copy(
            src_ref=outgoing_fall.at[k],
            dst_ref=got_fall.at[k],
            send_sem=fsend_sem.at[k],
            recv_sem=frecv_sem.at[k],
            device_id=(device, head),
            device_id_type=MESH,
        )

    outgoing_fall[0] = fall_ref[...]

    @pl.when(can_send(0) == 1)
    def _():
        fall_copy(0, me + 1).start()
        for c in range(chunks):
            state_copy(0, c, sent0_ref, me + 1).start()

    whole[...] = state_ref[...]
    whole_fall[...] = fall_ref[...]
    out_ref[...] = jnp.zeros_like(out_ref)
    out_fall[...] = jnp.ones_like(out_fall)
    for k in range(rounds):
        last = k == rounds - 1
        for c in range(chunks):
            rows = pl.ds(c * width, width)

            @pl.when(receives(k) == 1)
            def _():
                state_copy(k, c, got.at[k], me - 2**k).wait_recv()
                arrived = got[k, rows].astype(jnp.float32)
                out_ref[rows] = out_fall[rows][:, None, :] * arrived + out_ref[rows]
                if not last:
                    whole[rows] = whole_fall[rows][:, None, :] * arrived + whole[rows]

            if not last:

                @pl.when(can_send(k + 1) == 1)
                def _():
                    outgoing[k + 1, rows] = whole[rows].astype(jnp.bfloat16)
                    state_copy(k + 1, c, outgoing.at[k + 1], me + 2 ** (k + 1)).start()

        @pl.when(receives(k) == 1)
        def _():
            fall_copy(k, me - 2**k).wait_recv()
            arrived = got_fall[k]
            out_fall[...] = arrived * out_fall[...]
            if not last:
                whole_fall[...] = arrived * whole_fall[...]

        if not last:

            @pl.when(can_send(k + 1) == 1)
            def _():
                outgoing_fall[k + 1] = whole_fall[...]
                fall_copy(k + 1, me + 2 ** (k + 1)).start()

    for k in range(rounds):

        @pl.when(can_send(k) == 1)
        def _():
            fall_copy(k, me + 2**k).wait_send()
            for c in range(chunks):
                state_copy(k, c, got.at[k], me + 2**k).wait_send()


def exclusive_scan(falling, state, axis):
    length = lax.axis_size(axis)
    rounds = length.bit_length() - 1
    chunks = 4
    heads, rows, columns = state.shape
    fall_rows = jnp.broadcast_to(falling[:, None], (heads, columns))
    vmem = pl.BlockSpec(memory_space=pltpu.VMEM)
    return pl.pallas_call(
        functools.partial(scan_kernel, rounds, chunks),
        out_shape=jax.ShapeDtypeStruct(state.shape, jnp.float32),
        in_specs=[vmem] * 3,
        out_specs=vmem,
        scratch_shapes=[
            pltpu.VMEM(state.shape, jnp.float32),
            pltpu.VMEM((heads, columns), jnp.float32),
            pltpu.VMEM((heads, columns), jnp.float32),
            pltpu.VMEM((rounds,) + state.shape, jnp.bfloat16),
            pltpu.VMEM((rounds, heads, columns), jnp.float32),
            pltpu.VMEM((rounds,) + state.shape, jnp.bfloat16),
            pltpu.VMEM((rounds, heads, columns), jnp.float32),
            pltpu.SemaphoreType.DMA((rounds, chunks)),
            pltpu.SemaphoreType.DMA((rounds, chunks)),
            pltpu.SemaphoreType.DMA((rounds,)),
            pltpu.SemaphoreType.DMA((rounds,)),
        ],
        compiler_params=pltpu.CompilerParams(collective_id=0, has_side_effects=True),
    )(fall_rows, state, state.astype(jnp.bfloat16))


def from_behind(value, axis, steps):
    count = lax.axis_size(axis)
    first, last = (max(0, -steps), min(count, count - steps))
    return lax.ppermute(value, axis, [(source, source + steps) for source in range(first, last)])


def combine_states(earlier, later):
    return (earlier[0] * later[0], later[0][:, None, None] * earlier[1] + later[1])


def split_parts(matrix):
    upper = matrix.astype(jnp.bfloat16)
    lower = (matrix - upper.astype(jnp.float32)).astype(jnp.bfloat16)
    return (upper, lower)


def attend(carried_over_state, query_rows, key_rows, value_rows, visible, score_scale):
    running_max, running_sum, accumulated = carried_over_state
    attention_logits = (
        jnp.einsum("cphm,npm->phcn", query_rows, key_rows, preferred_element_type=jnp.float32)
        * score_scale
    )
    masked = jnp.where(visible, attention_logits, -jnp.inf)
    new_max = jnp.maximum(running_max, jnp.max(masked, axis=-1))
    power_exponent = jnp.exp(masked - new_max[..., None])
    fading = jnp.exp(running_max - new_max)
    new_sum = running_sum * fading + jnp.sum(power_exponent, axis=-1)
    product = jnp.einsum(
        "qyjl,lqu->qyju",
        power_exponent.astype(jnp.bfloat16),
        value_rows,
        preferred_element_type=jnp.float32,
    )
    return (new_max, new_sum, accumulated * fading[..., None] + product)


def body(
    linear_query_rows,
    lin_keys,
    linear_value_rows,
    log_decay,
    norm_gain,
    soft_queries,
    soft_keys,
    soft_values,
    window_start,
):
    row_count, heads_here, head_width = linear_query_rows.shape
    cumulated = jnp.cumsum(log_decay, axis=1)
    token_locations = jnp.arange(row_count, dtype=jnp.int32)
    lower_mask = token_locations[:, None] >= token_locations[None, :]
    tail = jnp.exp(cumulated[:, -1:] - cumulated)
    key_product = lin_keys.astype(jnp.float32) * tail.T[:, :, None]
    key_product_upper, key_product_lower = split_parts(key_product)
    recurrent_state = jnp.einsum(
        "egz,egc->gzc", key_product_upper, linear_value_rows, preferred_element_type=jnp.float32
    )
    recurrent_state = recurrent_state + jnp.einsum(
        "egz,egc->gzc", key_product_lower, linear_value_rows, preferred_element_type=jnp.float32
    )
    falling = jnp.exp(cumulated[:, -1])
    preceding_state = exclusive_scan(falling, recurrent_state, "seq")
    lin_scores = jnp.einsum(
        "thd,shd->hts", linear_query_rows, lin_keys, preferred_element_type=jnp.float32
    )
    gap = jnp.where(lower_mask[None], cumulated[:, :, None] - cumulated[:, None, :], -jnp.inf)
    lin_weights = (lin_scores * jnp.exp(gap)).astype(jnp.bfloat16)
    local_part = jnp.einsum(
        "hts,shd->thd", lin_weights, linear_value_rows, preferred_element_type=jnp.float32
    )
    preceding_upper, preceding_lower = split_parts(preceding_state)
    carried_part = jnp.einsum(
        "nwg,wgq->nwq", linear_query_rows, preceding_upper, preferred_element_type=jnp.float32
    )
    carried_part = carried_part + jnp.einsum(
        "nwg,wgq->nwq", linear_query_rows, preceding_lower, preferred_element_type=jnp.float32
    )
    mixed = local_part + jnp.exp(cumulated).T[:, :, None] * carried_part
    squares = lax.psum(jnp.sum(mixed * mixed, axis=(1, 2)), "head")
    lin_out = (
        mixed
        * lax.rsqrt(squares / (HEADS * DH) + 1e-06)[:, None, None]
        * norm_gain.astype(jnp.float32)
    ).astype(jnp.bfloat16)
    kv_here = soft_keys.shape[1]
    group = heads_here // kv_here
    score_scale = float(head_width) ** (-0.5)
    query_rows = soft_queries.reshape(row_count, kv_here, group, head_width)
    block_index = lax.axis_index("seq")
    first_block = window_start[0]
    previous = [from_behind((soft_keys, soft_values), "seq", back) for back in range(REACH, 0, -1)]
    all_keys = jnp.concatenate([p[0] for p in previous] + [soft_keys], axis=0)
    all_values = jnp.concatenate([p[1] for p in previous] + [soft_values], axis=0)
    key_index = jnp.arange((REACH + 1) * row_count, dtype=jnp.int32)
    key_block = block_index - REACH + key_index // row_count
    causal = (key_index % row_count)[None, :] <= token_locations[:, None]
    visible = ((key_block[None, :] < block_index) | causal) & (key_block[None, :] >= first_block)
    logits = (
        jnp.einsum("cphm,npm->phcn", query_rows, all_keys, preferred_element_type=jnp.float32)
        * score_scale
    )
    masked = jnp.where(visible, logits, -jnp.inf)
    top = jnp.max(masked, axis=-1)
    exps = jnp.exp(masked - top[..., None])
    total = jnp.sum(exps, axis=-1)
    summed = jnp.einsum(
        "qyjl,lqu->qyju", exps.astype(jnp.bfloat16), all_values, preferred_element_type=jnp.float32
    )
    carried_over_state = (top, total, summed)
    final_output = carried_over_state[2] / carried_over_state[1][..., None]
    soft_out = (
        final_output.transpose(2, 0, 1, 3)
        .reshape(row_count, heads_here, head_width)
        .astype(jnp.bfloat16)
    )
    return (lin_out, soft_out)


def solution(mesh):
    placed = (
        P("seq", "head", None),
        P("seq", "head", None),
        P("seq", "head", None),
        P("head", "seq"),
        P("head", None),
        P("seq", "head", None),
        P("seq", "head", None),
        P("seq", "head", None),
        P("seq"),
    )
    return jax.shard_map(
        body,
        mesh=mesh,
        in_specs=placed,
        out_specs=(P("seq", "head", None), P("seq", "head", None)),
        check_vma=False,
    )
```

```python
import functools

import jax
import jax.numpy as jnp
from jax import lax
from jax.experimental import pallas as pl
from jax.experimental.pallas import tpu as pltpu
from jax.sharding import PartitionSpec as P

MESH = pl.DeviceIdType.MESH

DH = 128
HEADS = 64
REACH = 3


def scan_kernel(
    rounds,
    chunks,
    reach,
    fall_ref,
    state_ref,
    sent0_ref,
    kv_ref,
    out_ref,
    kv_out,
    whole,
    whole_fall,
    out_fall,
    got,
    got_fall,
    outgoing,
    outgoing_fall,
    send_sem,
    recv_sem,
    fsend_sem,
    frecv_sem,
    kv_got,
    kv_send,
    kv_recv,
):
    me = lax.axis_index("seq")
    head = lax.axis_index("head")
    length = 2**rounds
    width = state_ref.shape[0] // chunks

    def receives(k):
        return (me - 2**k + length) // length

    def can_send(k):
        return 1 - (me + 2**k) // length

    def ahead(dist):
        return 1 - (me + dist) // length

    def behind(dist):
        return (me - dist + length) // length

    barrier = pltpu.get_barrier_semaphore()
    partners = 0
    for dist in sorted(set([2**k for k in range(rounds)] + list(range(1, reach + 1)))):
        partners = partners + ahead(dist) + behind(dist)

        @pl.when(ahead(dist) == 1)
        def _():
            pl.semaphore_signal(barrier, inc=1, device_id=(me + dist, head), device_id_type=MESH)

        @pl.when(behind(dist) == 1)
        def _():
            pl.semaphore_signal(barrier, inc=1, device_id=(me - dist, head), device_id_type=MESH)

    pl.semaphore_wait(barrier, partners)

    def kv_copy(dist, device):
        return pltpu.make_async_remote_copy(
            src_ref=kv_ref,
            dst_ref=kv_got.at[dist - 1],
            send_sem=kv_send.at[dist - 1],
            recv_sem=kv_recv.at[dist - 1],
            device_id=(device, head),
            device_id_type=MESH,
        )

    for dist in range(1, reach + 1):

        @pl.when(ahead(dist) == 1)
        def _():
            kv_copy(dist, me + dist).start()

    def state_copy(k, c, source, device):
        rows = pl.ds(c * width, width)
        return pltpu.make_async_remote_copy(
            src_ref=source.at[rows],
            dst_ref=got.at[k, rows],
            send_sem=send_sem.at[k, c],
            recv_sem=recv_sem.at[k, c],
            device_id=(device, head),
            device_id_type=MESH,
        )

    def fall_copy(k, device):
        return pltpu.make_async_remote_copy(
            src_ref=outgoing_fall.at[k],
            dst_ref=got_fall.at[k],
            send_sem=fsend_sem.at[k],
            recv_sem=frecv_sem.at[k],
            device_id=(device, head),
            device_id_type=MESH,
        )

    outgoing_fall[0] = fall_ref[...]

    @pl.when(can_send(0) == 1)
    def _():
        fall_copy(0, me + 1).start()
        for c in range(chunks):
            state_copy(0, c, sent0_ref, me + 1).start()

    whole[...] = state_ref[...]
    whole_fall[...] = fall_ref[...]
    out_ref[...] = jnp.zeros_like(out_ref)
    out_fall[...] = jnp.ones_like(out_fall)
    for k in range(rounds):
        last = k == rounds - 1
        for c in range(chunks):
            rows = pl.ds(c * width, width)

            @pl.when(receives(k) == 1)
            def _():
                state_copy(k, c, got.at[k], me - 2**k).wait_recv()
                arrived = got[k, rows].astype(jnp.float32)
                out_ref[rows] = out_fall[rows][:, None, :] * arrived + out_ref[rows]
                if not last:
                    whole[rows] = whole_fall[rows][:, None, :] * arrived + whole[rows]

            if not last:

                @pl.when(can_send(k + 1) == 1)
                def _():
                    outgoing[k + 1, rows] = whole[rows].astype(jnp.bfloat16)
                    state_copy(k + 1, c, outgoing.at[k + 1], me + 2 ** (k + 1)).start()

        @pl.when(receives(k) == 1)
        def _():
            fall_copy(k, me - 2**k).wait_recv()
            arrived = got_fall[k]
            out_fall[...] = arrived * out_fall[...]
            if not last:
                whole_fall[...] = arrived * whole_fall[...]

        if not last:

            @pl.when(can_send(k + 1) == 1)
            def _():
                outgoing_fall[k + 1] = whole_fall[...]
                fall_copy(k + 1, me + 2 ** (k + 1)).start()

    for dist in range(1, reach + 1):

        @pl.when(behind(dist) == 1)
        def _():
            kv_copy(dist, me - dist).wait_recv()
            kv_out[dist - 1] = kv_got[dist - 1]

        @pl.when(behind(dist) == 0)
        def _():
            kv_out[dist - 1] = jnp.zeros_like(kv_out.at[dist - 1])

        @pl.when(ahead(dist) == 1)
        def _():
            kv_copy(dist, me + dist).wait_send()

    for k in range(rounds):

        @pl.when(can_send(k) == 1)
        def _():
            fall_copy(k, me + 2**k).wait_send()
            for c in range(chunks):
                state_copy(k, c, got.at[k], me + 2**k).wait_send()


def exclusive_scan(falling, state, kv, axis):
    length = lax.axis_size(axis)
    rounds = length.bit_length() - 1
    chunks = 4
    heads, rows, columns = state.shape
    fall_rows = jnp.broadcast_to(falling[:, None], (heads, columns))
    vmem = pl.BlockSpec(memory_space=pltpu.VMEM)
    return pl.pallas_call(
        functools.partial(scan_kernel, rounds, chunks, REACH),
        out_shape=(
            jax.ShapeDtypeStruct(state.shape, jnp.float32),
            jax.ShapeDtypeStruct((REACH,) + kv.shape, kv.dtype),
        ),
        in_specs=[vmem] * 4,
        out_specs=(vmem, vmem),
        scratch_shapes=[
            pltpu.VMEM(state.shape, jnp.float32),
            pltpu.VMEM((heads, columns), jnp.float32),
            pltpu.VMEM((heads, columns), jnp.float32),
            pltpu.VMEM((rounds,) + state.shape, jnp.bfloat16),
            pltpu.VMEM((rounds, heads, columns), jnp.float32),
            pltpu.VMEM((rounds,) + state.shape, jnp.bfloat16),
            pltpu.VMEM((rounds, heads, columns), jnp.float32),
            pltpu.SemaphoreType.DMA((rounds, chunks)),
            pltpu.SemaphoreType.DMA((rounds, chunks)),
            pltpu.SemaphoreType.DMA((rounds,)),
            pltpu.SemaphoreType.DMA((rounds,)),
            pltpu.VMEM((REACH,) + kv.shape, kv.dtype),
            pltpu.SemaphoreType.DMA((REACH,)),
            pltpu.SemaphoreType.DMA((REACH,)),
        ],
        compiler_params=pltpu.CompilerParams(collective_id=0, has_side_effects=True),
    )(fall_rows, state, state.astype(jnp.bfloat16), kv)


def head_sum_kernel(count, value_ref, out_ref, slots, send_sem, recv_sem):
    me = lax.axis_index("seq")
    head = lax.axis_index("head")
    barrier = pltpu.get_barrier_semaphore()
    for other in range(count):

        @pl.when(other != head)
        def _():
            pl.semaphore_signal(barrier, inc=1, device_id=(me, other), device_id_type=MESH)

    pl.semaphore_wait(barrier, count - 1)
    slots[head] = value_ref[...]

    def copy(other, slot):
        return pltpu.make_async_remote_copy(
            src_ref=value_ref,
            dst_ref=slots.at[slot],
            send_sem=send_sem.at[other],
            recv_sem=recv_sem.at[slot],
            device_id=(me, other),
            device_id_type=MESH,
        )

    for other in range(count):

        @pl.when(other != head)
        def _():
            copy(other, head).start()

    for other in range(count):

        @pl.when(other != head)
        def _():
            copy(other, other).wait_recv()
            copy(other, head).wait_send()

    total = slots[0]
    for other in range(1, count):
        total = total + slots[other]
    out_ref[...] = total


def head_sum(value, axis):
    count = lax.axis_size(axis)
    vmem = pl.BlockSpec(memory_space=pltpu.VMEM)
    row = value.reshape(1, -1)
    return pl.pallas_call(
        functools.partial(head_sum_kernel, count),
        out_shape=jax.ShapeDtypeStruct(row.shape, row.dtype),
        in_specs=[vmem],
        out_specs=vmem,
        scratch_shapes=[
            pltpu.VMEM((count,) + row.shape, row.dtype),
            pltpu.SemaphoreType.DMA((count,)),
            pltpu.SemaphoreType.DMA((count,)),
        ],
        compiler_params=pltpu.CompilerParams(collective_id=1, has_side_effects=True),
    )(row).reshape(value.shape)


def from_behind(value, axis, steps):
    count = lax.axis_size(axis)
    first, last = (max(0, -steps), min(count, count - steps))
    return lax.ppermute(value, axis, [(source, source + steps) for source in range(first, last)])


def combine_states(earlier, later):
    return (earlier[0] * later[0], later[0][:, None, None] * earlier[1] + later[1])


def split_parts(matrix):
    upper = matrix.astype(jnp.bfloat16)
    lower = (matrix - upper.astype(jnp.float32)).astype(jnp.bfloat16)
    return (upper, lower)


def attend(carried_over_state, query_rows, key_rows, value_rows, visible, score_scale):
    running_max, running_sum, accumulated = carried_over_state
    attention_logits = (
        jnp.einsum("cphm,npm->phcn", query_rows, key_rows, preferred_element_type=jnp.float32)
        * score_scale
    )
    masked = jnp.where(visible, attention_logits, -jnp.inf)
    new_max = jnp.maximum(running_max, jnp.max(masked, axis=-1))
    power_exponent = jnp.exp(masked - new_max[..., None])
    fading = jnp.exp(running_max - new_max)
    new_sum = running_sum * fading + jnp.sum(power_exponent, axis=-1)
    product = jnp.einsum(
        "qyjl,lqu->qyju",
        power_exponent.astype(jnp.bfloat16),
        value_rows,
        preferred_element_type=jnp.float32,
    )
    return (new_max, new_sum, accumulated * fading[..., None] + product)


def body(
    linear_query_rows,
    lin_keys,
    linear_value_rows,
    log_decay,
    norm_gain,
    soft_queries,
    soft_keys,
    soft_values,
    window_start,
):
    row_count, heads_here, head_width = linear_query_rows.shape
    cumulated = jnp.cumsum(log_decay, axis=1)
    token_locations = jnp.arange(row_count, dtype=jnp.int32)
    lower_mask = token_locations[:, None] >= token_locations[None, :]
    tail = jnp.exp(cumulated[:, -1:] - cumulated)
    key_product = lin_keys.astype(jnp.float32) * tail.T[:, :, None]
    key_product_upper, key_product_lower = split_parts(key_product)
    recurrent_state = jnp.einsum(
        "egz,egc->gzc", key_product_upper, linear_value_rows, preferred_element_type=jnp.float32
    )
    recurrent_state = recurrent_state + jnp.einsum(
        "egz,egc->gzc", key_product_lower, linear_value_rows, preferred_element_type=jnp.float32
    )
    falling = jnp.exp(cumulated[:, -1])
    preceding_state, previous = exclusive_scan(
        falling, recurrent_state, jnp.stack([soft_keys, soft_values]), "seq"
    )
    lin_scores = jnp.einsum(
        "thd,shd->hts", linear_query_rows, lin_keys, preferred_element_type=jnp.float32
    )
    gap = jnp.where(lower_mask[None], cumulated[:, :, None] - cumulated[:, None, :], -jnp.inf)
    lin_weights = (lin_scores * jnp.exp(gap)).astype(jnp.bfloat16)
    local_part = jnp.einsum(
        "hts,shd->thd", lin_weights, linear_value_rows, preferred_element_type=jnp.float32
    )
    preceding_upper, preceding_lower = split_parts(preceding_state)
    carried_part = jnp.einsum(
        "nwg,wgq->nwq", linear_query_rows, preceding_upper, preferred_element_type=jnp.float32
    )
    carried_part = carried_part + jnp.einsum(
        "nwg,wgq->nwq", linear_query_rows, preceding_lower, preferred_element_type=jnp.float32
    )
    mixed = local_part + jnp.exp(cumulated).T[:, :, None] * carried_part
    squares = head_sum(jnp.sum(mixed * mixed, axis=(1, 2)), "head")
    lin_out = (
        mixed
        * lax.rsqrt(squares / (HEADS * DH) + 1e-06)[:, None, None]
        * norm_gain.astype(jnp.float32)
    ).astype(jnp.bfloat16)
    kv_here = soft_keys.shape[1]
    group = heads_here // kv_here
    score_scale = float(head_width) ** (-0.5)
    query_rows = soft_queries.reshape(row_count, kv_here, group, head_width)
    block_index = lax.axis_index("seq")
    first_block = window_start[0]
    all_keys = jnp.concatenate([previous[back, 0] for back in range(REACH - 1, -1, -1)] + [soft_keys], axis=0)
    all_values = jnp.concatenate(
        [previous[back, 1] for back in range(REACH - 1, -1, -1)] + [soft_values], axis=0
    )
    key_index = jnp.arange((REACH + 1) * row_count, dtype=jnp.int32)
    key_block = block_index - REACH + key_index // row_count
    causal = (key_index % row_count)[None, :] <= token_locations[:, None]
    visible = ((key_block[None, :] < block_index) | causal) & (key_block[None, :] >= first_block)
    logits = (
        jnp.einsum("cphm,npm->phcn", query_rows, all_keys, preferred_element_type=jnp.float32)
        * score_scale
    )
    masked = jnp.where(visible, logits, -jnp.inf)
    top = jnp.max(masked, axis=-1)
    exps = jnp.exp(masked - top[..., None])
    total = jnp.sum(exps, axis=-1)
    summed = jnp.einsum(
        "qyjl,lqu->qyju", exps.astype(jnp.bfloat16), all_values, preferred_element_type=jnp.float32
    )
    carried_over_state = (top, total, summed)
    final_output = carried_over_state[2] / carried_over_state[1][..., None]
    soft_out = (
        final_output.transpose(2, 0, 1, 3)
        .reshape(row_count, heads_here, head_width)
        .astype(jnp.bfloat16)
    )
    return (lin_out, soft_out)


def solution(mesh):
    placed = (
        P("seq", "head", None),
        P("seq", "head", None),
        P("seq", "head", None),
        P("head", "seq"),
        P("head", None),
        P("seq", "head", None),
        P("seq", "head", None),
        P("seq", "head", None),
        P("seq"),
    )
    return jax.shard_map(
        body,
        mesh=mesh,
        in_specs=placed,
        out_specs=(P("seq", "head", None), P("seq", "head", None)),
        check_vma=False,
    )
```

```python
import functools

import jax
import jax.numpy as jnp
from jax import lax
from jax.experimental import pallas as pl
from jax.experimental.pallas import tpu as pltpu
from jax.sharding import PartitionSpec as P

MESH = pl.DeviceIdType.MESH

DH = 128
HEADS = 64
REACH = 3


def scan_kernel(
    rounds,
    chunks,
    reach,
    fall_ref,
    state_ref,
    sent0_ref,
    kv_ref,
    out_ref,
    kv_out,
    whole,
    whole_fall,
    out_fall,
    got,
    got_fall,
    outgoing,
    outgoing_fall,
    send_sem,
    recv_sem,
    fsend_sem,
    frecv_sem,
    kv_got,
    kv_send,
    kv_recv,
):
    me = lax.axis_index("seq")
    head = lax.axis_index("head")
    length = 2**rounds
    width = state_ref.shape[0] // chunks

    def receives(k):
        return (me - 2**k + length) // length

    def can_send(k):
        return 1 - (me + 2**k) // length

    def ahead(dist):
        return 1 - (me + dist) // length

    def behind(dist):
        return (me - dist + length) // length

    barrier = pltpu.get_barrier_semaphore()
    partners = 0
    for dist in sorted(set([2**k for k in range(rounds)] + list(range(1, reach + 1)))):
        partners = partners + ahead(dist) + behind(dist)

        @pl.when(ahead(dist) == 1)
        def _():
            pl.semaphore_signal(barrier, inc=1, device_id=(me + dist, head), device_id_type=MESH)

        @pl.when(behind(dist) == 1)
        def _():
            pl.semaphore_signal(barrier, inc=1, device_id=(me - dist, head), device_id_type=MESH)

    pl.semaphore_wait(barrier, partners)

    def kv_copy(dist, device):
        return pltpu.make_async_remote_copy(
            src_ref=kv_ref,
            dst_ref=kv_got.at[dist - 1],
            send_sem=kv_send.at[dist - 1],
            recv_sem=kv_recv.at[dist - 1],
            device_id=(device, head),
            device_id_type=MESH,
        )

    for dist in range(1, reach + 1):

        @pl.when(ahead(dist) == 1)
        def _():
            kv_copy(dist, me + dist).start()

    def state_copy(k, c, source, device):
        rows = pl.ds(c * width, width)
        return pltpu.make_async_remote_copy(
            src_ref=source.at[rows],
            dst_ref=got.at[k, rows],
            send_sem=send_sem.at[k, c],
            recv_sem=recv_sem.at[k, c],
            device_id=(device, head),
            device_id_type=MESH,
        )

    def fall_copy(k, device):
        return pltpu.make_async_remote_copy(
            src_ref=outgoing_fall.at[k],
            dst_ref=got_fall.at[k],
            send_sem=fsend_sem.at[k],
            recv_sem=frecv_sem.at[k],
            device_id=(device, head),
            device_id_type=MESH,
        )

    outgoing_fall[0] = fall_ref[...]

    @pl.when(can_send(0) == 1)
    def _():
        fall_copy(0, me + 1).start()
        for c in range(chunks):
            state_copy(0, c, sent0_ref, me + 1).start()

    whole[...] = state_ref[...]
    whole_fall[...] = fall_ref[...]
    out_ref[...] = jnp.zeros_like(out_ref)
    out_fall[...] = jnp.ones_like(out_fall)
    for k in range(rounds):
        last = k == rounds - 1
        for c in range(chunks):
            rows = pl.ds(c * width, width)

            @pl.when(receives(k) == 1)
            def _():
                state_copy(k, c, got.at[k], me - 2**k).wait_recv()
                arrived = got[k, rows].astype(jnp.float32)
                out_ref[rows] = out_fall[rows][:, None, :] * arrived + out_ref[rows]
                if not last:
                    whole[rows] = whole_fall[rows][:, None, :] * arrived + whole[rows]

            if not last:

                @pl.when(can_send(k + 1) == 1)
                def _():
                    outgoing[k + 1, rows] = whole[rows].astype(jnp.bfloat16)
                    state_copy(k + 1, c, outgoing.at[k + 1], me + 2 ** (k + 1)).start()

        @pl.when(receives(k) == 1)
        def _():
            fall_copy(k, me - 2**k).wait_recv()
            arrived = got_fall[k]
            out_fall[...] = arrived * out_fall[...]
            if not last:
                whole_fall[...] = arrived * whole_fall[...]

        if not last:

            @pl.when(can_send(k + 1) == 1)
            def _():
                outgoing_fall[k + 1] = whole_fall[...]
                fall_copy(k + 1, me + 2 ** (k + 1)).start()

    for dist in range(1, reach + 1):

        @pl.when(behind(dist) == 1)
        def _():
            kv_copy(dist, me - dist).wait_recv()
            kv_out[dist - 1] = kv_got[dist - 1]

        @pl.when(behind(dist) == 0)
        def _():
            kv_out[dist - 1] = jnp.zeros_like(kv_out.at[dist - 1])

        @pl.when(ahead(dist) == 1)
        def _():
            kv_copy(dist, me + dist).wait_send()

    for k in range(rounds):

        @pl.when(can_send(k) == 1)
        def _():
            fall_copy(k, me + 2**k).wait_send()
            for c in range(chunks):
                state_copy(k, c, got.at[k], me + 2**k).wait_send()


def exclusive_scan(falling, state, kv, axis):
    length = lax.axis_size(axis)
    rounds = length.bit_length() - 1
    chunks = 8
    heads, rows, columns = state.shape
    fall_rows = jnp.broadcast_to(falling[:, None], (heads, columns))
    vmem = pl.BlockSpec(memory_space=pltpu.VMEM)
    return pl.pallas_call(
        functools.partial(scan_kernel, rounds, chunks, REACH),
        out_shape=(
            jax.ShapeDtypeStruct(state.shape, jnp.float32),
            jax.ShapeDtypeStruct((REACH,) + kv.shape, kv.dtype),
        ),
        in_specs=[vmem] * 4,
        out_specs=(vmem, vmem),
        scratch_shapes=[
            pltpu.VMEM(state.shape, jnp.float32),
            pltpu.VMEM((heads, columns), jnp.float32),
            pltpu.VMEM((heads, columns), jnp.float32),
            pltpu.VMEM((rounds,) + state.shape, jnp.bfloat16),
            pltpu.VMEM((rounds, heads, columns), jnp.float32),
            pltpu.VMEM((rounds,) + state.shape, jnp.bfloat16),
            pltpu.VMEM((rounds, heads, columns), jnp.float32),
            pltpu.SemaphoreType.DMA((rounds, chunks)),
            pltpu.SemaphoreType.DMA((rounds, chunks)),
            pltpu.SemaphoreType.DMA((rounds,)),
            pltpu.SemaphoreType.DMA((rounds,)),
            pltpu.VMEM((REACH,) + kv.shape, kv.dtype),
            pltpu.SemaphoreType.DMA((REACH,)),
            pltpu.SemaphoreType.DMA((REACH,)),
        ],
        compiler_params=pltpu.CompilerParams(collective_id=0, has_side_effects=True),
    )(fall_rows, state, state.astype(jnp.bfloat16), kv)


def head_sum_kernel(count, value_ref, out_ref, slots, send_sem, recv_sem):
    me = lax.axis_index("seq")
    head = lax.axis_index("head")
    barrier = pltpu.get_barrier_semaphore()
    for other in range(count):

        @pl.when(other != head)
        def _():
            pl.semaphore_signal(barrier, inc=1, device_id=(me, other), device_id_type=MESH)

    pl.semaphore_wait(barrier, count - 1)
    slots[head] = value_ref[...]

    def copy(other, slot):
        return pltpu.make_async_remote_copy(
            src_ref=value_ref,
            dst_ref=slots.at[slot],
            send_sem=send_sem.at[other],
            recv_sem=recv_sem.at[slot],
            device_id=(me, other),
            device_id_type=MESH,
        )

    for other in range(count):

        @pl.when(other != head)
        def _():
            copy(other, head).start()

    for other in range(count):

        @pl.when(other != head)
        def _():
            copy(other, other).wait_recv()
            copy(other, head).wait_send()

    total = slots[0]
    for other in range(1, count):
        total = total + slots[other]
    out_ref[...] = total


def head_sum(value, axis):
    count = lax.axis_size(axis)
    vmem = pl.BlockSpec(memory_space=pltpu.VMEM)
    row = value.reshape(1, -1)
    return pl.pallas_call(
        functools.partial(head_sum_kernel, count),
        out_shape=jax.ShapeDtypeStruct(row.shape, row.dtype),
        in_specs=[vmem],
        out_specs=vmem,
        scratch_shapes=[
            pltpu.VMEM((count,) + row.shape, row.dtype),
            pltpu.SemaphoreType.DMA((count,)),
            pltpu.SemaphoreType.DMA((count,)),
        ],
        compiler_params=pltpu.CompilerParams(collective_id=1, has_side_effects=True),
    )(row).reshape(value.shape)


def from_behind(value, axis, steps):
    count = lax.axis_size(axis)
    first, last = (max(0, -steps), min(count, count - steps))
    return lax.ppermute(value, axis, [(source, source + steps) for source in range(first, last)])


def combine_states(earlier, later):
    return (earlier[0] * later[0], later[0][:, None, None] * earlier[1] + later[1])


def split_parts(matrix):
    upper = matrix.astype(jnp.bfloat16)
    lower = (matrix - upper.astype(jnp.float32)).astype(jnp.bfloat16)
    return (upper, lower)


def attend(carried_over_state, query_rows, key_rows, value_rows, visible, score_scale):
    running_max, running_sum, accumulated = carried_over_state
    attention_logits = (
        jnp.einsum("cphm,npm->phcn", query_rows, key_rows, preferred_element_type=jnp.float32)
        * score_scale
    )
    masked = jnp.where(visible, attention_logits, -jnp.inf)
    new_max = jnp.maximum(running_max, jnp.max(masked, axis=-1))
    power_exponent = jnp.exp(masked - new_max[..., None])
    fading = jnp.exp(running_max - new_max)
    new_sum = running_sum * fading + jnp.sum(power_exponent, axis=-1)
    product = jnp.einsum(
        "qyjl,lqu->qyju",
        power_exponent.astype(jnp.bfloat16),
        value_rows,
        preferred_element_type=jnp.float32,
    )
    return (new_max, new_sum, accumulated * fading[..., None] + product)


def body(
    linear_query_rows,
    lin_keys,
    linear_value_rows,
    log_decay,
    norm_gain,
    soft_queries,
    soft_keys,
    soft_values,
    window_start,
):
    row_count, heads_here, head_width = linear_query_rows.shape
    cumulated = jnp.cumsum(log_decay, axis=1)
    token_locations = jnp.arange(row_count, dtype=jnp.int32)
    lower_mask = token_locations[:, None] >= token_locations[None, :]
    tail = jnp.exp(cumulated[:, -1:] - cumulated)
    key_product = lin_keys.astype(jnp.float32) * tail.T[:, :, None]
    key_product_upper, key_product_lower = split_parts(key_product)
    recurrent_state = jnp.einsum(
        "egz,egc->gzc", key_product_upper, linear_value_rows, preferred_element_type=jnp.float32
    )
    recurrent_state = recurrent_state + jnp.einsum(
        "egz,egc->gzc", key_product_lower, linear_value_rows, preferred_element_type=jnp.float32
    )
    falling = jnp.exp(cumulated[:, -1])
    preceding_state, previous = exclusive_scan(
        falling, recurrent_state, jnp.stack([soft_keys, soft_values]), "seq"
    )
    lin_scores = jnp.einsum(
        "thd,shd->hts", linear_query_rows, lin_keys, preferred_element_type=jnp.float32
    )
    gap = jnp.where(lower_mask[None], cumulated[:, :, None] - cumulated[:, None, :], -jnp.inf)
    lin_weights = (lin_scores * jnp.exp(gap)).astype(jnp.bfloat16)
    local_part = jnp.einsum(
        "hts,shd->thd", lin_weights, linear_value_rows, preferred_element_type=jnp.float32
    )
    preceding_upper, preceding_lower = split_parts(preceding_state)
    carried_part = jnp.einsum(
        "nwg,wgq->nwq", linear_query_rows, preceding_upper, preferred_element_type=jnp.float32
    )
    carried_part = carried_part + jnp.einsum(
        "nwg,wgq->nwq", linear_query_rows, preceding_lower, preferred_element_type=jnp.float32
    )
    mixed = local_part + jnp.exp(cumulated).T[:, :, None] * carried_part
    squares = head_sum(jnp.sum(mixed * mixed, axis=(1, 2)), "head")
    lin_out = (
        mixed
        * lax.rsqrt(squares / (HEADS * DH) + 1e-06)[:, None, None]
        * norm_gain.astype(jnp.float32)
    ).astype(jnp.bfloat16)
    kv_here = soft_keys.shape[1]
    group = heads_here // kv_here
    score_scale = float(head_width) ** (-0.5)
    query_rows = soft_queries.reshape(row_count, kv_here, group, head_width)
    block_index = lax.axis_index("seq")
    first_block = window_start[0]
    all_keys = jnp.concatenate([previous[back, 0] for back in range(REACH - 1, -1, -1)] + [soft_keys], axis=0)
    all_values = jnp.concatenate(
        [previous[back, 1] for back in range(REACH - 1, -1, -1)] + [soft_values], axis=0
    )
    key_index = jnp.arange((REACH + 1) * row_count, dtype=jnp.int32)
    key_block = block_index - REACH + key_index // row_count
    causal = (key_index % row_count)[None, :] <= token_locations[:, None]
    visible = ((key_block[None, :] < block_index) | causal) & (key_block[None, :] >= first_block)
    logits = (
        jnp.einsum("cphm,npm->phcn", query_rows, all_keys, preferred_element_type=jnp.float32)
        * score_scale
    )
    masked = jnp.where(visible, logits, -jnp.inf)
    top = jnp.max(masked, axis=-1)
    exps = jnp.exp(masked - top[..., None])
    total = jnp.sum(exps, axis=-1)
    summed = jnp.einsum(
        "qyjl,lqu->qyju", exps.astype(jnp.bfloat16), all_values, preferred_element_type=jnp.float32
    )
    carried_over_state = (top, total, summed)
    final_output = carried_over_state[2] / carried_over_state[1][..., None]
    soft_out = (
        final_output.transpose(2, 0, 1, 3)
        .reshape(row_count, heads_here, head_width)
        .astype(jnp.bfloat16)
    )
    return (lin_out, soft_out)


def solution(mesh):
    placed = (
        P("seq", "head", None),
        P("seq", "head", None),
        P("seq", "head", None),
        P("head", "seq"),
        P("head", None),
        P("seq", "head", None),
        P("seq", "head", None),
        P("seq", "head", None),
        P("seq"),
    )
    return jax.shard_map(
        body,
        mesh=mesh,
        in_specs=placed,
        out_specs=(P("seq", "head", None), P("seq", "head", None)),
        check_vma=False,
    )
```

```python
import functools

import jax
import jax.numpy as jnp
from jax import lax
from jax.experimental import pallas as pl
from jax.experimental.pallas import tpu as pltpu
from jax.sharding import PartitionSpec as P

MESH = pl.DeviceIdType.MESH

DH = 128
HEADS = 64
REACH = 3


def scan_kernel(
    line,
    rounds,
    chunks,
    reach,
    fall_ref,
    state_ref,
    kv_ref,
    out_ref,
    kv_out,
    whole,
    whole_fall,
    out_fall,
    inline,
    inline_fall,
    before_fall,
    after_fall,
    got,
    got_fall,
    outgoing,
    outgoing_fall,
    send_sem,
    recv_sem,
    fsend_sem,
    frecv_sem,
    kv_got,
    kv_send,
    kv_recv,
):
    me = lax.axis_index("seq")
    head = lax.axis_index("head")
    length = line * 2**rounds
    width = state_ref.shape[0] // chunks
    z = me % line
    forward, backward, diagonal = 0, 1, 2

    def ahead(dist):
        return 1 - (me + dist) // length

    def behind(dist):
        return (me - dist + length) // length

    not_first = (z + line - 1) // line
    not_last = 1 - (z + 1) // line
    diag_send = not_first * ahead(line - 1)
    diag_recv = not_last * behind(line - 1)

    barrier = pltpu.get_barrier_semaphore()
    partners = 0
    distances = [line - 1] + [line * 2**r for r in range(rounds)] + list(range(1, reach + 1))
    for dist in sorted(set(distances)):
        partners = partners + ahead(dist) + behind(dist)

        @pl.when(ahead(dist) == 1)
        def _():
            pl.semaphore_signal(barrier, inc=1, device_id=(me + dist, head), device_id_type=MESH)

        @pl.when(behind(dist) == 1)
        def _():
            pl.semaphore_signal(barrier, inc=1, device_id=(me - dist, head), device_id_type=MESH)

    pl.semaphore_wait(barrier, partners)

    def kv_copy(dist, device):
        return pltpu.make_async_remote_copy(
            src_ref=kv_ref,
            dst_ref=kv_got.at[dist - 1],
            send_sem=kv_send.at[dist - 1],
            recv_sem=kv_recv.at[dist - 1],
            device_id=(device, head),
            device_id_type=MESH,
        )

    for dist in range(1, reach + 1):

        @pl.when(ahead(dist) == 1)
        def _():
            kv_copy(dist, me + dist).start()

    def state_copy(stage, source, c, device):
        rows = pl.ds(c * width, width)
        return pltpu.make_async_remote_copy(
            src_ref=outgoing.at[source, rows],
            dst_ref=got.at[stage, rows],
            send_sem=send_sem.at[stage, c],
            recv_sem=recv_sem.at[stage, c],
            device_id=(device, head),
            device_id_type=MESH,
        )

    def fall_copy(stage, source, device):
        return pltpu.make_async_remote_copy(
            src_ref=outgoing_fall.at[source],
            dst_ref=got_fall.at[stage],
            send_sem=fsend_sem.at[stage],
            recv_sem=frecv_sem.at[stage],
            device_id=(device, head),
            device_id_type=MESH,
        )

    def forward_fall():
        before_fall[...] = jnp.ones_like(before_fall)

        @pl.when(not_first == 1)
        def _():
            fall_copy(forward, forward, me - 1).wait_recv()
            before_fall[...] = got_fall[forward]

        inline_fall[...] = before_fall[...] * fall_ref[...]

        @pl.when(not_last == 1)
        def _():
            outgoing_fall[forward] = inline_fall[...]
            fall_copy(forward, forward, me + 1).start()

    def backward_fall():
        after_fall[...] = jnp.ones_like(after_fall)

        @pl.when(not_last == 1)
        def _():
            fall_copy(backward, backward, me + 1).wait_recv()
            after_fall[...] = got_fall[backward]

        @pl.when(not_first == 1)
        def _():
            outgoing_fall[backward] = fall_ref[...] * after_fall[...]
            fall_copy(backward, backward, me - 1).start()

        @pl.when(diag_send == 1)
        def _():
            fall_copy(diagonal, backward, me + line - 1).start()

    def forward_chunk(c):
        rows = pl.ds(c * width, width)
        out_ref[rows] = jnp.zeros_like(out_ref.at[rows])

        @pl.when(not_first == 1)
        def _():
            state_copy(forward, forward, c, me - 1).wait_recv()
            out_ref[rows] = got[forward, rows].astype(jnp.float32)

        inline[rows] = fall_ref[rows][:, None, :] * out_ref[rows] + state_ref[rows]

        @pl.when(not_last == 1)
        def _():
            outgoing[forward, rows] = inline[rows].astype(jnp.bfloat16)
            state_copy(forward, forward, c, me + 1).start()

    def backward_chunk(c):
        rows = pl.ds(c * width, width)

        @pl.when(not_last == 1)
        def _():
            state_copy(backward, backward, c, me + 1).wait_recv()

        @pl.when(not_first == 1)
        def _():
            @pl.when(not_last == 1)
            def _():
                later = got[backward, rows].astype(jnp.float32)
                total = after_fall[rows][:, None, :] * state_ref[rows] + later
                outgoing[backward, rows] = total.astype(jnp.bfloat16)

            @pl.when(not_last == 0)
            def _():
                outgoing[backward, rows] = state_ref[rows].astype(jnp.bfloat16)

            state_copy(backward, backward, c, me - 1).start()

            @pl.when(diag_send == 1)
            def _():
                state_copy(diagonal, backward, c, me + line - 1).start()

    def chains(forward_first):
        if forward_first:
            forward_fall()
            backward_fall()
        else:
            backward_fall()
            forward_fall()
        for c in range(chunks):
            if forward_first:
                forward_chunk(c)
                backward_chunk(c)
            else:
                backward_chunk(c)
                forward_chunk(c)

    @pl.when(z < line // 2)
    def _():
        chains(True)

    @pl.when(z >= line // 2)
    def _():
        chains(False)

    whole_fall[...] = inline_fall[...]
    out_fall[...] = before_fall[...]

    @pl.when(diag_recv == 1)
    def _():
        fall_copy(diagonal, backward, me - line + 1).wait_recv()
        whole_fall[...] = got_fall[diagonal] * inline_fall[...]
        out_fall[...] = got_fall[diagonal] * before_fall[...]

    first_stage = 3
    if rounds > 0:

        @pl.when(ahead(line) == 1)
        def _():
            outgoing_fall[first_stage] = whole_fall[...]
            fall_copy(first_stage, first_stage, me + line).start()

    for c in range(chunks):
        rows = pl.ds(c * width, width)
        whole[rows] = inline[rows]

        @pl.when(diag_recv == 1)
        def _():
            state_copy(diagonal, backward, c, me - line + 1).wait_recv()
            earlier = got[diagonal, rows].astype(jnp.float32)
            whole[rows] = inline_fall[rows][:, None, :] * earlier + inline[rows]
            out_ref[rows] = before_fall[rows][:, None, :] * earlier + out_ref[rows]

        if rounds > 0:

            @pl.when(ahead(line) == 1)
            def _():
                outgoing[first_stage, rows] = whole[rows].astype(jnp.bfloat16)
                state_copy(first_stage, first_stage, c, me + line).start()

    for r in range(rounds):
        stage, shift, last = first_stage + r, line * 2**r, r == rounds - 1
        for c in range(chunks):
            rows = pl.ds(c * width, width)

            @pl.when(behind(shift) == 1)
            def _():
                state_copy(stage, stage, c, me - shift).wait_recv()
                arrived = got[stage, rows].astype(jnp.float32)
                out_ref[rows] = out_fall[rows][:, None, :] * arrived + out_ref[rows]
                if not last:
                    whole[rows] = whole_fall[rows][:, None, :] * arrived + whole[rows]

            if not last:

                @pl.when(ahead(2 * shift) == 1)
                def _():
                    outgoing[stage + 1, rows] = whole[rows].astype(jnp.bfloat16)
                    state_copy(stage + 1, stage + 1, c, me + 2 * shift).start()

        @pl.when(behind(shift) == 1)
        def _():
            fall_copy(stage, stage, me - shift).wait_recv()
            arrived = got_fall[stage]
            out_fall[...] = arrived * out_fall[...]
            if not last:
                whole_fall[...] = arrived * whole_fall[...]

        if not last:

            @pl.when(ahead(2 * shift) == 1)
            def _():
                outgoing_fall[stage + 1] = whole_fall[...]
                fall_copy(stage + 1, stage + 1, me + 2 * shift).start()

    for dist in range(1, reach + 1):

        @pl.when(behind(dist) == 1)
        def _():
            kv_copy(dist, me - dist).wait_recv()
            kv_out[dist - 1] = kv_got[dist - 1]

        @pl.when(behind(dist) == 0)
        def _():
            kv_out[dist - 1] = jnp.zeros_like(kv_out.at[dist - 1])

        @pl.when(ahead(dist) == 1)
        def _():
            kv_copy(dist, me + dist).wait_send()

    sends = [(forward, forward, 1, not_last), (backward, backward, -1, not_first)]
    sends.append((diagonal, backward, line - 1, diag_send))
    sends += [(first_stage + r, first_stage + r, line * 2**r, ahead(line * 2**r)) for r in range(rounds)]
    for stage, source, dist, flag in sends:

        @pl.when(flag == 1)
        def _():
            fall_copy(stage, source, me + dist).wait_send()
            for c in range(chunks):
                state_copy(stage, source, c, me + dist).wait_send()


def exclusive_scan(falling, state, kv, axis):
    line = 8
    length = lax.axis_size(axis)
    rounds = (length // line).bit_length() - 1
    stages = 3 + rounds
    chunks = 8
    heads, rows, columns = state.shape
    fall_rows = jnp.broadcast_to(falling[:, None], (heads, columns))
    vmem = pl.BlockSpec(memory_space=pltpu.VMEM)
    return pl.pallas_call(
        functools.partial(scan_kernel, line, rounds, chunks, REACH),
        out_shape=(
            jax.ShapeDtypeStruct(state.shape, jnp.float32),
            jax.ShapeDtypeStruct((REACH,) + kv.shape, kv.dtype),
        ),
        in_specs=[vmem] * 3,
        out_specs=(vmem, vmem),
        scratch_shapes=[
            pltpu.VMEM(state.shape, jnp.float32),
            pltpu.VMEM((heads, columns), jnp.float32),
            pltpu.VMEM((heads, columns), jnp.float32),
            pltpu.VMEM(state.shape, jnp.float32),
            pltpu.VMEM((heads, columns), jnp.float32),
            pltpu.VMEM((heads, columns), jnp.float32),
            pltpu.VMEM((heads, columns), jnp.float32),
            pltpu.VMEM((stages,) + state.shape, jnp.bfloat16),
            pltpu.VMEM((stages, heads, columns), jnp.float32),
            pltpu.VMEM((stages,) + state.shape, jnp.bfloat16),
            pltpu.VMEM((stages, heads, columns), jnp.float32),
            pltpu.SemaphoreType.DMA((stages, chunks)),
            pltpu.SemaphoreType.DMA((stages, chunks)),
            pltpu.SemaphoreType.DMA((stages,)),
            pltpu.SemaphoreType.DMA((stages,)),
            pltpu.VMEM((REACH,) + kv.shape, kv.dtype),
            pltpu.SemaphoreType.DMA((REACH,)),
            pltpu.SemaphoreType.DMA((REACH,)),
        ],
        compiler_params=pltpu.CompilerParams(collective_id=0, has_side_effects=True),
    )(fall_rows, state, kv)


def head_sum_kernel(count, value_ref, out_ref, slots, send_sem, recv_sem):
    me = lax.axis_index("seq")
    head = lax.axis_index("head")
    barrier = pltpu.get_barrier_semaphore()
    for other in range(count):

        @pl.when(other != head)
        def _():
            pl.semaphore_signal(barrier, inc=1, device_id=(me, other), device_id_type=MESH)

    pl.semaphore_wait(barrier, count - 1)
    slots[head] = value_ref[...]

    def copy(other, slot):
        return pltpu.make_async_remote_copy(
            src_ref=value_ref,
            dst_ref=slots.at[slot],
            send_sem=send_sem.at[other],
            recv_sem=recv_sem.at[slot],
            device_id=(me, other),
            device_id_type=MESH,
        )

    for other in range(count):

        @pl.when(other != head)
        def _():
            copy(other, head).start()

    for other in range(count):

        @pl.when(other != head)
        def _():
            copy(other, other).wait_recv()
            copy(other, head).wait_send()

    total = slots[0]
    for other in range(1, count):
        total = total + slots[other]
    out_ref[...] = total


def head_sum(value, axis):
    count = lax.axis_size(axis)
    vmem = pl.BlockSpec(memory_space=pltpu.VMEM)
    row = value.reshape(1, -1)
    return pl.pallas_call(
        functools.partial(head_sum_kernel, count),
        out_shape=jax.ShapeDtypeStruct(row.shape, row.dtype),
        in_specs=[vmem],
        out_specs=vmem,
        scratch_shapes=[
            pltpu.VMEM((count,) + row.shape, row.dtype),
            pltpu.SemaphoreType.DMA((count,)),
            pltpu.SemaphoreType.DMA((count,)),
        ],
        compiler_params=pltpu.CompilerParams(collective_id=1, has_side_effects=True),
    )(row).reshape(value.shape)


def from_behind(value, axis, steps):
    count = lax.axis_size(axis)
    first, last = (max(0, -steps), min(count, count - steps))
    return lax.ppermute(value, axis, [(source, source + steps) for source in range(first, last)])


def combine_states(earlier, later):
    return (earlier[0] * later[0], later[0][:, None, None] * earlier[1] + later[1])


def split_parts(matrix):
    upper = matrix.astype(jnp.bfloat16)
    lower = (matrix - upper.astype(jnp.float32)).astype(jnp.bfloat16)
    return (upper, lower)


def attend(carried_over_state, query_rows, key_rows, value_rows, visible, score_scale):
    running_max, running_sum, accumulated = carried_over_state
    attention_logits = (
        jnp.einsum("cphm,npm->phcn", query_rows, key_rows, preferred_element_type=jnp.float32)
        * score_scale
    )
    masked = jnp.where(visible, attention_logits, -jnp.inf)
    new_max = jnp.maximum(running_max, jnp.max(masked, axis=-1))
    power_exponent = jnp.exp(masked - new_max[..., None])
    fading = jnp.exp(running_max - new_max)
    new_sum = running_sum * fading + jnp.sum(power_exponent, axis=-1)
    product = jnp.einsum(
        "qyjl,lqu->qyju",
        power_exponent.astype(jnp.bfloat16),
        value_rows,
        preferred_element_type=jnp.float32,
    )
    return (new_max, new_sum, accumulated * fading[..., None] + product)


def body(
    linear_query_rows,
    lin_keys,
    linear_value_rows,
    log_decay,
    norm_gain,
    soft_queries,
    soft_keys,
    soft_values,
    window_start,
):
    row_count, heads_here, head_width = linear_query_rows.shape
    cumulated = jnp.cumsum(log_decay, axis=1)
    token_locations = jnp.arange(row_count, dtype=jnp.int32)
    lower_mask = token_locations[:, None] >= token_locations[None, :]
    tail = jnp.exp(cumulated[:, -1:] - cumulated)
    key_product = lin_keys.astype(jnp.float32) * tail.T[:, :, None]
    key_product_upper, key_product_lower = split_parts(key_product)
    recurrent_state = jnp.einsum(
        "egz,egc->gzc", key_product_upper, linear_value_rows, preferred_element_type=jnp.float32
    )
    recurrent_state = recurrent_state + jnp.einsum(
        "egz,egc->gzc", key_product_lower, linear_value_rows, preferred_element_type=jnp.float32
    )
    falling = jnp.exp(cumulated[:, -1])
    preceding_state, previous = exclusive_scan(
        falling, recurrent_state, jnp.stack([soft_keys, soft_values]), "seq"
    )
    lin_scores = jnp.einsum(
        "thd,shd->hts", linear_query_rows, lin_keys, preferred_element_type=jnp.float32
    )
    gap = jnp.where(lower_mask[None], cumulated[:, :, None] - cumulated[:, None, :], -jnp.inf)
    lin_weights = (lin_scores * jnp.exp(gap)).astype(jnp.bfloat16)
    local_part = jnp.einsum(
        "hts,shd->thd", lin_weights, linear_value_rows, preferred_element_type=jnp.float32
    )
    preceding_upper, preceding_lower = split_parts(preceding_state)
    carried_part = jnp.einsum(
        "nwg,wgq->nwq", linear_query_rows, preceding_upper, preferred_element_type=jnp.float32
    )
    carried_part = carried_part + jnp.einsum(
        "nwg,wgq->nwq", linear_query_rows, preceding_lower, preferred_element_type=jnp.float32
    )
    mixed = local_part + jnp.exp(cumulated).T[:, :, None] * carried_part
    squares = head_sum(jnp.sum(mixed * mixed, axis=(1, 2)), "head")
    lin_out = (
        mixed
        * lax.rsqrt(squares / (HEADS * DH) + 1e-06)[:, None, None]
        * norm_gain.astype(jnp.float32)
    ).astype(jnp.bfloat16)
    kv_here = soft_keys.shape[1]
    group = heads_here // kv_here
    score_scale = float(head_width) ** (-0.5)
    query_rows = soft_queries.reshape(row_count, kv_here, group, head_width)
    block_index = lax.axis_index("seq")
    first_block = window_start[0]
    all_keys = jnp.concatenate([previous[back, 0] for back in range(REACH - 1, -1, -1)] + [soft_keys], axis=0)
    all_values = jnp.concatenate(
        [previous[back, 1] for back in range(REACH - 1, -1, -1)] + [soft_values], axis=0
    )
    key_index = jnp.arange((REACH + 1) * row_count, dtype=jnp.int32)
    key_block = block_index - REACH + key_index // row_count
    causal = (key_index % row_count)[None, :] <= token_locations[:, None]
    visible = ((key_block[None, :] < block_index) | causal) & (key_block[None, :] >= first_block)
    logits = (
        jnp.einsum("cphm,npm->phcn", query_rows, all_keys, preferred_element_type=jnp.float32)
        * score_scale
    )
    masked = jnp.where(visible, logits, -jnp.inf)
    top = jnp.max(masked, axis=-1)
    exps = jnp.exp(masked - top[..., None])
    total = jnp.sum(exps, axis=-1)
    summed = jnp.einsum(
        "qyjl,lqu->qyju", exps.astype(jnp.bfloat16), all_values, preferred_element_type=jnp.float32
    )
    carried_over_state = (top, total, summed)
    final_output = carried_over_state[2] / carried_over_state[1][..., None]
    soft_out = (
        final_output.transpose(2, 0, 1, 3)
        .reshape(row_count, heads_here, head_width)
        .astype(jnp.bfloat16)
    )
    return (lin_out, soft_out)


def solution(mesh):
    placed = (
        P("seq", "head", None),
        P("seq", "head", None),
        P("seq", "head", None),
        P("head", "seq"),
        P("head", None),
        P("seq", "head", None),
        P("seq", "head", None),
        P("seq", "head", None),
        P("seq"),
    )
    return jax.shard_map(
        body,
        mesh=mesh,
        in_specs=placed,
        out_specs=(P("seq", "head", None), P("seq", "head", None)),
        check_vma=False,
    )
```

```python
import functools

import jax
import jax.numpy as jnp
from jax import lax
from jax.experimental import pallas as pl
from jax.experimental.pallas import tpu as pltpu
from jax.sharding import PartitionSpec as P

MESH = pl.DeviceIdType.MESH

DH = 128
HEADS = 64
REACH = 3


def scan_kernel(
    rounds,
    chunks,
    reach,
    fall_ref,
    state_ref,
    sent0_ref,
    kv_ref,
    out_ref,
    kv_out,
    whole,
    whole_fall,
    out_fall,
    suffix,
    suffix_fall,
    got,
    got_fall,
    outgoing,
    outgoing_fall,
    send_sem,
    recv_sem,
    fsend_sem,
    frecv_sem,
    kv_got,
    kv_send,
    kv_recv,
):
    me = lax.axis_index("seq")
    head = lax.axis_index("head")
    length = 2**rounds
    width = state_ref.shape[0] // chunks
    jump = 7
    back0, back1, near = rounds, rounds + 1, rounds + 2

    def ahead(dist):
        return 1 - (me + dist) // length

    def behind(dist):
        return (me - dist + length) // length

    far_recv = behind(jump)
    near_recv = behind(4) * (1 - far_recv)
    near_send = 1 - (me + length - 3) // length

    barrier = pltpu.get_barrier_semaphore()
    partners = 0
    distances = [2**k for k in range(rounds)] + list(range(1, reach + 1)) + [jump]
    for dist in sorted(set(distances)):
        partners = partners + ahead(dist) + behind(dist)

        @pl.when(ahead(dist) == 1)
        def _():
            pl.semaphore_signal(barrier, inc=1, device_id=(me + dist, head), device_id_type=MESH)

        @pl.when(behind(dist) == 1)
        def _():
            pl.semaphore_signal(barrier, inc=1, device_id=(me - dist, head), device_id_type=MESH)

    pl.semaphore_wait(barrier, partners)

    def kv_copy(dist, device):
        return pltpu.make_async_remote_copy(
            src_ref=kv_ref,
            dst_ref=kv_got.at[dist - 1],
            send_sem=kv_send.at[dist - 1],
            recv_sem=kv_recv.at[dist - 1],
            device_id=(device, head),
            device_id_type=MESH,
        )

    for dist in range(1, reach + 1):

        @pl.when(ahead(dist) == 1)
        def _():
            kv_copy(dist, me + dist).start()

    def state_copy(stage, source, c, device):
        rows = pl.ds(c * width, width)
        return pltpu.make_async_remote_copy(
            src_ref=source.at[rows],
            dst_ref=got.at[stage, rows],
            send_sem=send_sem.at[stage, c],
            recv_sem=recv_sem.at[stage, c],
            device_id=(device, head),
            device_id_type=MESH,
        )

    def fall_copy(stage, source, device):
        return pltpu.make_async_remote_copy(
            src_ref=source,
            dst_ref=got_fall.at[stage],
            send_sem=fsend_sem.at[stage],
            recv_sem=frecv_sem.at[stage],
            device_id=(device, head),
            device_id_type=MESH,
        )

    outgoing_fall[0] = fall_ref[...]

    @pl.when(ahead(1) == 1)
    def _():
        fall_copy(0, outgoing_fall.at[0], me + 1).start()
        for c in range(chunks):
            state_copy(0, sent0_ref, c, me + 1).start()

    @pl.when(behind(1) == 1)
    def _():
        fall_copy(back0, outgoing_fall.at[0], me - 1).start()
        for c in range(chunks):
            state_copy(back0, sent0_ref, c, me - 1).start()

    whole[...] = state_ref[...]
    whole_fall[...] = fall_ref[...]
    suffix[...] = state_ref[...]
    suffix_fall[...] = fall_ref[...]
    out_ref[...] = jnp.zeros_like(out_ref)
    out_fall[...] = jnp.ones_like(out_fall)

    def forward_fall(stage, shift):
        @pl.when(behind(shift) == 1)
        def _():
            fall_copy(stage, outgoing_fall.at[stage], me - shift).wait_recv()
            arrived = got_fall[stage]
            out_fall[...] = arrived * out_fall[...]
            whole_fall[...] = arrived * whole_fall[...]

    def forward_chunk(stage, shift, c, update_whole=True):
        rows = pl.ds(c * width, width)

        @pl.when(behind(shift) == 1)
        def _():
            state_copy(stage, outgoing.at[stage], c, me - shift).wait_recv()
            arrived = got[stage, rows].astype(jnp.float32)
            out_ref[rows] = out_fall[rows][:, None, :] * arrived + out_ref[rows]
            if update_whole:
                whole[rows] = whole_fall[rows][:, None, :] * arrived + whole[rows]

    def backward_fall(stage, shift):
        @pl.when(ahead(shift) == 1)
        def _():
            fall_copy(stage, outgoing_fall.at[stage], me + shift).wait_recv()

    def backward_chunk(stage, shift, c):
        rows = pl.ds(c * width, width)

        @pl.when(ahead(shift) == 1)
        def _():
            state_copy(stage, outgoing.at[stage], c, me + shift).wait_recv()
            arrived = got[stage, rows].astype(jnp.float32)
            suffix[rows] = got_fall[stage][rows][:, None, :] * suffix[rows] + arrived

    def backward_fall_update(stage, shift):
        @pl.when(ahead(shift) == 1)
        def _():
            suffix_fall[...] = suffix_fall[...] * got_fall[stage]

    def send(stage, flag, buffer, buffer_fall, dist, c):
        rows = pl.ds(c * width, width)

        @pl.when(flag == 1)
        def _():
            if c == 0:
                outgoing_fall[stage] = buffer_fall[...]
                fall_copy(stage, outgoing_fall.at[stage], me + dist).start()
            outgoing[stage, rows] = buffer[rows].astype(jnp.bfloat16)
            state_copy(stage, outgoing.at[stage], c, me + dist).start()

    for stage, back, shift in ((0, back0, 1), (1, back1, 2)):
        backward_fall(back, shift)
        for c in range(chunks):
            rows = pl.ds(c * width, width)
            forward_chunk(stage, shift, c)
            backward_chunk(back, shift, c)
        forward_fall(stage, shift)
        backward_fall_update(back, shift)
        if stage == 0:
            for c in range(chunks):
                send(1, ahead(2), whole, whole_fall, 2, c)
                send(back1, behind(2), suffix, suffix_fall, -2, c)
        else:
            for c in range(chunks):
                send(2, ahead(jump), suffix, suffix_fall, jump, c)
                send(near, near_send, whole, whole_fall, 4, c)

    for c in range(chunks):
        rows = pl.ds(c * width, width)
        for flag, dist, stage in ((far_recv, jump, 2), (near_recv, 4, near)):

            @pl.when(flag == 1)
            def _():
                state_copy(stage, outgoing.at[stage], c, me - dist).wait_recv()
                arrived = got[stage, rows].astype(jnp.float32)
                out_ref[rows] = out_fall[rows][:, None, :] * arrived + out_ref[rows]
                whole[rows] = whole_fall[rows][:, None, :] * arrived + whole[rows]

    for flag, dist, stage in ((far_recv, jump, 2), (near_recv, 4, near)):

        @pl.when(flag == 1)
        def _():
            fall_copy(stage, outgoing_fall.at[stage], me - dist).wait_recv()
            arrived = got_fall[stage]
            out_fall[...] = arrived * out_fall[...]
            whole_fall[...] = arrived * whole_fall[...]

    if rounds > 3:
        for c in range(chunks):
            send(3, ahead(8), whole, whole_fall, 8, c)

    for k in range(3, rounds):
        shift, last = 2**k, k == rounds - 1
        for c in range(chunks):
            forward_chunk(k, shift, c, update_whole=not last)
            if not last:
                rows = pl.ds(c * width, width)

                @pl.when(ahead(2 * shift) == 1)
                def _():
                    outgoing[k + 1, rows] = whole[rows].astype(jnp.bfloat16)
                    state_copy(k + 1, outgoing.at[k + 1], c, me + 2 * shift).start()

        @pl.when(behind(shift) == 1)
        def _():
            fall_copy(k, outgoing_fall.at[k], me - shift).wait_recv()
            arrived = got_fall[k]
            out_fall[...] = arrived * out_fall[...]
            if not last:
                whole_fall[...] = arrived * whole_fall[...]

        if not last:

            @pl.when(ahead(2 * shift) == 1)
            def _():
                outgoing_fall[k + 1] = whole_fall[...]
                fall_copy(k + 1, outgoing_fall.at[k + 1], me + 2 * shift).start()

    for dist in range(1, reach + 1):

        @pl.when(behind(dist) == 1)
        def _():
            kv_copy(dist, me - dist).wait_recv()
            kv_out[dist - 1] = kv_got[dist - 1]

        @pl.when(behind(dist) == 0)
        def _():
            kv_out[dist - 1] = jnp.zeros_like(kv_out.at[dist - 1])

        @pl.when(ahead(dist) == 1)
        def _():
            kv_copy(dist, me + dist).wait_send()

    sends = [(0, 1, ahead(1)), (back0, -1, behind(1)), (1, 2, ahead(2)), (back1, -2, behind(2))]
    sends += [(2, jump, ahead(jump)), (near, 4, near_send)]
    sends += [(k, 2**k, ahead(2**k)) for k in range(3, rounds)]
    for stage, dist, flag in sends:

        @pl.when(flag == 1)
        def _():
            fall_copy(stage, outgoing_fall.at[stage], me + dist).wait_send()
            for c in range(chunks):
                state_copy(stage, outgoing.at[stage], c, me + dist).wait_send()


def exclusive_scan(falling, state, kv, axis):
    length = lax.axis_size(axis)
    rounds = length.bit_length() - 1
    stages = rounds + 3
    chunks = 8
    heads, rows, columns = state.shape
    fall_rows = jnp.broadcast_to(falling[:, None], (heads, columns))
    vmem = pl.BlockSpec(memory_space=pltpu.VMEM)
    return pl.pallas_call(
        functools.partial(scan_kernel, rounds, chunks, REACH),
        out_shape=(
            jax.ShapeDtypeStruct(state.shape, jnp.float32),
            jax.ShapeDtypeStruct((REACH,) + kv.shape, kv.dtype),
        ),
        in_specs=[vmem] * 4,
        out_specs=(vmem, vmem),
        scratch_shapes=[
            pltpu.VMEM(state.shape, jnp.float32),
            pltpu.VMEM((heads, columns), jnp.float32),
            pltpu.VMEM((heads, columns), jnp.float32),
            pltpu.VMEM(state.shape, jnp.float32),
            pltpu.VMEM((heads, columns), jnp.float32),
            pltpu.VMEM((stages,) + state.shape, jnp.bfloat16),
            pltpu.VMEM((stages, heads, columns), jnp.float32),
            pltpu.VMEM((stages,) + state.shape, jnp.bfloat16),
            pltpu.VMEM((stages, heads, columns), jnp.float32),
            pltpu.SemaphoreType.DMA((stages, chunks)),
            pltpu.SemaphoreType.DMA((stages, chunks)),
            pltpu.SemaphoreType.DMA((stages,)),
            pltpu.SemaphoreType.DMA((stages,)),
            pltpu.VMEM((REACH,) + kv.shape, kv.dtype),
            pltpu.SemaphoreType.DMA((REACH,)),
            pltpu.SemaphoreType.DMA((REACH,)),
        ],
        compiler_params=pltpu.CompilerParams(collective_id=0, has_side_effects=True),
    )(fall_rows, state, state.astype(jnp.bfloat16), kv)


def head_sum_kernel(count, value_ref, out_ref, slots, send_sem, recv_sem):
    me = lax.axis_index("seq")
    head = lax.axis_index("head")
    barrier = pltpu.get_barrier_semaphore()
    for other in range(count):

        @pl.when(other != head)
        def _():
            pl.semaphore_signal(barrier, inc=1, device_id=(me, other), device_id_type=MESH)

    pl.semaphore_wait(barrier, count - 1)
    slots[head] = value_ref[...]

    def copy(other, slot):
        return pltpu.make_async_remote_copy(
            src_ref=value_ref,
            dst_ref=slots.at[slot],
            send_sem=send_sem.at[other],
            recv_sem=recv_sem.at[slot],
            device_id=(me, other),
            device_id_type=MESH,
        )

    for other in range(count):

        @pl.when(other != head)
        def _():
            copy(other, head).start()

    for other in range(count):

        @pl.when(other != head)
        def _():
            copy(other, other).wait_recv()
            copy(other, head).wait_send()

    total = slots[0]
    for other in range(1, count):
        total = total + slots[other]
    out_ref[...] = total


def head_sum(value, axis):
    count = lax.axis_size(axis)
    vmem = pl.BlockSpec(memory_space=pltpu.VMEM)
    row = value.reshape(1, -1)
    return pl.pallas_call(
        functools.partial(head_sum_kernel, count),
        out_shape=jax.ShapeDtypeStruct(row.shape, row.dtype),
        in_specs=[vmem],
        out_specs=vmem,
        scratch_shapes=[
            pltpu.VMEM((count,) + row.shape, row.dtype),
            pltpu.SemaphoreType.DMA((count,)),
            pltpu.SemaphoreType.DMA((count,)),
        ],
        compiler_params=pltpu.CompilerParams(collective_id=1, has_side_effects=True),
    )(row).reshape(value.shape)


def from_behind(value, axis, steps):
    count = lax.axis_size(axis)
    first, last = (max(0, -steps), min(count, count - steps))
    return lax.ppermute(value, axis, [(source, source + steps) for source in range(first, last)])


def combine_states(earlier, later):
    return (earlier[0] * later[0], later[0][:, None, None] * earlier[1] + later[1])


def split_parts(matrix):
    upper = matrix.astype(jnp.bfloat16)
    lower = (matrix - upper.astype(jnp.float32)).astype(jnp.bfloat16)
    return (upper, lower)


def attend(carried_over_state, query_rows, key_rows, value_rows, visible, score_scale):
    running_max, running_sum, accumulated = carried_over_state
    attention_logits = (
        jnp.einsum("cphm,npm->phcn", query_rows, key_rows, preferred_element_type=jnp.float32)
        * score_scale
    )
    masked = jnp.where(visible, attention_logits, -jnp.inf)
    new_max = jnp.maximum(running_max, jnp.max(masked, axis=-1))
    power_exponent = jnp.exp(masked - new_max[..., None])
    fading = jnp.exp(running_max - new_max)
    new_sum = running_sum * fading + jnp.sum(power_exponent, axis=-1)
    product = jnp.einsum(
        "qyjl,lqu->qyju",
        power_exponent.astype(jnp.bfloat16),
        value_rows,
        preferred_element_type=jnp.float32,
    )
    return (new_max, new_sum, accumulated * fading[..., None] + product)


def body(
    linear_query_rows,
    lin_keys,
    linear_value_rows,
    log_decay,
    norm_gain,
    soft_queries,
    soft_keys,
    soft_values,
    window_start,
):
    row_count, heads_here, head_width = linear_query_rows.shape
    cumulated = jnp.cumsum(log_decay, axis=1)
    token_locations = jnp.arange(row_count, dtype=jnp.int32)
    lower_mask = token_locations[:, None] >= token_locations[None, :]
    tail = jnp.exp(cumulated[:, -1:] - cumulated)
    key_product = lin_keys.astype(jnp.float32) * tail.T[:, :, None]
    key_product_upper, key_product_lower = split_parts(key_product)
    recurrent_state = jnp.einsum(
        "egz,egc->gzc", key_product_upper, linear_value_rows, preferred_element_type=jnp.float32
    )
    recurrent_state = recurrent_state + jnp.einsum(
        "egz,egc->gzc", key_product_lower, linear_value_rows, preferred_element_type=jnp.float32
    )
    falling = jnp.exp(cumulated[:, -1])
    preceding_state, previous = exclusive_scan(
        falling, recurrent_state, jnp.stack([soft_keys, soft_values]), "seq"
    )
    lin_scores = jnp.einsum(
        "thd,shd->hts", linear_query_rows, lin_keys, preferred_element_type=jnp.float32
    )
    gap = jnp.where(lower_mask[None], cumulated[:, :, None] - cumulated[:, None, :], -jnp.inf)
    lin_weights = (lin_scores * jnp.exp(gap)).astype(jnp.bfloat16)
    local_part = jnp.einsum(
        "hts,shd->thd", lin_weights, linear_value_rows, preferred_element_type=jnp.float32
    )
    preceding_upper, preceding_lower = split_parts(preceding_state)
    carried_part = jnp.einsum(
        "nwg,wgq->nwq", linear_query_rows, preceding_upper, preferred_element_type=jnp.float32
    )
    carried_part = carried_part + jnp.einsum(
        "nwg,wgq->nwq", linear_query_rows, preceding_lower, preferred_element_type=jnp.float32
    )
    mixed = local_part + jnp.exp(cumulated).T[:, :, None] * carried_part
    squares = head_sum(jnp.sum(mixed * mixed, axis=(1, 2)), "head")
    lin_out = (
        mixed
        * lax.rsqrt(squares / (HEADS * DH) + 1e-06)[:, None, None]
        * norm_gain.astype(jnp.float32)
    ).astype(jnp.bfloat16)
    kv_here = soft_keys.shape[1]
    group = heads_here // kv_here
    score_scale = float(head_width) ** (-0.5)
    query_rows = soft_queries.reshape(row_count, kv_here, group, head_width)
    block_index = lax.axis_index("seq")
    first_block = window_start[0]
    all_keys = jnp.concatenate([previous[back, 0] for back in range(REACH - 1, -1, -1)] + [soft_keys], axis=0)
    all_values = jnp.concatenate(
        [previous[back, 1] for back in range(REACH - 1, -1, -1)] + [soft_values], axis=0
    )
    key_index = jnp.arange((REACH + 1) * row_count, dtype=jnp.int32)
    key_block = block_index - REACH + key_index // row_count
    causal = (key_index % row_count)[None, :] <= token_locations[:, None]
    visible = ((key_block[None, :] < block_index) | causal) & (key_block[None, :] >= first_block)
    logits = (
        jnp.einsum("cphm,npm->phcn", query_rows, all_keys, preferred_element_type=jnp.float32)
        * score_scale
    )
    masked = jnp.where(visible, logits, -jnp.inf)
    top = jnp.max(masked, axis=-1)
    exps = jnp.exp(masked - top[..., None])
    total = jnp.sum(exps, axis=-1)
    summed = jnp.einsum(
        "qyjl,lqu->qyju", exps.astype(jnp.bfloat16), all_values, preferred_element_type=jnp.float32
    )
    carried_over_state = (top, total, summed)
    final_output = carried_over_state[2] / carried_over_state[1][..., None]
    soft_out = (
        final_output.transpose(2, 0, 1, 3)
        .reshape(row_count, heads_here, head_width)
        .astype(jnp.bfloat16)
    )
    return (lin_out, soft_out)


def solution(mesh):
    placed = (
        P("seq", "head", None),
        P("seq", "head", None),
        P("seq", "head", None),
        P("head", "seq"),
        P("head", None),
        P("seq", "head", None),
        P("seq", "head", None),
        P("seq", "head", None),
        P("seq"),
    )
    return jax.shard_map(
        body,
        mesh=mesh,
        in_specs=placed,
        out_specs=(P("seq", "head", None), P("seq", "head", None)),
        check_vma=False,
    )
```

```python
import functools

import jax
import jax.numpy as jnp
from jax import lax
from jax.experimental import pallas as pl
from jax.experimental.pallas import tpu as pltpu
from jax.sharding import PartitionSpec as P

MESH = pl.DeviceIdType.MESH

DH = 128
HEADS = 64
REACH = 3


def scan_kernel(
    rounds,
    chunks,
    reach,
    fall_ref,
    state_ref,
    sent0_ref,
    kv_ref,
    out_ref,
    kv_out,
    whole,
    whole_fall,
    out_fall,
    suffix,
    suffix_fall,
    got,
    got_fall,
    outgoing,
    outgoing_fall,
    send_sem,
    recv_sem,
    fsend_sem,
    frecv_sem,
    kv_got,
    kv_send,
    kv_recv,
):
    me = lax.axis_index("seq")
    head = lax.axis_index("head")
    length = 2**rounds
    width = state_ref.shape[0] // chunks
    jump = 7
    back0, back1, near = rounds, rounds + 1, rounds + 2

    def ahead(dist):
        return 1 - (me + dist) // length

    def behind(dist):
        return (me - dist + length) // length

    far_recv = behind(jump)
    near_recv = behind(4) * (1 - far_recv)
    near_send = 1 - (me + length - 3) // length

    barrier = pltpu.get_barrier_semaphore()
    partners = 0
    distances = [2**k for k in range(rounds)] + list(range(1, reach + 1)) + [jump]
    for dist in sorted(set(distances)):
        partners = partners + ahead(dist) + behind(dist)

        @pl.when(ahead(dist) == 1)
        def _():
            pl.semaphore_signal(barrier, inc=1, device_id=(me + dist, head), device_id_type=MESH)

        @pl.when(behind(dist) == 1)
        def _():
            pl.semaphore_signal(barrier, inc=1, device_id=(me - dist, head), device_id_type=MESH)

    pl.semaphore_wait(barrier, partners)

    def kv_copy(dist, device):
        return pltpu.make_async_remote_copy(
            src_ref=kv_ref,
            dst_ref=kv_got.at[dist - 1],
            send_sem=kv_send.at[dist - 1],
            recv_sem=kv_recv.at[dist - 1],
            device_id=(device, head),
            device_id_type=MESH,
        )

    for dist in range(1, reach + 1):

        @pl.when(ahead(dist) == 1)
        def _():
            kv_copy(dist, me + dist).start()

    def state_copy(stage, source, c, device):
        rows = pl.ds(c * width, width)
        return pltpu.make_async_remote_copy(
            src_ref=source.at[rows],
            dst_ref=got.at[stage, rows],
            send_sem=send_sem.at[stage, c],
            recv_sem=recv_sem.at[stage, c],
            device_id=(device, head),
            device_id_type=MESH,
        )

    def fall_copy(stage, source, device):
        return pltpu.make_async_remote_copy(
            src_ref=source,
            dst_ref=got_fall.at[stage],
            send_sem=fsend_sem.at[stage],
            recv_sem=frecv_sem.at[stage],
            device_id=(device, head),
            device_id_type=MESH,
        )

    outgoing_fall[0] = fall_ref[...]

    @pl.when(ahead(1) == 1)
    def _():
        fall_copy(0, outgoing_fall.at[0], me + 1).start()
        for c in range(chunks):
            state_copy(0, sent0_ref, c, me + 1).start()

    @pl.when(behind(1) == 1)
    def _():
        fall_copy(back0, outgoing_fall.at[0], me - 1).start()
        for c in range(chunks):
            state_copy(back0, sent0_ref, c, me - 1).start()

    whole[...] = state_ref[...]
    whole_fall[...] = fall_ref[...]
    suffix[...] = state_ref[...]
    suffix_fall[...] = fall_ref[...]
    out_ref[...] = jnp.zeros_like(out_ref)
    out_fall[...] = jnp.ones_like(out_fall)

    def forward_fall(stage, shift):
        @pl.when(behind(shift) == 1)
        def _():
            fall_copy(stage, outgoing_fall.at[stage], me - shift).wait_recv()
            arrived = got_fall[stage]
            out_fall[...] = arrived * out_fall[...]
            whole_fall[...] = arrived * whole_fall[...]

    def forward_chunk(stage, shift, c, update_whole=True):
        rows = pl.ds(c * width, width)

        @pl.when(behind(shift) == 1)
        def _():
            state_copy(stage, outgoing.at[stage], c, me - shift).wait_recv()
            arrived = got[stage, rows].astype(jnp.float32)
            out_ref[rows] = out_fall[rows][:, None, :] * arrived + out_ref[rows]
            if update_whole:
                whole[rows] = whole_fall[rows][:, None, :] * arrived + whole[rows]

    def backward_fall(stage, shift):
        @pl.when(ahead(shift) == 1)
        def _():
            fall_copy(stage, outgoing_fall.at[stage], me + shift).wait_recv()
            suffix_fall[...] = suffix_fall[...] * got_fall[stage]

    def backward_chunk(stage, shift, c):
        rows = pl.ds(c * width, width)

        @pl.when(ahead(shift) == 1)
        def _():
            state_copy(stage, outgoing.at[stage], c, me + shift).wait_recv()
            arrived = got[stage, rows].astype(jnp.float32)
            suffix[rows] = got_fall[stage][rows][:, None, :] * suffix[rows] + arrived

    def send_chunk(stage, flag, buffer, dist, c):
        rows = pl.ds(c * width, width)

        @pl.when(flag == 1)
        def _():
            outgoing[stage, rows] = buffer[rows].astype(jnp.bfloat16)
            state_copy(stage, outgoing.at[stage], c, me + dist).start()

    def send_fall(stage, flag, buffer_fall, dist):
        @pl.when(flag == 1)
        def _():
            outgoing_fall[stage] = buffer_fall[...]
            fall_copy(stage, outgoing_fall.at[stage], me + dist).start()

    backward_fall(back0, 1)
    send_fall(back1, behind(2), suffix_fall, -2)
    for c in range(chunks):
        forward_chunk(0, 1, c)
        send_chunk(1, ahead(2), whole, 2, c)
        backward_chunk(back0, 1, c)
        send_chunk(back1, behind(2), suffix, -2, c)
    forward_fall(0, 1)
    send_fall(1, ahead(2), whole_fall, 2)

    backward_fall(back1, 2)
    send_fall(2, ahead(jump), suffix_fall, jump)
    for c in range(chunks):
        forward_chunk(1, 2, c)
        send_chunk(near, near_send, whole, 4, c)
        backward_chunk(back1, 2, c)
        send_chunk(2, ahead(jump), suffix, jump, c)
    forward_fall(1, 2)
    send_fall(near, near_send, whole_fall, 4)

    for c in range(chunks):
        rows = pl.ds(c * width, width)
        for flag, dist, stage in ((far_recv, jump, 2), (near_recv, 4, near)):

            @pl.when(flag == 1)
            def _():
                state_copy(stage, outgoing.at[stage], c, me - dist).wait_recv()
                arrived = got[stage, rows].astype(jnp.float32)
                out_ref[rows] = out_fall[rows][:, None, :] * arrived + out_ref[rows]
                whole[rows] = whole_fall[rows][:, None, :] * arrived + whole[rows]

        if rounds > 3:
            send_chunk(3, ahead(8), whole, 8, c)

    for flag, dist, stage in ((far_recv, jump, 2), (near_recv, 4, near)):

        @pl.when(flag == 1)
        def _():
            fall_copy(stage, outgoing_fall.at[stage], me - dist).wait_recv()
            arrived = got_fall[stage]
            out_fall[...] = arrived * out_fall[...]
            whole_fall[...] = arrived * whole_fall[...]

    if rounds > 3:
        send_fall(3, ahead(8), whole_fall, 8)

    for k in range(3, rounds):
        shift, last = 2**k, k == rounds - 1
        for c in range(chunks):
            forward_chunk(k, shift, c, update_whole=not last)
            if not last:
                rows = pl.ds(c * width, width)

                @pl.when(ahead(2 * shift) == 1)
                def _():
                    outgoing[k + 1, rows] = whole[rows].astype(jnp.bfloat16)
                    state_copy(k + 1, outgoing.at[k + 1], c, me + 2 * shift).start()

        @pl.when(behind(shift) == 1)
        def _():
            fall_copy(k, outgoing_fall.at[k], me - shift).wait_recv()
            arrived = got_fall[k]
            out_fall[...] = arrived * out_fall[...]
            if not last:
                whole_fall[...] = arrived * whole_fall[...]

        if not last:

            @pl.when(ahead(2 * shift) == 1)
            def _():
                outgoing_fall[k + 1] = whole_fall[...]
                fall_copy(k + 1, outgoing_fall.at[k + 1], me + 2 * shift).start()

    for dist in range(1, reach + 1):

        @pl.when(behind(dist) == 1)
        def _():
            kv_copy(dist, me - dist).wait_recv()
            kv_out[dist - 1] = kv_got[dist - 1]

        @pl.when(behind(dist) == 0)
        def _():
            kv_out[dist - 1] = jnp.zeros_like(kv_out.at[dist - 1])

        @pl.when(ahead(dist) == 1)
        def _():
            kv_copy(dist, me + dist).wait_send()

    sends = [(0, 1, ahead(1)), (back0, -1, behind(1)), (1, 2, ahead(2)), (back1, -2, behind(2))]
    sends += [(2, jump, ahead(jump)), (near, 4, near_send)]
    sends += [(k, 2**k, ahead(2**k)) for k in range(3, rounds)]
    for stage, dist, flag in sends:

        @pl.when(flag == 1)
        def _():
            fall_copy(stage, outgoing_fall.at[stage], me + dist).wait_send()
            for c in range(chunks):
                state_copy(stage, outgoing.at[stage], c, me + dist).wait_send()


def exclusive_scan(falling, state, kv, axis):
    length = lax.axis_size(axis)
    rounds = length.bit_length() - 1
    stages = rounds + 3
    chunks = 8
    heads, rows, columns = state.shape
    fall_rows = jnp.broadcast_to(falling[:, None], (heads, columns))
    vmem = pl.BlockSpec(memory_space=pltpu.VMEM)
    return pl.pallas_call(
        functools.partial(scan_kernel, rounds, chunks, REACH),
        out_shape=(
            jax.ShapeDtypeStruct(state.shape, jnp.float32),
            jax.ShapeDtypeStruct((REACH,) + kv.shape, kv.dtype),
        ),
        in_specs=[vmem] * 4,
        out_specs=(vmem, vmem),
        scratch_shapes=[
            pltpu.VMEM(state.shape, jnp.float32),
            pltpu.VMEM((heads, columns), jnp.float32),
            pltpu.VMEM((heads, columns), jnp.float32),
            pltpu.VMEM(state.shape, jnp.float32),
            pltpu.VMEM((heads, columns), jnp.float32),
            pltpu.VMEM((stages,) + state.shape, jnp.bfloat16),
            pltpu.VMEM((stages, heads, columns), jnp.float32),
            pltpu.VMEM((stages,) + state.shape, jnp.bfloat16),
            pltpu.VMEM((stages, heads, columns), jnp.float32),
            pltpu.SemaphoreType.DMA((stages, chunks)),
            pltpu.SemaphoreType.DMA((stages, chunks)),
            pltpu.SemaphoreType.DMA((stages,)),
            pltpu.SemaphoreType.DMA((stages,)),
            pltpu.VMEM((REACH,) + kv.shape, kv.dtype),
            pltpu.SemaphoreType.DMA((REACH,)),
            pltpu.SemaphoreType.DMA((REACH,)),
        ],
        compiler_params=pltpu.CompilerParams(collective_id=0, has_side_effects=True),
    )(fall_rows, state, state.astype(jnp.bfloat16), kv)


def head_sum_kernel(count, value_ref, out_ref, slots, send_sem, recv_sem):
    me = lax.axis_index("seq")
    head = lax.axis_index("head")
    barrier = pltpu.get_barrier_semaphore()
    for other in range(count):

        @pl.when(other != head)
        def _():
            pl.semaphore_signal(barrier, inc=1, device_id=(me, other), device_id_type=MESH)

    pl.semaphore_wait(barrier, count - 1)
    slots[head] = value_ref[...]

    def copy(other, slot):
        return pltpu.make_async_remote_copy(
            src_ref=value_ref,
            dst_ref=slots.at[slot],
            send_sem=send_sem.at[other],
            recv_sem=recv_sem.at[slot],
            device_id=(me, other),
            device_id_type=MESH,
        )

    for other in range(count):

        @pl.when(other != head)
        def _():
            copy(other, head).start()

    for other in range(count):

        @pl.when(other != head)
        def _():
            copy(other, other).wait_recv()
            copy(other, head).wait_send()

    total = slots[0]
    for other in range(1, count):
        total = total + slots[other]
    out_ref[...] = total


def head_sum(value, axis):
    count = lax.axis_size(axis)
    vmem = pl.BlockSpec(memory_space=pltpu.VMEM)
    row = value.reshape(1, -1)
    return pl.pallas_call(
        functools.partial(head_sum_kernel, count),
        out_shape=jax.ShapeDtypeStruct(row.shape, row.dtype),
        in_specs=[vmem],
        out_specs=vmem,
        scratch_shapes=[
            pltpu.VMEM((count,) + row.shape, row.dtype),
            pltpu.SemaphoreType.DMA((count,)),
            pltpu.SemaphoreType.DMA((count,)),
        ],
        compiler_params=pltpu.CompilerParams(collective_id=1, has_side_effects=True),
    )(row).reshape(value.shape)


def from_behind(value, axis, steps):
    count = lax.axis_size(axis)
    first, last = (max(0, -steps), min(count, count - steps))
    return lax.ppermute(value, axis, [(source, source + steps) for source in range(first, last)])


def combine_states(earlier, later):
    return (earlier[0] * later[0], later[0][:, None, None] * earlier[1] + later[1])


def split_parts(matrix):
    upper = matrix.astype(jnp.bfloat16)
    lower = (matrix - upper.astype(jnp.float32)).astype(jnp.bfloat16)
    return (upper, lower)


def attend(carried_over_state, query_rows, key_rows, value_rows, visible, score_scale):
    running_max, running_sum, accumulated = carried_over_state
    attention_logits = (
        jnp.einsum("cphm,npm->phcn", query_rows, key_rows, preferred_element_type=jnp.float32)
        * score_scale
    )
    masked = jnp.where(visible, attention_logits, -jnp.inf)
    new_max = jnp.maximum(running_max, jnp.max(masked, axis=-1))
    power_exponent = jnp.exp(masked - new_max[..., None])
    fading = jnp.exp(running_max - new_max)
    new_sum = running_sum * fading + jnp.sum(power_exponent, axis=-1)
    product = jnp.einsum(
        "qyjl,lqu->qyju",
        power_exponent.astype(jnp.bfloat16),
        value_rows,
        preferred_element_type=jnp.float32,
    )
    return (new_max, new_sum, accumulated * fading[..., None] + product)


def body(
    linear_query_rows,
    lin_keys,
    linear_value_rows,
    log_decay,
    norm_gain,
    soft_queries,
    soft_keys,
    soft_values,
    window_start,
):
    row_count, heads_here, head_width = linear_query_rows.shape
    cumulated = jnp.cumsum(log_decay, axis=1)
    token_locations = jnp.arange(row_count, dtype=jnp.int32)
    lower_mask = token_locations[:, None] >= token_locations[None, :]
    tail = jnp.exp(cumulated[:, -1:] - cumulated)
    key_product = lin_keys.astype(jnp.float32) * tail.T[:, :, None]
    key_product_upper, key_product_lower = split_parts(key_product)
    recurrent_state = jnp.einsum(
        "egz,egc->gzc", key_product_upper, linear_value_rows, preferred_element_type=jnp.float32
    )
    recurrent_state = recurrent_state + jnp.einsum(
        "egz,egc->gzc", key_product_lower, linear_value_rows, preferred_element_type=jnp.float32
    )
    falling = jnp.exp(cumulated[:, -1])
    preceding_state, previous = exclusive_scan(
        falling, recurrent_state, jnp.stack([soft_keys, soft_values]), "seq"
    )
    lin_scores = jnp.einsum(
        "thd,shd->hts", linear_query_rows, lin_keys, preferred_element_type=jnp.float32
    )
    gap = jnp.where(lower_mask[None], cumulated[:, :, None] - cumulated[:, None, :], -jnp.inf)
    lin_weights = (lin_scores * jnp.exp(gap)).astype(jnp.bfloat16)
    local_part = jnp.einsum(
        "hts,shd->thd", lin_weights, linear_value_rows, preferred_element_type=jnp.float32
    )
    preceding_upper, preceding_lower = split_parts(preceding_state)
    carried_part = jnp.einsum(
        "nwg,wgq->nwq", linear_query_rows, preceding_upper, preferred_element_type=jnp.float32
    )
    carried_part = carried_part + jnp.einsum(
        "nwg,wgq->nwq", linear_query_rows, preceding_lower, preferred_element_type=jnp.float32
    )
    mixed = local_part + jnp.exp(cumulated).T[:, :, None] * carried_part
    squares = head_sum(jnp.sum(mixed * mixed, axis=(1, 2)), "head")
    lin_out = (
        mixed
        * lax.rsqrt(squares / (HEADS * DH) + 1e-06)[:, None, None]
        * norm_gain.astype(jnp.float32)
    ).astype(jnp.bfloat16)
    kv_here = soft_keys.shape[1]
    group = heads_here // kv_here
    score_scale = float(head_width) ** (-0.5)
    query_rows = soft_queries.reshape(row_count, kv_here, group, head_width)
    block_index = lax.axis_index("seq")
    first_block = window_start[0]
    all_keys = jnp.concatenate([previous[back, 0] for back in range(REACH - 1, -1, -1)] + [soft_keys], axis=0)
    all_values = jnp.concatenate(
        [previous[back, 1] for back in range(REACH - 1, -1, -1)] + [soft_values], axis=0
    )
    key_index = jnp.arange((REACH + 1) * row_count, dtype=jnp.int32)
    key_block = block_index - REACH + key_index // row_count
    causal = (key_index % row_count)[None, :] <= token_locations[:, None]
    visible = ((key_block[None, :] < block_index) | causal) & (key_block[None, :] >= first_block)
    logits = (
        jnp.einsum("cphm,npm->phcn", query_rows, all_keys, preferred_element_type=jnp.float32)
        * score_scale
    )
    masked = jnp.where(visible, logits, -jnp.inf)
    top = jnp.max(masked, axis=-1)
    exps = jnp.exp(masked - top[..., None])
    total = jnp.sum(exps, axis=-1)
    summed = jnp.einsum(
        "qyjl,lqu->qyju", exps.astype(jnp.bfloat16), all_values, preferred_element_type=jnp.float32
    )
    carried_over_state = (top, total, summed)
    final_output = carried_over_state[2] / carried_over_state[1][..., None]
    soft_out = (
        final_output.transpose(2, 0, 1, 3)
        .reshape(row_count, heads_here, head_width)
        .astype(jnp.bfloat16)
    )
    return (lin_out, soft_out)


def solution(mesh):
    placed = (
        P("seq", "head", None),
        P("seq", "head", None),
        P("seq", "head", None),
        P("head", "seq"),
        P("head", None),
        P("seq", "head", None),
        P("seq", "head", None),
        P("seq", "head", None),
        P("seq"),
    )
    return jax.shard_map(
        body,
        mesh=mesh,
        in_specs=placed,
        out_specs=(P("seq", "head", None), P("seq", "head", None)),
        check_vma=False,
    )
```

```python
import functools

import jax
import jax.numpy as jnp
from jax import lax
from jax.experimental import pallas as pl
from jax.experimental.pallas import tpu as pltpu
from jax.sharding import PartitionSpec as P

MESH = pl.DeviceIdType.MESH

DH = 128
HEADS = 64
REACH = 3


def scan_kernel(
    rounds,
    chunks,
    reach,
    fall_ref,
    state_ref,
    sent0_ref,
    kv_ref,
    q_ref,
    bias_ref,
    out_ref,
    soft_ref,
    whole,
    whole_fall,
    out_fall,
    suffix,
    suffix_fall,
    got,
    got_fall,
    outgoing,
    outgoing_fall,
    send_sem,
    recv_sem,
    fsend_sem,
    frecv_sem,
    kv_got,
    kv_send,
    kv_recv,
):
    me = lax.axis_index("seq")
    head = lax.axis_index("head")
    length = 2**rounds
    width = state_ref.shape[0] // chunks
    jump = 7
    back0, back1, near = rounds, rounds + 1, rounds + 2

    def ahead(dist):
        return 1 - (me + dist) // length

    def behind(dist):
        return (me - dist + length) // length

    far_recv = behind(jump)
    near_recv = behind(4) * (1 - far_recv)
    near_send = 1 - (me + length - 3) // length

    barrier = pltpu.get_barrier_semaphore()
    partners = 0
    distances = [2**k for k in range(rounds)] + list(range(1, reach + 1)) + [jump]
    for dist in sorted(set(distances)):
        partners = partners + ahead(dist) + behind(dist)

        @pl.when(ahead(dist) == 1)
        def _():
            pl.semaphore_signal(barrier, inc=1, device_id=(me + dist, head), device_id_type=MESH)

        @pl.when(behind(dist) == 1)
        def _():
            pl.semaphore_signal(barrier, inc=1, device_id=(me - dist, head), device_id_type=MESH)

    pl.semaphore_wait(barrier, partners)

    def kv_copy(dist, device):
        return pltpu.make_async_remote_copy(
            src_ref=kv_ref,
            dst_ref=kv_got.at[dist - 1],
            send_sem=kv_send.at[dist - 1],
            recv_sem=kv_recv.at[dist - 1],
            device_id=(device, head),
            device_id_type=MESH,
        )

    for dist in range(1, reach + 1):

        @pl.when(ahead(dist) == 1)
        def _():
            kv_copy(dist, me + dist).start()

    def state_copy(stage, source, c, device):
        rows = pl.ds(c * width, width)
        return pltpu.make_async_remote_copy(
            src_ref=source.at[rows],
            dst_ref=got.at[stage, rows],
            send_sem=send_sem.at[stage, c],
            recv_sem=recv_sem.at[stage, c],
            device_id=(device, head),
            device_id_type=MESH,
        )

    def fall_copy(stage, source, device):
        return pltpu.make_async_remote_copy(
            src_ref=source,
            dst_ref=got_fall.at[stage],
            send_sem=fsend_sem.at[stage],
            recv_sem=frecv_sem.at[stage],
            device_id=(device, head),
            device_id_type=MESH,
        )

    outgoing_fall[0] = fall_ref[...]

    @pl.when(ahead(1) == 1)
    def _():
        fall_copy(0, outgoing_fall.at[0], me + 1).start()
        for c in range(chunks):
            state_copy(0, sent0_ref, c, me + 1).start()

    @pl.when(behind(1) == 1)
    def _():
        fall_copy(back0, outgoing_fall.at[0], me - 1).start()
        for c in range(chunks):
            state_copy(back0, sent0_ref, c, me - 1).start()

    whole[...] = state_ref[...]
    whole_fall[...] = fall_ref[...]
    suffix[...] = state_ref[...]
    suffix_fall[...] = fall_ref[...]
    out_ref[...] = jnp.zeros_like(out_ref)
    out_fall[...] = jnp.ones_like(out_fall)

    def forward_fall(stage, shift):
        @pl.when(behind(shift) == 1)
        def _():
            fall_copy(stage, outgoing_fall.at[stage], me - shift).wait_recv()
            arrived = got_fall[stage]
            out_fall[...] = arrived * out_fall[...]
            whole_fall[...] = arrived * whole_fall[...]

    def forward_chunk(stage, shift, c, update_whole=True):
        rows = pl.ds(c * width, width)

        @pl.when(behind(shift) == 1)
        def _():
            state_copy(stage, outgoing.at[stage], c, me - shift).wait_recv()
            arrived = got[stage, rows].astype(jnp.float32)
            out_ref[rows] = out_fall[rows][:, None, :] * arrived + out_ref[rows]
            if update_whole:
                whole[rows] = whole_fall[rows][:, None, :] * arrived + whole[rows]

    def backward_fall(stage, shift):
        @pl.when(ahead(shift) == 1)
        def _():
            fall_copy(stage, outgoing_fall.at[stage], me + shift).wait_recv()
            suffix_fall[...] = suffix_fall[...] * got_fall[stage]

    def backward_chunk(stage, shift, c):
        rows = pl.ds(c * width, width)

        @pl.when(ahead(shift) == 1)
        def _():
            state_copy(stage, outgoing.at[stage], c, me + shift).wait_recv()
            arrived = got[stage, rows].astype(jnp.float32)
            suffix[rows] = got_fall[stage][rows][:, None, :] * suffix[rows] + arrived

    def send_chunk(stage, flag, buffer, dist, c):
        rows = pl.ds(c * width, width)

        @pl.when(flag == 1)
        def _():
            outgoing[stage, rows] = buffer[rows].astype(jnp.bfloat16)
            state_copy(stage, outgoing.at[stage], c, me + dist).start()

    def send_fall(stage, flag, buffer_fall, dist):
        @pl.when(flag == 1)
        def _():
            outgoing_fall[stage] = buffer_fall[...]
            fall_copy(stage, outgoing_fall.at[stage], me + dist).start()

    backward_fall(back0, 1)
    send_fall(back1, behind(2), suffix_fall, -2)
    for c in range(chunks):
        forward_chunk(0, 1, c)
        send_chunk(1, ahead(2), whole, 2, c)
        backward_chunk(back0, 1, c)
        send_chunk(back1, behind(2), suffix, -2, c)
    forward_fall(0, 1)
    send_fall(1, ahead(2), whole_fall, 2)

    backward_fall(back1, 2)
    send_fall(2, ahead(jump), suffix_fall, jump)
    for c in range(chunks):
        forward_chunk(1, 2, c)
        send_chunk(near, near_send, whole, 4, c)
        backward_chunk(back1, 2, c)
        send_chunk(2, ahead(jump), suffix, jump, c)
    forward_fall(1, 2)
    send_fall(near, near_send, whole_fall, 4)

    for c in range(chunks):
        rows = pl.ds(c * width, width)
        for flag, dist, stage in ((far_recv, jump, 2), (near_recv, 4, near)):

            @pl.when(flag == 1)
            def _():
                state_copy(stage, outgoing.at[stage], c, me - dist).wait_recv()
                arrived = got[stage, rows].astype(jnp.float32)
                out_ref[rows] = out_fall[rows][:, None, :] * arrived + out_ref[rows]
                whole[rows] = whole_fall[rows][:, None, :] * arrived + whole[rows]

        if rounds > 3:
            send_chunk(3, ahead(8), whole, 8, c)

    for flag, dist, stage in ((far_recv, jump, 2), (near_recv, 4, near)):

        @pl.when(flag == 1)
        def _():
            fall_copy(stage, outgoing_fall.at[stage], me - dist).wait_recv()
            arrived = got_fall[stage]
            out_fall[...] = arrived * out_fall[...]
            whole_fall[...] = arrived * whole_fall[...]

    if rounds > 3:
        send_fall(3, ahead(8), whole_fall, 8)

    def attention():
        for dist in range(1, reach + 1):

            @pl.when(behind(dist) == 1)
            def _():
                kv_copy(dist, me - dist).wait_recv()

            @pl.when(behind(dist) == 0)
            def _():
                kv_got[dist - 1] = jnp.zeros_like(kv_got.at[dist - 1])

            @pl.when(ahead(dist) == 1)
            def _():
                kv_copy(dist, me + dist).wait_send()

        tokens, groups, group = q_ref.shape[0], q_ref.shape[1], q_ref.shape[2]
        scale = float(q_ref.shape[3]) ** (-0.5)
        for g in range(groups):
            q = q_ref[:, g].astype(jnp.float32).reshape(tokens * group, -1).astype(jnp.bfloat16)
            keys = [kv_got[slot, 0, g] for slot in range(reach - 1, -1, -1)] + [kv_ref[0, g]]
            values = [kv_got[slot, 1, g] for slot in range(reach - 1, -1, -1)] + [kv_ref[1, g]]
            logits = jnp.concatenate(
                [
                    lax.dot_general(q, k, (((1,), (1,)), ((), ())), preferred_element_type=jnp.float32)
                    for k in keys
                ],
                axis=1,
            )
            masked = (logits * scale).reshape(tokens, group, -1) + bias_ref[...][:, None, :]
            top = jnp.max(masked, axis=-1, keepdims=True)
            exps = jnp.exp(masked - top)
            total = jnp.sum(exps, axis=-1, keepdims=True)
            probs = exps.reshape(tokens * group, -1).astype(jnp.bfloat16)
            summed = jnp.dot(probs, jnp.concatenate(values, axis=0), preferred_element_type=jnp.float32)
            soft_ref[:, g] = (summed.reshape(tokens, group, -1) / total).astype(soft_ref.dtype)

    for k in range(3, rounds):
        shift, last = 2**k, k == rounds - 1
        if last:
            attention()
        for c in range(chunks):
            forward_chunk(k, shift, c, update_whole=not last)
            if not last:
                rows = pl.ds(c * width, width)

                @pl.when(ahead(2 * shift) == 1)
                def _():
                    outgoing[k + 1, rows] = whole[rows].astype(jnp.bfloat16)
                    state_copy(k + 1, outgoing.at[k + 1], c, me + 2 * shift).start()

        @pl.when(behind(shift) == 1)
        def _():
            fall_copy(k, outgoing_fall.at[k], me - shift).wait_recv()
            arrived = got_fall[k]
            out_fall[...] = arrived * out_fall[...]
            if not last:
                whole_fall[...] = arrived * whole_fall[...]

        if not last:

            @pl.when(ahead(2 * shift) == 1)
            def _():
                outgoing_fall[k + 1] = whole_fall[...]
                fall_copy(k + 1, outgoing_fall.at[k + 1], me + 2 * shift).start()

    sends = [(0, 1, ahead(1)), (back0, -1, behind(1)), (1, 2, ahead(2)), (back1, -2, behind(2))]
    sends += [(2, jump, ahead(jump)), (near, 4, near_send)]
    sends += [(k, 2**k, ahead(2**k)) for k in range(3, rounds)]
    for stage, dist, flag in sends:

        @pl.when(flag == 1)
        def _():
            fall_copy(stage, outgoing_fall.at[stage], me + dist).wait_send()
            for c in range(chunks):
                state_copy(stage, outgoing.at[stage], c, me + dist).wait_send()


def exclusive_scan(falling, state, kv, queries, bias, axis):
    length = lax.axis_size(axis)
    rounds = length.bit_length() - 1
    stages = rounds + 3
    chunks = 8
    heads, rows, columns = state.shape
    fall_rows = jnp.broadcast_to(falling[:, None], (heads, columns))
    vmem = pl.BlockSpec(memory_space=pltpu.VMEM)
    return pl.pallas_call(
        functools.partial(scan_kernel, rounds, chunks, REACH),
        out_shape=(
            jax.ShapeDtypeStruct(state.shape, jnp.float32),
            jax.ShapeDtypeStruct(queries.shape, queries.dtype),
        ),
        in_specs=[vmem] * 6,
        out_specs=(vmem, vmem),
        scratch_shapes=[
            pltpu.VMEM(state.shape, jnp.float32),
            pltpu.VMEM((heads, columns), jnp.float32),
            pltpu.VMEM((heads, columns), jnp.float32),
            pltpu.VMEM(state.shape, jnp.float32),
            pltpu.VMEM((heads, columns), jnp.float32),
            pltpu.VMEM((stages,) + state.shape, jnp.bfloat16),
            pltpu.VMEM((stages, heads, columns), jnp.float32),
            pltpu.VMEM((stages,) + state.shape, jnp.bfloat16),
            pltpu.VMEM((stages, heads, columns), jnp.float32),
            pltpu.SemaphoreType.DMA((stages, chunks)),
            pltpu.SemaphoreType.DMA((stages, chunks)),
            pltpu.SemaphoreType.DMA((stages,)),
            pltpu.SemaphoreType.DMA((stages,)),
            pltpu.VMEM((REACH,) + kv.shape, kv.dtype),
            pltpu.SemaphoreType.DMA((REACH,)),
            pltpu.SemaphoreType.DMA((REACH,)),
        ],
        compiler_params=pltpu.CompilerParams(collective_id=0, has_side_effects=True),
    )(fall_rows, state, state.astype(jnp.bfloat16), kv, queries, bias)


def head_sum_kernel(count, value_ref, out_ref, slots, send_sem, recv_sem):
    me = lax.axis_index("seq")
    head = lax.axis_index("head")
    barrier = pltpu.get_barrier_semaphore()
    for other in range(count):

        @pl.when(other != head)
        def _():
            pl.semaphore_signal(barrier, inc=1, device_id=(me, other), device_id_type=MESH)

    pl.semaphore_wait(barrier, count - 1)
    slots[head] = value_ref[...]

    def copy(other, slot):
        return pltpu.make_async_remote_copy(
            src_ref=value_ref,
            dst_ref=slots.at[slot],
            send_sem=send_sem.at[other],
            recv_sem=recv_sem.at[slot],
            device_id=(me, other),
            device_id_type=MESH,
        )

    for other in range(count):

        @pl.when(other != head)
        def _():
            copy(other, head).start()

    for other in range(count):

        @pl.when(other != head)
        def _():
            copy(other, other).wait_recv()
            copy(other, head).wait_send()

    total = slots[0]
    for other in range(1, count):
        total = total + slots[other]
    out_ref[...] = total


def head_sum(value, axis):
    count = lax.axis_size(axis)
    vmem = pl.BlockSpec(memory_space=pltpu.VMEM)
    row = value.reshape(1, -1)
    return pl.pallas_call(
        functools.partial(head_sum_kernel, count),
        out_shape=jax.ShapeDtypeStruct(row.shape, row.dtype),
        in_specs=[vmem],
        out_specs=vmem,
        scratch_shapes=[
            pltpu.VMEM((count,) + row.shape, row.dtype),
            pltpu.SemaphoreType.DMA((count,)),
            pltpu.SemaphoreType.DMA((count,)),
        ],
        compiler_params=pltpu.CompilerParams(collective_id=1, has_side_effects=True),
    )(row).reshape(value.shape)


def from_behind(value, axis, steps):
    count = lax.axis_size(axis)
    first, last = (max(0, -steps), min(count, count - steps))
    return lax.ppermute(value, axis, [(source, source + steps) for source in range(first, last)])


def combine_states(earlier, later):
    return (earlier[0] * later[0], later[0][:, None, None] * earlier[1] + later[1])


def split_parts(matrix):
    upper = matrix.astype(jnp.bfloat16)
    lower = (matrix - upper.astype(jnp.float32)).astype(jnp.bfloat16)
    return (upper, lower)


def attend(carried_over_state, query_rows, key_rows, value_rows, visible, score_scale):
    running_max, running_sum, accumulated = carried_over_state
    attention_logits = (
        jnp.einsum("cphm,npm->phcn", query_rows, key_rows, preferred_element_type=jnp.float32)
        * score_scale
    )
    masked = jnp.where(visible, attention_logits, -jnp.inf)
    new_max = jnp.maximum(running_max, jnp.max(masked, axis=-1))
    power_exponent = jnp.exp(masked - new_max[..., None])
    fading = jnp.exp(running_max - new_max)
    new_sum = running_sum * fading + jnp.sum(power_exponent, axis=-1)
    product = jnp.einsum(
        "qyjl,lqu->qyju",
        power_exponent.astype(jnp.bfloat16),
        value_rows,
        preferred_element_type=jnp.float32,
    )
    return (new_max, new_sum, accumulated * fading[..., None] + product)


def body(
    linear_query_rows,
    lin_keys,
    linear_value_rows,
    log_decay,
    norm_gain,
    soft_queries,
    soft_keys,
    soft_values,
    window_start,
):
    row_count, heads_here, head_width = linear_query_rows.shape
    cumulated = jnp.cumsum(log_decay, axis=1)
    token_locations = jnp.arange(row_count, dtype=jnp.int32)
    lower_mask = token_locations[:, None] >= token_locations[None, :]
    tail = jnp.exp(cumulated[:, -1:] - cumulated)
    key_product = lin_keys.astype(jnp.float32) * tail.T[:, :, None]
    key_product_upper, key_product_lower = split_parts(key_product)
    recurrent_state = jnp.einsum(
        "egz,egc->gzc", key_product_upper, linear_value_rows, preferred_element_type=jnp.float32
    )
    recurrent_state = recurrent_state + jnp.einsum(
        "egz,egc->gzc", key_product_lower, linear_value_rows, preferred_element_type=jnp.float32
    )
    falling = jnp.exp(cumulated[:, -1])
    kv_here = soft_keys.shape[1]
    group = heads_here // kv_here
    block_index = lax.axis_index("seq")
    key_index = jnp.arange((REACH + 1) * row_count, dtype=jnp.int32)
    key_block = block_index - REACH + key_index // row_count
    causal = (key_index % row_count)[None, :] <= token_locations[:, None]
    visible = ((key_block[None, :] < block_index) | causal) & (key_block[None, :] >= window_start[0])
    preceding_state, soft_out = exclusive_scan(
        falling,
        recurrent_state,
        jnp.stack([soft_keys, soft_values]).transpose(0, 2, 1, 3),
        soft_queries.reshape(row_count, kv_here, group, head_width),
        jnp.where(visible, 0.0, -jnp.inf).astype(jnp.float32),
        "seq",
    )
    lin_scores = jnp.einsum(
        "thd,shd->hts", linear_query_rows, lin_keys, preferred_element_type=jnp.float32
    )
    gap = jnp.where(lower_mask[None], cumulated[:, :, None] - cumulated[:, None, :], -jnp.inf)
    lin_weights = (lin_scores * jnp.exp(gap)).astype(jnp.bfloat16)
    local_part = jnp.einsum(
        "hts,shd->thd", lin_weights, linear_value_rows, preferred_element_type=jnp.float32
    )
    preceding_upper, preceding_lower = split_parts(preceding_state)
    carried_part = jnp.einsum(
        "nwg,wgq->nwq", linear_query_rows, preceding_upper, preferred_element_type=jnp.float32
    )
    carried_part = carried_part + jnp.einsum(
        "nwg,wgq->nwq", linear_query_rows, preceding_lower, preferred_element_type=jnp.float32
    )
    mixed = local_part + jnp.exp(cumulated).T[:, :, None] * carried_part
    squares = head_sum(jnp.sum(mixed * mixed, axis=(1, 2)), "head")
    lin_out = (
        mixed
        * lax.rsqrt(squares / (HEADS * DH) + 1e-06)[:, None, None]
        * norm_gain.astype(jnp.float32)
    ).astype(jnp.bfloat16)
    soft_out = soft_out.reshape(row_count, heads_here, head_width)
    return (lin_out, soft_out)


def solution(mesh):
    placed = (
        P("seq", "head", None),
        P("seq", "head", None),
        P("seq", "head", None),
        P("head", "seq"),
        P("head", None),
        P("seq", "head", None),
        P("seq", "head", None),
        P("seq", "head", None),
        P("seq"),
    )
    return jax.shard_map(
        body,
        mesh=mesh,
        in_specs=placed,
        out_specs=(P("seq", "head", None), P("seq", "head", None)),
        check_vma=False,
    )
```

```python
import functools

import jax
import jax.numpy as jnp
from jax import lax
from jax.experimental import pallas as pl
from jax.experimental.pallas import tpu as pltpu
from jax.sharding import PartitionSpec as P

MESH = pl.DeviceIdType.MESH

DH = 128
HEADS = 64
REACH = 3


def scan_kernel(
    rounds,
    chunks,
    reach,
    fall_ref,
    state_ref,
    sent0_ref,
    kv_ref,
    q_ref,
    bias_ref,
    lq_ref,
    local_ref,
    grow_ref,
    gain_ref,
    out_ref,
    soft_ref,
    lin_ref,
    whole,
    whole_fall,
    out_fall,
    suffix,
    suffix_fall,
    got,
    got_fall,
    outgoing,
    outgoing_fall,
    send_sem,
    recv_sem,
    fsend_sem,
    frecv_sem,
    kv_got,
    kv_send,
    kv_recv,
    head_slots,
    head_send,
    head_recv,
):
    me = lax.axis_index("seq")
    head = lax.axis_index("head")
    length = 2**rounds
    width = state_ref.shape[0] // chunks
    jump = 7
    back0, back1, near = rounds, rounds + 1, rounds + 2

    def ahead(dist):
        return 1 - (me + dist) // length

    def behind(dist):
        return (me - dist + length) // length

    far_recv = behind(jump)
    near_recv = behind(4) * (1 - far_recv)
    near_send = 1 - (me + length - 3) // length

    barrier = pltpu.get_barrier_semaphore()
    partners = 0
    distances = [2**k for k in range(rounds)] + list(range(1, reach + 1)) + [jump]
    for dist in sorted(set(distances)):
        partners = partners + ahead(dist) + behind(dist)

        @pl.when(ahead(dist) == 1)
        def _():
            pl.semaphore_signal(barrier, inc=1, device_id=(me + dist, head), device_id_type=MESH)

        @pl.when(behind(dist) == 1)
        def _():
            pl.semaphore_signal(barrier, inc=1, device_id=(me - dist, head), device_id_type=MESH)

    head_count = head_slots.shape[0]
    for other in range(head_count):

        @pl.when(other != head)
        def _():
            pl.semaphore_signal(barrier, inc=1, device_id=(me, other), device_id_type=MESH)

    pl.semaphore_wait(barrier, partners + head_count - 1)

    def kv_copy(dist, device):
        return pltpu.make_async_remote_copy(
            src_ref=kv_ref,
            dst_ref=kv_got.at[dist - 1],
            send_sem=kv_send.at[dist - 1],
            recv_sem=kv_recv.at[dist - 1],
            device_id=(device, head),
            device_id_type=MESH,
        )

    for dist in range(1, reach + 1):

        @pl.when(ahead(dist) == 1)
        def _():
            kv_copy(dist, me + dist).start()

    def state_copy(stage, source, c, device):
        rows = pl.ds(c * width, width)
        return pltpu.make_async_remote_copy(
            src_ref=source.at[rows],
            dst_ref=got.at[stage, rows],
            send_sem=send_sem.at[stage, c],
            recv_sem=recv_sem.at[stage, c],
            device_id=(device, head),
            device_id_type=MESH,
        )

    def fall_copy(stage, source, device):
        return pltpu.make_async_remote_copy(
            src_ref=source,
            dst_ref=got_fall.at[stage],
            send_sem=fsend_sem.at[stage],
            recv_sem=frecv_sem.at[stage],
            device_id=(device, head),
            device_id_type=MESH,
        )

    outgoing_fall[0] = fall_ref[...]

    @pl.when(ahead(1) == 1)
    def _():
        fall_copy(0, outgoing_fall.at[0], me + 1).start()
        for c in range(chunks):
            state_copy(0, sent0_ref, c, me + 1).start()

    @pl.when(behind(1) == 1)
    def _():
        fall_copy(back0, outgoing_fall.at[0], me - 1).start()
        for c in range(chunks):
            state_copy(back0, sent0_ref, c, me - 1).start()

    whole[...] = state_ref[...]
    whole_fall[...] = fall_ref[...]
    suffix[...] = state_ref[...]
    suffix_fall[...] = fall_ref[...]
    out_ref[...] = jnp.zeros_like(out_ref)
    out_fall[...] = jnp.ones_like(out_fall)

    def forward_fall(stage, shift):
        @pl.when(behind(shift) == 1)
        def _():
            fall_copy(stage, outgoing_fall.at[stage], me - shift).wait_recv()
            arrived = got_fall[stage]
            out_fall[...] = arrived * out_fall[...]
            whole_fall[...] = arrived * whole_fall[...]

    def forward_chunk(stage, shift, c, update_whole=True):
        rows = pl.ds(c * width, width)

        @pl.when(behind(shift) == 1)
        def _():
            state_copy(stage, outgoing.at[stage], c, me - shift).wait_recv()
            arrived = got[stage, rows].astype(jnp.float32)
            out_ref[rows] = out_fall[rows][:, None, :] * arrived + out_ref[rows]
            if update_whole:
                whole[rows] = whole_fall[rows][:, None, :] * arrived + whole[rows]

    def backward_fall(stage, shift):
        @pl.when(ahead(shift) == 1)
        def _():
            fall_copy(stage, outgoing_fall.at[stage], me + shift).wait_recv()
            suffix_fall[...] = suffix_fall[...] * got_fall[stage]

    def backward_chunk(stage, shift, c):
        rows = pl.ds(c * width, width)

        @pl.when(ahead(shift) == 1)
        def _():
            state_copy(stage, outgoing.at[stage], c, me + shift).wait_recv()
            arrived = got[stage, rows].astype(jnp.float32)
            suffix[rows] = got_fall[stage][rows][:, None, :] * suffix[rows] + arrived

    def send_chunk(stage, flag, buffer, dist, c):
        rows = pl.ds(c * width, width)

        @pl.when(flag == 1)
        def _():
            outgoing[stage, rows] = buffer[rows].astype(jnp.bfloat16)
            state_copy(stage, outgoing.at[stage], c, me + dist).start()

    def send_fall(stage, flag, buffer_fall, dist):
        @pl.when(flag == 1)
        def _():
            outgoing_fall[stage] = buffer_fall[...]
            fall_copy(stage, outgoing_fall.at[stage], me + dist).start()

    backward_fall(back0, 1)
    send_fall(back1, behind(2), suffix_fall, -2)
    for c in range(chunks):
        forward_chunk(0, 1, c)
        send_chunk(1, ahead(2), whole, 2, c)
        backward_chunk(back0, 1, c)
        send_chunk(back1, behind(2), suffix, -2, c)
    forward_fall(0, 1)
    send_fall(1, ahead(2), whole_fall, 2)

    backward_fall(back1, 2)
    send_fall(2, ahead(jump), suffix_fall, jump)
    for c in range(chunks):
        forward_chunk(1, 2, c)
        send_chunk(near, near_send, whole, 4, c)
        backward_chunk(back1, 2, c)
        send_chunk(2, ahead(jump), suffix, jump, c)
    forward_fall(1, 2)
    send_fall(near, near_send, whole_fall, 4)

    for c in range(chunks):
        rows = pl.ds(c * width, width)
        for flag, dist, stage in ((far_recv, jump, 2), (near_recv, 4, near)):

            @pl.when(flag == 1)
            def _():
                state_copy(stage, outgoing.at[stage], c, me - dist).wait_recv()
                arrived = got[stage, rows].astype(jnp.float32)
                out_ref[rows] = out_fall[rows][:, None, :] * arrived + out_ref[rows]
                whole[rows] = whole_fall[rows][:, None, :] * arrived + whole[rows]

        if rounds > 3:
            send_chunk(3, ahead(8), whole, 8, c)

    for flag, dist, stage in ((far_recv, jump, 2), (near_recv, 4, near)):

        @pl.when(flag == 1)
        def _():
            fall_copy(stage, outgoing_fall.at[stage], me - dist).wait_recv()
            arrived = got_fall[stage]
            out_fall[...] = arrived * out_fall[...]
            whole_fall[...] = arrived * whole_fall[...]

    if rounds > 3:
        send_fall(3, ahead(8), whole_fall, 8)

    def attention():
        for dist in range(1, reach + 1):

            @pl.when(behind(dist) == 1)
            def _():
                kv_copy(dist, me - dist).wait_recv()

            @pl.when(behind(dist) == 0)
            def _():
                kv_got[dist - 1] = jnp.zeros_like(kv_got.at[dist - 1])

            @pl.when(ahead(dist) == 1)
            def _():
                kv_copy(dist, me + dist).wait_send()

        tokens, groups, group = q_ref.shape[0], q_ref.shape[1], q_ref.shape[2]
        scale = float(q_ref.shape[3]) ** (-0.5)
        for g in range(groups):
            q = q_ref[:, g].astype(jnp.float32).reshape(tokens * group, -1).astype(jnp.bfloat16)
            keys = [kv_got[slot, 0, g] for slot in range(reach - 1, -1, -1)] + [kv_ref[0, g]]
            values = [kv_got[slot, 1, g] for slot in range(reach - 1, -1, -1)] + [kv_ref[1, g]]
            logits = jnp.concatenate(
                [
                    lax.dot_general(q, k, (((1,), (1,)), ((), ())), preferred_element_type=jnp.float32)
                    for k in keys
                ],
                axis=1,
            )
            masked = (logits * scale).reshape(tokens, group, -1) + bias_ref[...][:, None, :]
            top = jnp.max(masked, axis=-1, keepdims=True)
            exps = jnp.exp(masked - top)
            total = jnp.sum(exps, axis=-1, keepdims=True)
            probs = exps.reshape(tokens * group, -1).astype(jnp.bfloat16)
            summed = jnp.dot(probs, jnp.concatenate(values, axis=0), preferred_element_type=jnp.float32)
            soft_ref[:, g] = (summed.reshape(tokens, group, -1) / total).astype(soft_ref.dtype)

    for k in range(3, rounds):
        shift, last = 2**k, k == rounds - 1
        if last:
            attention()
        for c in range(chunks):
            forward_chunk(k, shift, c, update_whole=not last)
            if not last:
                rows = pl.ds(c * width, width)

                @pl.when(ahead(2 * shift) == 1)
                def _():
                    outgoing[k + 1, rows] = whole[rows].astype(jnp.bfloat16)
                    state_copy(k + 1, outgoing.at[k + 1], c, me + 2 * shift).start()

        @pl.when(behind(shift) == 1)
        def _():
            fall_copy(k, outgoing_fall.at[k], me - shift).wait_recv()
            arrived = got_fall[k]
            out_fall[...] = arrived * out_fall[...]
            if not last:
                whole_fall[...] = arrived * whole_fall[...]

        if not last:

            @pl.when(ahead(2 * shift) == 1)
            def _():
                outgoing_fall[k + 1] = whole_fall[...]
                fall_copy(k + 1, outgoing_fall.at[k + 1], me + 2 * shift).start()

    sends = [(0, 1, ahead(1)), (back0, -1, behind(1)), (1, 2, ahead(2)), (back1, -2, behind(2))]
    sends += [(2, jump, ahead(jump)), (near, 4, near_send)]
    sends += [(k, 2**k, ahead(2**k)) for k in range(3, rounds)]
    for stage, dist, flag in sends:

        @pl.when(flag == 1)
        def _():
            fall_copy(stage, outgoing_fall.at[stage], me + dist).wait_send()
            for c in range(chunks):
                state_copy(stage, outgoing.at[stage], c, me + dist).wait_send()

    prior = out_ref[...]
    upper = prior.astype(jnp.bfloat16)
    lower = (prior - upper.astype(jnp.float32)).astype(jnp.bfloat16)
    queries = lq_ref[...]
    carried = jnp.einsum("hti,hij->htj", queries, upper, preferred_element_type=jnp.float32)
    carried = carried + jnp.einsum("hti,hij->htj", queries, lower, preferred_element_type=jnp.float32)
    mixed = local_ref[...] + grow_ref[...] * carried
    column = jnp.sum(jnp.sum(mixed * mixed, axis=0), axis=1, keepdims=True)
    head_slots[head] = jnp.transpose(jnp.broadcast_to(column, (column.shape[0], 128)))[0:1, :]

    def head_copy(other, slot):
        return pltpu.make_async_remote_copy(
            src_ref=head_slots.at[head],
            dst_ref=head_slots.at[slot],
            send_sem=head_send.at[other],
            recv_sem=head_recv.at[slot],
            device_id=(me, other),
            device_id_type=MESH,
        )

    for other in range(head_count):

        @pl.when(other != head)
        def _():
            head_copy(other, head).start()

    for other in range(head_count):

        @pl.when(other != head)
        def _():
            head_copy(other, other).wait_recv()
            head_copy(other, head).wait_send()

    total = head_slots[0]
    for other in range(1, head_count):
        total = total + head_slots[other]
    heads_all, width_all = lq_ref.shape[0] * head_count, lq_ref.shape[2]
    scale_row = lax.rsqrt(total / (heads_all * width_all) + 1e-06)
    scale = jnp.transpose(jnp.broadcast_to(scale_row, (128, scale_row.shape[1])))[:, 0:1]
    lin_ref[...] = (mixed * scale[None] * gain_ref[...][:, None, :]).astype(lin_ref.dtype)


def exclusive_scan(falling, state, kv, queries, bias, lq, local, grow, gain, axis):
    length = lax.axis_size(axis)
    rounds = length.bit_length() - 1
    stages = rounds + 3
    chunks = 8
    heads, rows, columns = state.shape
    fall_rows = jnp.broadcast_to(falling[:, None], (heads, columns))
    vmem = pl.BlockSpec(memory_space=pltpu.VMEM)
    return pl.pallas_call(
        functools.partial(scan_kernel, rounds, chunks, REACH),
        out_shape=(
            jax.ShapeDtypeStruct(state.shape, jnp.float32),
            jax.ShapeDtypeStruct(queries.shape, queries.dtype),
            jax.ShapeDtypeStruct(lq.shape, jnp.bfloat16),
        ),
        in_specs=[vmem] * 10,
        out_specs=(vmem, vmem, vmem),
        scratch_shapes=[
            pltpu.VMEM(state.shape, jnp.float32),
            pltpu.VMEM((heads, columns), jnp.float32),
            pltpu.VMEM((heads, columns), jnp.float32),
            pltpu.VMEM(state.shape, jnp.float32),
            pltpu.VMEM((heads, columns), jnp.float32),
            pltpu.VMEM((stages,) + state.shape, jnp.bfloat16),
            pltpu.VMEM((stages, heads, columns), jnp.float32),
            pltpu.VMEM((stages,) + state.shape, jnp.bfloat16),
            pltpu.VMEM((stages, heads, columns), jnp.float32),
            pltpu.SemaphoreType.DMA((stages, chunks)),
            pltpu.SemaphoreType.DMA((stages, chunks)),
            pltpu.SemaphoreType.DMA((stages,)),
            pltpu.SemaphoreType.DMA((stages,)),
            pltpu.VMEM((REACH,) + kv.shape, kv.dtype),
            pltpu.SemaphoreType.DMA((REACH,)),
            pltpu.SemaphoreType.DMA((REACH,)),
            pltpu.VMEM((lax.axis_size("head"), 1, columns), jnp.float32),
            pltpu.SemaphoreType.DMA((lax.axis_size("head"),)),
            pltpu.SemaphoreType.DMA((lax.axis_size("head"),)),
        ],
        compiler_params=pltpu.CompilerParams(collective_id=0, has_side_effects=True),
    )(fall_rows, state, state.astype(jnp.bfloat16), kv, queries, bias, lq, local, grow, gain)


def head_sum_kernel(count, value_ref, out_ref, slots, send_sem, recv_sem):
    me = lax.axis_index("seq")
    head = lax.axis_index("head")
    barrier = pltpu.get_barrier_semaphore()
    for other in range(count):

        @pl.when(other != head)
        def _():
            pl.semaphore_signal(barrier, inc=1, device_id=(me, other), device_id_type=MESH)

    pl.semaphore_wait(barrier, count - 1)
    slots[head] = value_ref[...]

    def copy(other, slot):
        return pltpu.make_async_remote_copy(
            src_ref=value_ref,
            dst_ref=slots.at[slot],
            send_sem=send_sem.at[other],
            recv_sem=recv_sem.at[slot],
            device_id=(me, other),
            device_id_type=MESH,
        )

    for other in range(count):

        @pl.when(other != head)
        def _():
            copy(other, head).start()

    for other in range(count):

        @pl.when(other != head)
        def _():
            copy(other, other).wait_recv()
            copy(other, head).wait_send()

    total = slots[0]
    for other in range(1, count):
        total = total + slots[other]
    out_ref[...] = total


def head_sum(value, axis):
    count = lax.axis_size(axis)
    vmem = pl.BlockSpec(memory_space=pltpu.VMEM)
    row = value.reshape(1, -1)
    return pl.pallas_call(
        functools.partial(head_sum_kernel, count),
        out_shape=jax.ShapeDtypeStruct(row.shape, row.dtype),
        in_specs=[vmem],
        out_specs=vmem,
        scratch_shapes=[
            pltpu.VMEM((count,) + row.shape, row.dtype),
            pltpu.SemaphoreType.DMA((count,)),
            pltpu.SemaphoreType.DMA((count,)),
        ],
        compiler_params=pltpu.CompilerParams(collective_id=1, has_side_effects=True),
    )(row).reshape(value.shape)


def from_behind(value, axis, steps):
    count = lax.axis_size(axis)
    first, last = (max(0, -steps), min(count, count - steps))
    return lax.ppermute(value, axis, [(source, source + steps) for source in range(first, last)])


def combine_states(earlier, later):
    return (earlier[0] * later[0], later[0][:, None, None] * earlier[1] + later[1])


def split_parts(matrix):
    upper = matrix.astype(jnp.bfloat16)
    lower = (matrix - upper.astype(jnp.float32)).astype(jnp.bfloat16)
    return (upper, lower)


def attend(carried_over_state, query_rows, key_rows, value_rows, visible, score_scale):
    running_max, running_sum, accumulated = carried_over_state
    attention_logits = (
        jnp.einsum("cphm,npm->phcn", query_rows, key_rows, preferred_element_type=jnp.float32)
        * score_scale
    )
    masked = jnp.where(visible, attention_logits, -jnp.inf)
    new_max = jnp.maximum(running_max, jnp.max(masked, axis=-1))
    power_exponent = jnp.exp(masked - new_max[..., None])
    fading = jnp.exp(running_max - new_max)
    new_sum = running_sum * fading + jnp.sum(power_exponent, axis=-1)
    product = jnp.einsum(
        "qyjl,lqu->qyju",
        power_exponent.astype(jnp.bfloat16),
        value_rows,
        preferred_element_type=jnp.float32,
    )
    return (new_max, new_sum, accumulated * fading[..., None] + product)


def body(
    linear_query_rows,
    lin_keys,
    linear_value_rows,
    log_decay,
    norm_gain,
    soft_queries,
    soft_keys,
    soft_values,
    window_start,
):
    row_count, heads_here, head_width = linear_query_rows.shape
    cumulated = jnp.cumsum(log_decay, axis=1)
    token_locations = jnp.arange(row_count, dtype=jnp.int32)
    lower_mask = token_locations[:, None] >= token_locations[None, :]
    tail = jnp.exp(cumulated[:, -1:] - cumulated)
    key_product = lin_keys.astype(jnp.float32) * tail.T[:, :, None]
    key_product_upper, key_product_lower = split_parts(key_product)
    recurrent_state = jnp.einsum(
        "egz,egc->gzc", key_product_upper, linear_value_rows, preferred_element_type=jnp.float32
    )
    recurrent_state = recurrent_state + jnp.einsum(
        "egz,egc->gzc", key_product_lower, linear_value_rows, preferred_element_type=jnp.float32
    )
    falling = jnp.exp(cumulated[:, -1])
    kv_here = soft_keys.shape[1]
    group = heads_here // kv_here
    block_index = lax.axis_index("seq")
    key_index = jnp.arange((REACH + 1) * row_count, dtype=jnp.int32)
    key_block = block_index - REACH + key_index // row_count
    causal = (key_index % row_count)[None, :] <= token_locations[:, None]
    visible = ((key_block[None, :] < block_index) | causal) & (key_block[None, :] >= window_start[0])
    lin_scores = jnp.einsum(
        "thd,shd->hts", linear_query_rows, lin_keys, preferred_element_type=jnp.float32
    )
    gap = jnp.where(lower_mask[None], cumulated[:, :, None] - cumulated[:, None, :], -jnp.inf)
    lin_weights = (lin_scores * jnp.exp(gap)).astype(jnp.bfloat16)
    local_part = jnp.einsum(
        "hts,shd->htd", lin_weights, linear_value_rows, preferred_element_type=jnp.float32
    )
    normed, soft_out, lin_out = exclusive_scan(
        falling,
        recurrent_state,
        jnp.stack([soft_keys, soft_values]).transpose(0, 2, 1, 3),
        soft_queries.reshape(row_count, kv_here, group, head_width),
        jnp.where(visible, 0.0, -jnp.inf).astype(jnp.float32),
        linear_query_rows.transpose(1, 0, 2),
        local_part,
        jnp.exp(cumulated)[:, :, None],
        norm_gain.astype(jnp.float32),
        "seq",
    )
    lin_out = lin_out.transpose(1, 0, 2)
    soft_out = soft_out.reshape(row_count, heads_here, head_width)
    return (lin_out, soft_out)


def solution(mesh):
    placed = (
        P("seq", "head", None),
        P("seq", "head", None),
        P("seq", "head", None),
        P("head", "seq"),
        P("head", None),
        P("seq", "head", None),
        P("seq", "head", None),
        P("seq", "head", None),
        P("seq"),
    )
    return jax.shard_map(
        body,
        mesh=mesh,
        in_specs=placed,
        out_specs=(P("seq", "head", None), P("seq", "head", None)),
        check_vma=False,
    )
```

```python
import functools

import jax
import jax.numpy as jnp
from jax import lax
from jax.experimental import pallas as pl
from jax.experimental.pallas import tpu as pltpu
from jax.sharding import PartitionSpec as P

MESH = pl.DeviceIdType.MESH

DH = 128
HEADS = 64
REACH = 3


def scan_kernel(
    rounds,
    chunks,
    reach,
    fall_ref,
    state_ref,
    sent0_ref,
    kv_ref,
    q_ref,
    bias_ref,
    lq_ref,
    local_ref,
    grow_ref,
    gain_ref,
    out_ref,
    soft_ref,
    lin_ref,
    whole,
    whole_fall,
    out_fall,
    suffix,
    suffix_fall,
    got,
    got_fall,
    outgoing,
    outgoing_fall,
    send_sem,
    recv_sem,
    fsend_sem,
    frecv_sem,
    kv_got,
    kv_send,
    kv_recv,
    head_slots,
    head_send,
    head_recv,
):
    me = lax.axis_index("seq")
    head = lax.axis_index("head")
    length = 2**rounds
    width = state_ref.shape[0] // chunks
    jump = 7
    back0, back1, near = rounds, rounds + 1, rounds + 2

    def ahead(dist):
        return 1 - (me + dist) // length

    def behind(dist):
        return (me - dist + length) // length

    far_recv = behind(jump)
    near_recv = behind(4) * (1 - far_recv)
    near_send = 1 - (me + length - 3) // length

    barrier = pltpu.get_barrier_semaphore()
    partners = 0
    distances = [2**k for k in range(rounds)] + list(range(1, reach + 1)) + [jump]
    for dist in sorted(set(distances)):
        partners = partners + ahead(dist) + behind(dist)

        @pl.when(ahead(dist) == 1)
        def _():
            pl.semaphore_signal(barrier, inc=1, device_id=(me + dist, head), device_id_type=MESH)

        @pl.when(behind(dist) == 1)
        def _():
            pl.semaphore_signal(barrier, inc=1, device_id=(me - dist, head), device_id_type=MESH)

    head_count = head_slots.shape[0]
    for other in range(head_count):

        @pl.when(other != head)
        def _():
            pl.semaphore_signal(barrier, inc=1, device_id=(me, other), device_id_type=MESH)

    pl.semaphore_wait(barrier, partners + head_count - 1)

    def kv_copy(dist, device):
        return pltpu.make_async_remote_copy(
            src_ref=kv_ref,
            dst_ref=kv_got.at[dist - 1],
            send_sem=kv_send.at[dist - 1],
            recv_sem=kv_recv.at[dist - 1],
            device_id=(device, head),
            device_id_type=MESH,
        )

    for dist in range(1, reach + 1):

        @pl.when(ahead(dist) == 1)
        def _():
            kv_copy(dist, me + dist).start()

    def state_copy(stage, source, c, device):
        rows = pl.ds(c * width, width)
        return pltpu.make_async_remote_copy(
            src_ref=source.at[rows],
            dst_ref=got.at[stage, rows],
            send_sem=send_sem.at[stage, c],
            recv_sem=recv_sem.at[stage, c],
            device_id=(device, head),
            device_id_type=MESH,
        )

    def fall_copy(stage, source, device):
        return pltpu.make_async_remote_copy(
            src_ref=source,
            dst_ref=got_fall.at[stage],
            send_sem=fsend_sem.at[stage],
            recv_sem=frecv_sem.at[stage],
            device_id=(device, head),
            device_id_type=MESH,
        )

    outgoing_fall[0] = fall_ref[...]

    @pl.when(ahead(1) == 1)
    def _():
        fall_copy(0, outgoing_fall.at[0], me + 1).start()
        for c in range(chunks):
            state_copy(0, sent0_ref, c, me + 1).start()

    @pl.when(behind(1) == 1)
    def _():
        fall_copy(back0, outgoing_fall.at[0], me - 1).start()
        for c in range(chunks):
            state_copy(back0, sent0_ref, c, me - 1).start()

    whole[...] = state_ref[...]
    whole_fall[...] = fall_ref[...]
    suffix[...] = state_ref[...]
    suffix_fall[...] = fall_ref[...]
    out_ref[...] = jnp.zeros_like(out_ref)
    out_fall[...] = jnp.ones_like(out_fall)

    def forward_fall(stage, shift):
        @pl.when(behind(shift) == 1)
        def _():
            fall_copy(stage, outgoing_fall.at[stage], me - shift).wait_recv()
            arrived = got_fall[stage]
            out_fall[...] = arrived * out_fall[...]
            whole_fall[...] = arrived * whole_fall[...]

    def forward_chunk(stage, shift, c, update_whole=True):
        rows = pl.ds(c * width, width)

        @pl.when(behind(shift) == 1)
        def _():
            state_copy(stage, outgoing.at[stage], c, me - shift).wait_recv()
            arrived = got[stage, rows].astype(jnp.float32)
            out_ref[rows] = out_fall[rows][:, None, :] * arrived + out_ref[rows]
            if update_whole:
                whole[rows] = whole_fall[rows][:, None, :] * arrived + whole[rows]

    def backward_fall(stage, shift):
        @pl.when(ahead(shift) == 1)
        def _():
            fall_copy(stage, outgoing_fall.at[stage], me + shift).wait_recv()
            suffix_fall[...] = suffix_fall[...] * got_fall[stage]

    def backward_chunk(stage, shift, c):
        rows = pl.ds(c * width, width)

        @pl.when(ahead(shift) == 1)
        def _():
            state_copy(stage, outgoing.at[stage], c, me + shift).wait_recv()
            arrived = got[stage, rows].astype(jnp.float32)
            suffix[rows] = got_fall[stage][rows][:, None, :] * suffix[rows] + arrived

    def send_chunk(stage, flag, buffer, dist, c):
        rows = pl.ds(c * width, width)

        @pl.when(flag == 1)
        def _():
            outgoing[stage, rows] = buffer[rows].astype(jnp.bfloat16)
            state_copy(stage, outgoing.at[stage], c, me + dist).start()

    def send_fall(stage, flag, buffer_fall, dist):
        @pl.when(flag == 1)
        def _():
            outgoing_fall[stage] = buffer_fall[...]
            fall_copy(stage, outgoing_fall.at[stage], me + dist).start()

    backward_fall(back0, 1)
    send_fall(back1, behind(2), suffix_fall, -2)
    for c in range(chunks):
        forward_chunk(0, 1, c)
        send_chunk(1, ahead(2), whole, 2, c)
        backward_chunk(back0, 1, c)
        send_chunk(back1, behind(2), suffix, -2, c)
    forward_fall(0, 1)
    send_fall(1, ahead(2), whole_fall, 2)

    backward_fall(back1, 2)
    send_fall(2, ahead(jump), suffix_fall, jump)
    for c in range(chunks):
        forward_chunk(1, 2, c)
        send_chunk(near, near_send, whole, 4, c)
        backward_chunk(back1, 2, c)
        send_chunk(2, ahead(jump), suffix, jump, c)
    forward_fall(1, 2)
    send_fall(near, near_send, whole_fall, 4)

    for c in range(chunks):
        rows = pl.ds(c * width, width)
        for flag, dist, stage in ((far_recv, jump, 2), (near_recv, 4, near)):

            @pl.when(flag == 1)
            def _():
                state_copy(stage, outgoing.at[stage], c, me - dist).wait_recv()
                arrived = got[stage, rows].astype(jnp.float32)
                out_ref[rows] = out_fall[rows][:, None, :] * arrived + out_ref[rows]
                whole[rows] = whole_fall[rows][:, None, :] * arrived + whole[rows]

        if rounds > 3:
            send_chunk(3, ahead(8), whole, 8, c)

    for flag, dist, stage in ((far_recv, jump, 2), (near_recv, 4, near)):

        @pl.when(flag == 1)
        def _():
            fall_copy(stage, outgoing_fall.at[stage], me - dist).wait_recv()
            arrived = got_fall[stage]
            out_fall[...] = arrived * out_fall[...]
            whole_fall[...] = arrived * whole_fall[...]

    if rounds > 3:
        send_fall(3, ahead(8), whole_fall, 8)

    def attention():
        for dist in range(1, reach + 1):

            @pl.when(behind(dist) == 1)
            def _():
                kv_copy(dist, me - dist).wait_recv()

            @pl.when(behind(dist) == 0)
            def _():
                kv_got[dist - 1] = jnp.zeros_like(kv_got.at[dist - 1])

            @pl.when(ahead(dist) == 1)
            def _():
                kv_copy(dist, me + dist).wait_send()

        tokens, groups, group = q_ref.shape[0], q_ref.shape[1], q_ref.shape[2]
        scale = float(q_ref.shape[3]) ** (-0.5)
        for g in range(groups):
            q = q_ref[:, g].astype(jnp.float32).reshape(tokens * group, -1).astype(jnp.bfloat16)
            keys = [kv_got[slot, 0, g] for slot in range(reach - 1, -1, -1)] + [kv_ref[0, g]]
            values = [kv_got[slot, 1, g] for slot in range(reach - 1, -1, -1)] + [kv_ref[1, g]]
            logits = jnp.concatenate(
                [
                    lax.dot_general(q, k, (((1,), (1,)), ((), ())), preferred_element_type=jnp.float32)
                    for k in keys
                ],
                axis=1,
            )
            masked = (logits * scale).reshape(tokens, group, -1) + bias_ref[...][:, None, :]
            top = jnp.max(masked, axis=-1, keepdims=True)
            exps = jnp.exp(masked - top)
            total = jnp.sum(exps, axis=-1, keepdims=True)
            probs = exps.reshape(tokens * group, -1).astype(jnp.bfloat16)
            summed = jnp.dot(probs, jnp.concatenate(values, axis=0), preferred_element_type=jnp.float32)
            soft_ref[:, g] = (summed.reshape(tokens, group, -1) / total).astype(soft_ref.dtype)

    for k in range(3, rounds):
        shift, last = 2**k, k == rounds - 1
        if last:
            attention()
        for c in range(chunks):
            forward_chunk(k, shift, c, update_whole=not last)
            if not last:
                rows = pl.ds(c * width, width)

                @pl.when(ahead(2 * shift) == 1)
                def _():
                    outgoing[k + 1, rows] = whole[rows].astype(jnp.bfloat16)
                    state_copy(k + 1, outgoing.at[k + 1], c, me + 2 * shift).start()

        @pl.when(behind(shift) == 1)
        def _():
            fall_copy(k, outgoing_fall.at[k], me - shift).wait_recv()
            arrived = got_fall[k]
            out_fall[...] = arrived * out_fall[...]
            if not last:
                whole_fall[...] = arrived * whole_fall[...]

        if not last:

            @pl.when(ahead(2 * shift) == 1)
            def _():
                outgoing_fall[k + 1] = whole_fall[...]
                fall_copy(k + 1, outgoing_fall.at[k + 1], me + 2 * shift).start()

    sends = [(0, 1, ahead(1)), (back0, -1, behind(1)), (1, 2, ahead(2)), (back1, -2, behind(2))]
    sends += [(2, jump, ahead(jump)), (near, 4, near_send)]
    sends += [(k, 2**k, ahead(2**k)) for k in range(3, rounds)]
    for stage, dist, flag in sends:

        @pl.when(flag == 1)
        def _():
            fall_copy(stage, outgoing_fall.at[stage], me + dist).wait_send()
            for c in range(chunks):
                state_copy(stage, outgoing.at[stage], c, me + dist).wait_send()

    prior = out_ref[...]
    upper = prior.astype(jnp.bfloat16)
    lower = (prior - upper.astype(jnp.float32)).astype(jnp.bfloat16)
    queries = lq_ref[...]
    carried = jnp.einsum("hti,hij->htj", queries, upper, preferred_element_type=jnp.float32)
    carried = carried + jnp.einsum("hti,hij->htj", queries, lower, preferred_element_type=jnp.float32)
    grow = jnp.transpose(grow_ref[...])
    mixed = local_ref[...] + jnp.stack([grow[:, h : h + 1] for h in range(grow.shape[1])]) * carried
    column = jnp.sum(jnp.sum(mixed * mixed, axis=0), axis=1, keepdims=True)
    head_slots[head] = jnp.transpose(jnp.broadcast_to(column, (column.shape[0], 128)))[0:1, :]

    def head_copy(other, slot):
        return pltpu.make_async_remote_copy(
            src_ref=head_slots.at[head],
            dst_ref=head_slots.at[slot],
            send_sem=head_send.at[other],
            recv_sem=head_recv.at[slot],
            device_id=(me, other),
            device_id_type=MESH,
        )

    for other in range(head_count):

        @pl.when(other != head)
        def _():
            head_copy(other, head).start()

    for other in range(head_count):

        @pl.when(other != head)
        def _():
            head_copy(other, other).wait_recv()
            head_copy(other, head).wait_send()

    total = head_slots[0]
    for other in range(1, head_count):
        total = total + head_slots[other]
    heads_all, width_all = lq_ref.shape[0] * head_count, lq_ref.shape[2]
    scale_row = lax.rsqrt(total / (heads_all * width_all) + 1e-06)
    scale = jnp.transpose(jnp.broadcast_to(scale_row, (128, scale_row.shape[1])))[:, 0:1]
    gain = gain_ref[...].astype(jnp.float32)
    lin_ref[...] = (mixed * scale[None] * gain[:, None, :]).astype(lin_ref.dtype)


def exclusive_scan(falling, state, kv, queries, bias, lq, local, grow, gain, axis):
    length = lax.axis_size(axis)
    rounds = length.bit_length() - 1
    stages = rounds + 3
    chunks = 8
    heads, rows, columns = state.shape
    fall_rows = jnp.broadcast_to(falling[:, None], (heads, columns))
    vmem = pl.BlockSpec(memory_space=pltpu.VMEM)
    return pl.pallas_call(
        functools.partial(scan_kernel, rounds, chunks, REACH),
        out_shape=(
            jax.ShapeDtypeStruct(state.shape, jnp.float32),
            jax.ShapeDtypeStruct(queries.shape, queries.dtype),
            jax.ShapeDtypeStruct(lq.shape, jnp.bfloat16),
        ),
        in_specs=[vmem] * 10,
        out_specs=(vmem, vmem, vmem),
        scratch_shapes=[
            pltpu.VMEM(state.shape, jnp.float32),
            pltpu.VMEM((heads, columns), jnp.float32),
            pltpu.VMEM((heads, columns), jnp.float32),
            pltpu.VMEM(state.shape, jnp.float32),
            pltpu.VMEM((heads, columns), jnp.float32),
            pltpu.VMEM((stages,) + state.shape, jnp.bfloat16),
            pltpu.VMEM((stages, heads, columns), jnp.float32),
            pltpu.VMEM((stages,) + state.shape, jnp.bfloat16),
            pltpu.VMEM((stages, heads, columns), jnp.float32),
            pltpu.SemaphoreType.DMA((stages, chunks)),
            pltpu.SemaphoreType.DMA((stages, chunks)),
            pltpu.SemaphoreType.DMA((stages,)),
            pltpu.SemaphoreType.DMA((stages,)),
            pltpu.VMEM((REACH,) + kv.shape, kv.dtype),
            pltpu.SemaphoreType.DMA((REACH,)),
            pltpu.SemaphoreType.DMA((REACH,)),
            pltpu.VMEM((lax.axis_size("head"), 1, columns), jnp.float32),
            pltpu.SemaphoreType.DMA((lax.axis_size("head"),)),
            pltpu.SemaphoreType.DMA((lax.axis_size("head"),)),
        ],
        compiler_params=pltpu.CompilerParams(collective_id=0, has_side_effects=True),
    )(fall_rows, state, state.astype(jnp.bfloat16), kv, queries, bias, lq, local, grow, gain)


def head_sum_kernel(count, value_ref, out_ref, slots, send_sem, recv_sem):
    me = lax.axis_index("seq")
    head = lax.axis_index("head")
    barrier = pltpu.get_barrier_semaphore()
    for other in range(count):

        @pl.when(other != head)
        def _():
            pl.semaphore_signal(barrier, inc=1, device_id=(me, other), device_id_type=MESH)

    pl.semaphore_wait(barrier, count - 1)
    slots[head] = value_ref[...]

    def copy(other, slot):
        return pltpu.make_async_remote_copy(
            src_ref=value_ref,
            dst_ref=slots.at[slot],
            send_sem=send_sem.at[other],
            recv_sem=recv_sem.at[slot],
            device_id=(me, other),
            device_id_type=MESH,
        )

    for other in range(count):

        @pl.when(other != head)
        def _():
            copy(other, head).start()

    for other in range(count):

        @pl.when(other != head)
        def _():
            copy(other, other).wait_recv()
            copy(other, head).wait_send()

    total = slots[0]
    for other in range(1, count):
        total = total + slots[other]
    out_ref[...] = total


def head_sum(value, axis):
    count = lax.axis_size(axis)
    vmem = pl.BlockSpec(memory_space=pltpu.VMEM)
    row = value.reshape(1, -1)
    return pl.pallas_call(
        functools.partial(head_sum_kernel, count),
        out_shape=jax.ShapeDtypeStruct(row.shape, row.dtype),
        in_specs=[vmem],
        out_specs=vmem,
        scratch_shapes=[
            pltpu.VMEM((count,) + row.shape, row.dtype),
            pltpu.SemaphoreType.DMA((count,)),
            pltpu.SemaphoreType.DMA((count,)),
        ],
        compiler_params=pltpu.CompilerParams(collective_id=1, has_side_effects=True),
    )(row).reshape(value.shape)


def from_behind(value, axis, steps):
    count = lax.axis_size(axis)
    first, last = (max(0, -steps), min(count, count - steps))
    return lax.ppermute(value, axis, [(source, source + steps) for source in range(first, last)])


def combine_states(earlier, later):
    return (earlier[0] * later[0], later[0][:, None, None] * earlier[1] + later[1])


def split_parts(matrix):
    upper = matrix.astype(jnp.bfloat16)
    lower = (matrix - upper.astype(jnp.float32)).astype(jnp.bfloat16)
    return (upper, lower)


def attend(carried_over_state, query_rows, key_rows, value_rows, visible, score_scale):
    running_max, running_sum, accumulated = carried_over_state
    attention_logits = (
        jnp.einsum("cphm,npm->phcn", query_rows, key_rows, preferred_element_type=jnp.float32)
        * score_scale
    )
    masked = jnp.where(visible, attention_logits, -jnp.inf)
    new_max = jnp.maximum(running_max, jnp.max(masked, axis=-1))
    power_exponent = jnp.exp(masked - new_max[..., None])
    fading = jnp.exp(running_max - new_max)
    new_sum = running_sum * fading + jnp.sum(power_exponent, axis=-1)
    product = jnp.einsum(
        "qyjl,lqu->qyju",
        power_exponent.astype(jnp.bfloat16),
        value_rows,
        preferred_element_type=jnp.float32,
    )
    return (new_max, new_sum, accumulated * fading[..., None] + product)


def body(
    linear_query_rows,
    lin_keys,
    linear_value_rows,
    log_decay,
    norm_gain,
    soft_queries,
    soft_keys,
    soft_values,
    window_start,
):
    row_count, heads_here, head_width = linear_query_rows.shape
    cumulated = jnp.cumsum(log_decay, axis=1)
    token_locations = jnp.arange(row_count, dtype=jnp.int32)
    lower_mask = token_locations[:, None] >= token_locations[None, :]
    tail = jnp.exp(cumulated[:, -1:] - cumulated)
    key_product = lin_keys.astype(jnp.float32) * tail.T[:, :, None]
    key_product_upper, key_product_lower = split_parts(key_product)
    recurrent_state = jnp.einsum(
        "egz,egc->gzc", key_product_upper, linear_value_rows, preferred_element_type=jnp.float32
    )
    recurrent_state = recurrent_state + jnp.einsum(
        "egz,egc->gzc", key_product_lower, linear_value_rows, preferred_element_type=jnp.float32
    )
    falling = jnp.exp(cumulated[:, -1])
    kv_here = soft_keys.shape[1]
    group = heads_here // kv_here
    block_index = lax.axis_index("seq")
    key_index = jnp.arange((REACH + 1) * row_count, dtype=jnp.int32)
    key_block = block_index - REACH + key_index // row_count
    causal = (key_index % row_count)[None, :] <= token_locations[:, None]
    visible = ((key_block[None, :] < block_index) | causal) & (key_block[None, :] >= window_start[0])
    lin_scores = jnp.einsum(
        "thd,shd->hts", linear_query_rows, lin_keys, preferred_element_type=jnp.float32
    )
    gap = jnp.where(lower_mask[None], cumulated[:, :, None] - cumulated[:, None, :], -jnp.inf)
    lin_weights = (lin_scores * jnp.exp(gap)).astype(jnp.bfloat16)
    local_part = jnp.einsum(
        "hts,shd->htd", lin_weights, linear_value_rows, preferred_element_type=jnp.float32
    )
    normed, soft_out, lin_out = exclusive_scan(
        falling,
        recurrent_state,
        jnp.stack([soft_keys, soft_values]).transpose(0, 2, 1, 3),
        soft_queries.reshape(row_count, kv_here, group, head_width),
        jnp.where(visible, 0.0, -jnp.inf).astype(jnp.float32),
        linear_query_rows.transpose(1, 0, 2),
        local_part,
        jnp.exp(cumulated),
        norm_gain,
        "seq",
    )
    lin_out = lin_out.transpose(1, 0, 2)
    soft_out = soft_out.reshape(row_count, heads_here, head_width)
    return (lin_out, soft_out)


def solution(mesh):
    placed = (
        P("seq", "head", None),
        P("seq", "head", None),
        P("seq", "head", None),
        P("head", "seq"),
        P("head", None),
        P("seq", "head", None),
        P("seq", "head", None),
        P("seq", "head", None),
        P("seq"),
    )
    return jax.shard_map(
        body,
        mesh=mesh,
        in_specs=placed,
        out_specs=(P("seq", "head", None), P("seq", "head", None)),
        check_vma=False,
    )
```

```python
import functools

import jax
import jax.numpy as jnp
from jax import lax
from jax.experimental import pallas as pl
from jax.experimental.pallas import tpu as pltpu
from jax.sharding import PartitionSpec as P

MESH = pl.DeviceIdType.MESH

DH = 128
HEADS = 64
REACH = 3


def scan_kernel(
    rounds,
    chunks,
    reach,
    fall_ref,
    state_ref,
    sent0_ref,
    kv_ref,
    q_ref,
    bias_ref,
    lq_ref,
    local_ref,
    grow_ref,
    gain_ref,
    out_ref,
    soft_ref,
    lin_ref,
    whole,
    whole_fall,
    out_fall,
    suffix,
    suffix_fall,
    got,
    got_fall,
    outgoing,
    outgoing_fall,
    send_sem,
    recv_sem,
    fsend_sem,
    frecv_sem,
    kv_got,
    kv_send,
    kv_recv,
    head_slots,
    head_send,
    head_recv,
):
    me = lax.axis_index("seq")
    head = lax.axis_index("head")
    length = 2**rounds
    width = state_ref.shape[0] // chunks
    jump = 7
    back0, back1, near = rounds, rounds + 1, rounds + 2

    def ahead(dist):
        return 1 - (me + dist) // length

    def behind(dist):
        return (me - dist + length) // length

    far_recv = behind(jump)
    near_recv = behind(4) * (1 - far_recv)
    near_send = 1 - (me + length - 3) // length

    barrier = pltpu.get_barrier_semaphore()
    partners = 0
    distances = [2**k for k in range(rounds)] + list(range(1, reach + 1)) + [jump]
    for dist in sorted(set(distances)):
        partners = partners + ahead(dist) + behind(dist)

        @pl.when(ahead(dist) == 1)
        def _():
            pl.semaphore_signal(barrier, inc=1, device_id=(me + dist, head), device_id_type=MESH)

        @pl.when(behind(dist) == 1)
        def _():
            pl.semaphore_signal(barrier, inc=1, device_id=(me - dist, head), device_id_type=MESH)

    head_count = head_slots.shape[0]
    for other in range(head_count):

        @pl.when(other != head)
        def _():
            pl.semaphore_signal(barrier, inc=1, device_id=(me, other), device_id_type=MESH)

    pl.semaphore_wait(barrier, partners + head_count - 1)

    def kv_copy(dist, device):
        return pltpu.make_async_remote_copy(
            src_ref=kv_ref,
            dst_ref=kv_got.at[dist - 1],
            send_sem=kv_send.at[dist - 1],
            recv_sem=kv_recv.at[dist - 1],
            device_id=(device, head),
            device_id_type=MESH,
        )

    for dist in range(1, reach + 1):

        @pl.when(ahead(dist) == 1)
        def _():
            kv_copy(dist, me + dist).start()

    def state_copy(stage, source, c, device):
        rows = pl.ds(c * width, width)
        return pltpu.make_async_remote_copy(
            src_ref=source.at[rows],
            dst_ref=got.at[stage, rows],
            send_sem=send_sem.at[stage, c],
            recv_sem=recv_sem.at[stage, c],
            device_id=(device, head),
            device_id_type=MESH,
        )

    def fall_copy(stage, source, device):
        return pltpu.make_async_remote_copy(
            src_ref=source,
            dst_ref=got_fall.at[stage],
            send_sem=fsend_sem.at[stage],
            recv_sem=frecv_sem.at[stage],
            device_id=(device, head),
            device_id_type=MESH,
        )

    outgoing_fall[0] = fall_ref[...]

    @pl.when(ahead(1) == 1)
    def _():
        fall_copy(0, outgoing_fall.at[0], me + 1).start()
        for c in range(chunks):
            state_copy(0, sent0_ref, c, me + 1).start()

    @pl.when(behind(1) == 1)
    def _():
        fall_copy(back0, outgoing_fall.at[0], me - 1).start()
        for c in range(chunks):
            state_copy(back0, sent0_ref, c, me - 1).start()

    whole[...] = state_ref[...]
    whole_fall[...] = fall_ref[...]
    suffix[...] = state_ref[...]
    suffix_fall[...] = fall_ref[...]
    out_ref[...] = jnp.zeros_like(out_ref)
    out_fall[...] = jnp.ones_like(out_fall)

    def forward_fall(stage, shift):
        @pl.when(behind(shift) == 1)
        def _():
            fall_copy(stage, outgoing_fall.at[stage], me - shift).wait_recv()
            arrived = got_fall[stage]
            out_fall[...] = arrived * out_fall[...]
            whole_fall[...] = arrived * whole_fall[...]

    def forward_chunk(stage, shift, c, update_whole=True):
        rows = pl.ds(c * width, width)

        @pl.when(behind(shift) == 1)
        def _():
            state_copy(stage, outgoing.at[stage], c, me - shift).wait_recv()
            arrived = got[stage, rows].astype(jnp.float32)
            out_ref[rows] = out_fall[rows][:, None, :] * arrived + out_ref[rows]
            if update_whole:
                whole[rows] = whole_fall[rows][:, None, :] * arrived + whole[rows]

    def backward_fall(stage, shift):
        @pl.when(ahead(shift) == 1)
        def _():
            fall_copy(stage, outgoing_fall.at[stage], me + shift).wait_recv()
            suffix_fall[...] = suffix_fall[...] * got_fall[stage]

    def backward_chunk(stage, shift, c):
        rows = pl.ds(c * width, width)

        @pl.when(ahead(shift) == 1)
        def _():
            state_copy(stage, outgoing.at[stage], c, me + shift).wait_recv()
            arrived = got[stage, rows].astype(jnp.float32)
            suffix[rows] = got_fall[stage][rows][:, None, :] * suffix[rows] + arrived

    def send_chunk(stage, flag, buffer, dist, c):
        rows = pl.ds(c * width, width)

        @pl.when(flag == 1)
        def _():
            outgoing[stage, rows] = buffer[rows].astype(jnp.bfloat16)
            state_copy(stage, outgoing.at[stage], c, me + dist).start()

    def send_fall(stage, flag, buffer_fall, dist):
        @pl.when(flag == 1)
        def _():
            outgoing_fall[stage] = buffer_fall[...]
            fall_copy(stage, outgoing_fall.at[stage], me + dist).start()

    backward_fall(back0, 1)
    send_fall(back1, behind(2), suffix_fall, -2)
    for c in range(chunks):
        forward_chunk(0, 1, c)
        send_chunk(1, ahead(2), whole, 2, c)
        backward_chunk(back0, 1, c)
        send_chunk(back1, behind(2), suffix, -2, c)
    forward_fall(0, 1)
    send_fall(1, ahead(2), whole_fall, 2)

    backward_fall(back1, 2)
    send_fall(2, ahead(jump), suffix_fall, jump)
    for c in range(chunks):
        forward_chunk(1, 2, c)
        send_chunk(near, near_send, whole, 4, c)
        backward_chunk(back1, 2, c)
        send_chunk(2, ahead(jump), suffix, jump, c)
    forward_fall(1, 2)
    send_fall(near, near_send, whole_fall, 4)

    for c in range(chunks):
        rows = pl.ds(c * width, width)
        for flag, dist, stage in ((far_recv, jump, 2), (near_recv, 4, near)):

            @pl.when(flag == 1)
            def _():
                state_copy(stage, outgoing.at[stage], c, me - dist).wait_recv()
                arrived = got[stage, rows].astype(jnp.float32)
                out_ref[rows] = out_fall[rows][:, None, :] * arrived + out_ref[rows]
                whole[rows] = whole_fall[rows][:, None, :] * arrived + whole[rows]

        if rounds > 3:
            send_chunk(3, ahead(8), whole, 8, c)

    for flag, dist, stage in ((far_recv, jump, 2), (near_recv, 4, near)):

        @pl.when(flag == 1)
        def _():
            fall_copy(stage, outgoing_fall.at[stage], me - dist).wait_recv()
            arrived = got_fall[stage]
            out_fall[...] = arrived * out_fall[...]
            whole_fall[...] = arrived * whole_fall[...]

    if rounds > 3:
        send_fall(3, ahead(8), whole_fall, 8)

    def attention():
        for dist in range(1, reach + 1):

            @pl.when(behind(dist) == 1)
            def _():
                kv_copy(dist, me - dist).wait_recv()

            @pl.when(behind(dist) == 0)
            def _():
                kv_got[dist - 1] = jnp.zeros_like(kv_got.at[dist - 1])

            @pl.when(ahead(dist) == 1)
            def _():
                kv_copy(dist, me + dist).wait_send()

        tokens, groups, group = q_ref.shape[0], q_ref.shape[1], q_ref.shape[2]
        scale = float(q_ref.shape[3]) ** (-0.5)
        for g in range(groups):
            q = q_ref[:, g].astype(jnp.float32).reshape(tokens * group, -1).astype(jnp.bfloat16)
            keys = [kv_got[slot, 0, g] for slot in range(reach - 1, -1, -1)] + [kv_ref[0, g]]
            values = [kv_got[slot, 1, g] for slot in range(reach - 1, -1, -1)] + [kv_ref[1, g]]
            logits = jnp.concatenate(
                [
                    lax.dot_general(q, k, (((1,), (1,)), ((), ())), preferred_element_type=jnp.float32)
                    for k in keys
                ],
                axis=1,
            )
            masked = (logits * scale).reshape(tokens, group, -1) + bias_ref[...][:, None, :]
            top = jnp.max(masked, axis=-1, keepdims=True)
            exps = jnp.exp(masked - top)
            total = jnp.sum(exps, axis=-1, keepdims=True)
            probs = exps.reshape(tokens * group, -1).astype(jnp.bfloat16)
            summed = jnp.dot(probs, jnp.concatenate(values, axis=0), preferred_element_type=jnp.float32)
            soft_ref[:, pl.ds(g * group, group), :] = (summed.reshape(tokens, group, -1) / total).astype(
                soft_ref.dtype
            )

    for k in range(3, rounds):
        shift, last = 2**k, k == rounds - 1
        if last:
            attention()
        for c in range(chunks):
            forward_chunk(k, shift, c, update_whole=not last)
            if not last:
                rows = pl.ds(c * width, width)

                @pl.when(ahead(2 * shift) == 1)
                def _():
                    outgoing[k + 1, rows] = whole[rows].astype(jnp.bfloat16)
                    state_copy(k + 1, outgoing.at[k + 1], c, me + 2 * shift).start()

        @pl.when(behind(shift) == 1)
        def _():
            fall_copy(k, outgoing_fall.at[k], me - shift).wait_recv()
            arrived = got_fall[k]
            out_fall[...] = arrived * out_fall[...]
            if not last:
                whole_fall[...] = arrived * whole_fall[...]

        if not last:

            @pl.when(ahead(2 * shift) == 1)
            def _():
                outgoing_fall[k + 1] = whole_fall[...]
                fall_copy(k + 1, outgoing_fall.at[k + 1], me + 2 * shift).start()

    sends = [(0, 1, ahead(1)), (back0, -1, behind(1)), (1, 2, ahead(2)), (back1, -2, behind(2))]
    sends += [(2, jump, ahead(jump)), (near, 4, near_send)]
    sends += [(k, 2**k, ahead(2**k)) for k in range(3, rounds)]
    for stage, dist, flag in sends:

        @pl.when(flag == 1)
        def _():
            fall_copy(stage, outgoing_fall.at[stage], me + dist).wait_send()
            for c in range(chunks):
                state_copy(stage, outgoing.at[stage], c, me + dist).wait_send()

    prior = out_ref[...]
    upper = prior.astype(jnp.bfloat16)
    lower = (prior - upper.astype(jnp.float32)).astype(jnp.bfloat16)
    queries = lq_ref[...]
    carried = jnp.einsum("hti,hij->htj", queries, upper, preferred_element_type=jnp.float32)
    carried = carried + jnp.einsum("hti,hij->htj", queries, lower, preferred_element_type=jnp.float32)
    grow = jnp.transpose(grow_ref[...])
    mixed = local_ref[...] + jnp.stack([grow[:, h : h + 1] for h in range(grow.shape[1])]) * carried
    column = jnp.sum(jnp.sum(mixed * mixed, axis=0), axis=1, keepdims=True)
    head_slots[head] = jnp.transpose(jnp.broadcast_to(column, (column.shape[0], 128)))[0:1, :]

    def head_copy(other, slot):
        return pltpu.make_async_remote_copy(
            src_ref=head_slots.at[head],
            dst_ref=head_slots.at[slot],
            send_sem=head_send.at[other],
            recv_sem=head_recv.at[slot],
            device_id=(me, other),
            device_id_type=MESH,
        )

    for other in range(head_count):

        @pl.when(other != head)
        def _():
            head_copy(other, head).start()

    for other in range(head_count):

        @pl.when(other != head)
        def _():
            head_copy(other, other).wait_recv()
            head_copy(other, head).wait_send()

    total = head_slots[0]
    for other in range(1, head_count):
        total = total + head_slots[other]
    heads_all, width_all = lq_ref.shape[0] * head_count, lq_ref.shape[2]
    scale_row = lax.rsqrt(total / (heads_all * width_all) + 1e-06)
    scale = jnp.transpose(jnp.broadcast_to(scale_row, (128, scale_row.shape[1])))[:, 0:1]
    gain = gain_ref[...].astype(jnp.float32)
    result = (mixed * scale[None] * gain[:, None, :]).astype(lin_ref.dtype)
    for h in range(result.shape[0]):
        lin_ref[:, h, :] = result[h]


def exclusive_scan(falling, state, kv, queries, bias, lq, local, grow, gain, axis):
    length = lax.axis_size(axis)
    rounds = length.bit_length() - 1
    stages = rounds + 3
    chunks = 8
    heads, rows, columns = state.shape
    fall_rows = jnp.broadcast_to(falling[:, None], (heads, columns))
    vmem = pl.BlockSpec(memory_space=pltpu.VMEM)
    return pl.pallas_call(
        functools.partial(scan_kernel, rounds, chunks, REACH),
        out_shape=(
            jax.ShapeDtypeStruct(state.shape, jnp.float32),
            jax.ShapeDtypeStruct((rows, heads, columns), queries.dtype),
            jax.ShapeDtypeStruct((rows, heads, columns), jnp.bfloat16),
        ),
        in_specs=[vmem] * 10,
        out_specs=(vmem, vmem, vmem),
        scratch_shapes=[
            pltpu.VMEM(state.shape, jnp.float32),
            pltpu.VMEM((heads, columns), jnp.float32),
            pltpu.VMEM((heads, columns), jnp.float32),
            pltpu.VMEM(state.shape, jnp.float32),
            pltpu.VMEM((heads, columns), jnp.float32),
            pltpu.VMEM((stages,) + state.shape, jnp.bfloat16),
            pltpu.VMEM((stages, heads, columns), jnp.float32),
            pltpu.VMEM((stages,) + state.shape, jnp.bfloat16),
            pltpu.VMEM((stages, heads, columns), jnp.float32),
            pltpu.SemaphoreType.DMA((stages, chunks)),
            pltpu.SemaphoreType.DMA((stages, chunks)),
            pltpu.SemaphoreType.DMA((stages,)),
            pltpu.SemaphoreType.DMA((stages,)),
            pltpu.VMEM((REACH,) + kv.shape, kv.dtype),
            pltpu.SemaphoreType.DMA((REACH,)),
            pltpu.SemaphoreType.DMA((REACH,)),
            pltpu.VMEM((lax.axis_size("head"), 1, columns), jnp.float32),
            pltpu.SemaphoreType.DMA((lax.axis_size("head"),)),
            pltpu.SemaphoreType.DMA((lax.axis_size("head"),)),
        ],
        compiler_params=pltpu.CompilerParams(collective_id=0, has_side_effects=True),
    )(fall_rows, state, state.astype(jnp.bfloat16), kv, queries, bias, lq, local, grow, gain)


def head_sum_kernel(count, value_ref, out_ref, slots, send_sem, recv_sem):
    me = lax.axis_index("seq")
    head = lax.axis_index("head")
    barrier = pltpu.get_barrier_semaphore()
    for other in range(count):

        @pl.when(other != head)
        def _():
            pl.semaphore_signal(barrier, inc=1, device_id=(me, other), device_id_type=MESH)

    pl.semaphore_wait(barrier, count - 1)
    slots[head] = value_ref[...]

    def copy(other, slot):
        return pltpu.make_async_remote_copy(
            src_ref=value_ref,
            dst_ref=slots.at[slot],
            send_sem=send_sem.at[other],
            recv_sem=recv_sem.at[slot],
            device_id=(me, other),
            device_id_type=MESH,
        )

    for other in range(count):

        @pl.when(other != head)
        def _():
            copy(other, head).start()

    for other in range(count):

        @pl.when(other != head)
        def _():
            copy(other, other).wait_recv()
            copy(other, head).wait_send()

    total = slots[0]
    for other in range(1, count):
        total = total + slots[other]
    out_ref[...] = total


def head_sum(value, axis):
    count = lax.axis_size(axis)
    vmem = pl.BlockSpec(memory_space=pltpu.VMEM)
    row = value.reshape(1, -1)
    return pl.pallas_call(
        functools.partial(head_sum_kernel, count),
        out_shape=jax.ShapeDtypeStruct(row.shape, row.dtype),
        in_specs=[vmem],
        out_specs=vmem,
        scratch_shapes=[
            pltpu.VMEM((count,) + row.shape, row.dtype),
            pltpu.SemaphoreType.DMA((count,)),
            pltpu.SemaphoreType.DMA((count,)),
        ],
        compiler_params=pltpu.CompilerParams(collective_id=1, has_side_effects=True),
    )(row).reshape(value.shape)


def from_behind(value, axis, steps):
    count = lax.axis_size(axis)
    first, last = (max(0, -steps), min(count, count - steps))
    return lax.ppermute(value, axis, [(source, source + steps) for source in range(first, last)])


def combine_states(earlier, later):
    return (earlier[0] * later[0], later[0][:, None, None] * earlier[1] + later[1])


def split_parts(matrix):
    upper = matrix.astype(jnp.bfloat16)
    lower = (matrix - upper.astype(jnp.float32)).astype(jnp.bfloat16)
    return (upper, lower)


def attend(carried_over_state, query_rows, key_rows, value_rows, visible, score_scale):
    running_max, running_sum, accumulated = carried_over_state
    attention_logits = (
        jnp.einsum("cphm,npm->phcn", query_rows, key_rows, preferred_element_type=jnp.float32)
        * score_scale
    )
    masked = jnp.where(visible, attention_logits, -jnp.inf)
    new_max = jnp.maximum(running_max, jnp.max(masked, axis=-1))
    power_exponent = jnp.exp(masked - new_max[..., None])
    fading = jnp.exp(running_max - new_max)
    new_sum = running_sum * fading + jnp.sum(power_exponent, axis=-1)
    product = jnp.einsum(
        "qyjl,lqu->qyju",
        power_exponent.astype(jnp.bfloat16),
        value_rows,
        preferred_element_type=jnp.float32,
    )
    return (new_max, new_sum, accumulated * fading[..., None] + product)


def body(
    linear_query_rows,
    lin_keys,
    linear_value_rows,
    log_decay,
    norm_gain,
    soft_queries,
    soft_keys,
    soft_values,
    window_start,
):
    row_count, heads_here, head_width = linear_query_rows.shape
    cumulated = jnp.cumsum(log_decay, axis=1)
    token_locations = jnp.arange(row_count, dtype=jnp.int32)
    lower_mask = token_locations[:, None] >= token_locations[None, :]
    tail = jnp.exp(cumulated[:, -1:] - cumulated)
    key_product = lin_keys.astype(jnp.float32) * tail.T[:, :, None]
    key_product_upper, key_product_lower = split_parts(key_product)
    recurrent_state = jnp.einsum(
        "egz,egc->gzc", key_product_upper, linear_value_rows, preferred_element_type=jnp.float32
    )
    recurrent_state = recurrent_state + jnp.einsum(
        "egz,egc->gzc", key_product_lower, linear_value_rows, preferred_element_type=jnp.float32
    )
    falling = jnp.exp(cumulated[:, -1])
    kv_here = soft_keys.shape[1]
    group = heads_here // kv_here
    block_index = lax.axis_index("seq")
    key_index = jnp.arange((REACH + 1) * row_count, dtype=jnp.int32)
    key_block = block_index - REACH + key_index // row_count
    causal = (key_index % row_count)[None, :] <= token_locations[:, None]
    visible = ((key_block[None, :] < block_index) | causal) & (key_block[None, :] >= window_start[0])
    lin_scores = jnp.einsum(
        "thd,shd->hts", linear_query_rows, lin_keys, preferred_element_type=jnp.float32
    )
    gap = jnp.where(lower_mask[None], cumulated[:, :, None] - cumulated[:, None, :], -jnp.inf)
    lin_weights = (lin_scores * jnp.exp(gap)).astype(jnp.bfloat16)
    local_part = jnp.einsum(
        "hts,shd->htd", lin_weights, linear_value_rows, preferred_element_type=jnp.float32
    )
    normed, soft_out, lin_out = exclusive_scan(
        falling,
        recurrent_state,
        jnp.stack([soft_keys, soft_values]).transpose(0, 2, 1, 3),
        soft_queries.reshape(row_count, kv_here, group, head_width),
        jnp.where(visible, 0.0, -jnp.inf).astype(jnp.float32),
        linear_query_rows.transpose(1, 0, 2),
        local_part,
        jnp.exp(cumulated),
        norm_gain,
        "seq",
    )
    soft_out = soft_out.reshape(row_count, heads_here, head_width)
    return (lin_out, soft_out)


def solution(mesh):
    placed = (
        P("seq", "head", None),
        P("seq", "head", None),
        P("seq", "head", None),
        P("head", "seq"),
        P("head", None),
        P("seq", "head", None),
        P("seq", "head", None),
        P("seq", "head", None),
        P("seq"),
    )
    return jax.shard_map(
        body,
        mesh=mesh,
        in_specs=placed,
        out_specs=(P("seq", "head", None), P("seq", "head", None)),
        check_vma=False,
    )
```

```python
import functools

import jax
import jax.numpy as jnp
from jax import lax
from jax.experimental import pallas as pl
from jax.experimental.pallas import tpu as pltpu
from jax.sharding import PartitionSpec as P

MESH = pl.DeviceIdType.MESH

DH = 128
HEADS = 64
REACH = 3


def scan_kernel(
    rounds,
    chunks,
    reach,
    fall_ref,
    state_ref,
    sent0_ref,
    kv_ref,
    q_ref,
    bias_ref,
    lq_ref,
    local_ref,
    grow_ref,
    gain_ref,
    out_ref,
    soft_ref,
    lin_ref,
    whole,
    whole_fall,
    out_fall,
    suffix,
    suffix_fall,
    got,
    got_fall,
    outgoing,
    outgoing_fall,
    send_sem,
    recv_sem,
    fsend_sem,
    frecv_sem,
    kv_got,
    kv_send,
    kv_recv,
    head_slots,
    head_send,
    head_recv,
):
    me = lax.axis_index("seq")
    head = lax.axis_index("head")
    length = 2**rounds
    width = state_ref.shape[0] // chunks
    jump = 7
    back0, back1, near = rounds, rounds + 1, rounds + 2

    def ahead(dist):
        return 1 - (me + dist) // length

    def behind(dist):
        return (me - dist + length) // length

    far_recv = behind(jump)
    near_recv = behind(4) * (1 - far_recv)
    near_send = 1 - (me + length - 3) // length

    barrier = pltpu.get_barrier_semaphore()
    partners = 0
    distances = [2**k for k in range(rounds)] + list(range(1, reach + 1)) + [jump]
    for dist in sorted(set(distances)):
        partners = partners + ahead(dist) + behind(dist)

        @pl.when(ahead(dist) == 1)
        def _():
            pl.semaphore_signal(barrier, inc=1, device_id=(me + dist, head), device_id_type=MESH)

        @pl.when(behind(dist) == 1)
        def _():
            pl.semaphore_signal(barrier, inc=1, device_id=(me - dist, head), device_id_type=MESH)

    head_count = head_slots.shape[0]
    for other in range(head_count):

        @pl.when(other != head)
        def _():
            pl.semaphore_signal(barrier, inc=1, device_id=(me, other), device_id_type=MESH)

    pl.semaphore_wait(barrier, partners + head_count - 1)

    def kv_copy(dist, device):
        return pltpu.make_async_remote_copy(
            src_ref=kv_ref,
            dst_ref=kv_got.at[dist - 1],
            send_sem=kv_send.at[dist - 1],
            recv_sem=kv_recv.at[dist - 1],
            device_id=(device, head),
            device_id_type=MESH,
        )

    for dist in range(1, reach + 1):

        @pl.when(ahead(dist) == 1)
        def _():
            kv_copy(dist, me + dist).start()

    def state_copy(stage, source, c, device):
        rows = pl.ds(c * width, width)
        return pltpu.make_async_remote_copy(
            src_ref=source.at[rows],
            dst_ref=got.at[stage, rows],
            send_sem=send_sem.at[stage, c],
            recv_sem=recv_sem.at[stage, c],
            device_id=(device, head),
            device_id_type=MESH,
        )

    def fall_copy(stage, source, device):
        return pltpu.make_async_remote_copy(
            src_ref=source,
            dst_ref=got_fall.at[stage],
            send_sem=fsend_sem.at[stage],
            recv_sem=frecv_sem.at[stage],
            device_id=(device, head),
            device_id_type=MESH,
        )

    outgoing_fall[0] = fall_ref[...]

    @pl.when(ahead(1) == 1)
    def _():
        fall_copy(0, outgoing_fall.at[0], me + 1).start()
        for c in range(chunks):
            state_copy(0, sent0_ref, c, me + 1).start()

    @pl.when(behind(1) == 1)
    def _():
        fall_copy(back0, outgoing_fall.at[0], me - 1).start()
        for c in range(chunks):
            state_copy(back0, sent0_ref, c, me - 1).start()

    whole[...] = state_ref[...]
    whole_fall[...] = fall_ref[...]
    suffix[...] = state_ref[...]
    suffix_fall[...] = fall_ref[...]
    out_ref[...] = jnp.zeros_like(out_ref)
    out_fall[...] = jnp.ones_like(out_fall)

    def forward_fall(stage, shift):
        @pl.when(behind(shift) == 1)
        def _():
            fall_copy(stage, outgoing_fall.at[stage], me - shift).wait_recv()
            arrived = got_fall[stage]
            out_fall[...] = arrived * out_fall[...]
            whole_fall[...] = arrived * whole_fall[...]

    def forward_chunk(stage, shift, c, update_whole=True):
        rows = pl.ds(c * width, width)

        @pl.when(behind(shift) == 1)
        def _():
            state_copy(stage, outgoing.at[stage], c, me - shift).wait_recv()
            arrived = got[stage, rows].astype(jnp.float32)
            out_ref[rows] = out_fall[rows][:, None, :] * arrived + out_ref[rows]
            if update_whole:
                whole[rows] = whole_fall[rows][:, None, :] * arrived + whole[rows]

    def backward_fall(stage, shift):
        @pl.when(ahead(shift) == 1)
        def _():
            fall_copy(stage, outgoing_fall.at[stage], me + shift).wait_recv()
            suffix_fall[...] = suffix_fall[...] * got_fall[stage]

    def backward_chunk(stage, shift, c):
        rows = pl.ds(c * width, width)

        @pl.when(ahead(shift) == 1)
        def _():
            state_copy(stage, outgoing.at[stage], c, me + shift).wait_recv()
            arrived = got[stage, rows].astype(jnp.float32)
            suffix[rows] = got_fall[stage][rows][:, None, :] * suffix[rows] + arrived

    def send_chunk(stage, flag, buffer, dist, c):
        rows = pl.ds(c * width, width)

        @pl.when(flag == 1)
        def _():
            outgoing[stage, rows] = buffer[rows].astype(jnp.bfloat16)
            state_copy(stage, outgoing.at[stage], c, me + dist).start()

    def send_fall(stage, flag, buffer_fall, dist):
        @pl.when(flag == 1)
        def _():
            outgoing_fall[stage] = buffer_fall[...]
            fall_copy(stage, outgoing_fall.at[stage], me + dist).start()

    backward_fall(back0, 1)
    send_fall(back1, behind(2), suffix_fall, -2)
    for c in range(chunks):
        forward_chunk(0, 1, c)
        send_chunk(1, ahead(2), whole, 2, c)
        backward_chunk(back0, 1, c)
        send_chunk(back1, behind(2), suffix, -2, c)
    forward_fall(0, 1)
    send_fall(1, ahead(2), whole_fall, 2)

    backward_fall(back1, 2)
    send_fall(2, ahead(jump), suffix_fall, jump)
    for c in range(chunks):
        forward_chunk(1, 2, c)
        send_chunk(near, near_send, whole, 4, c)
        backward_chunk(back1, 2, c)
        send_chunk(2, ahead(jump), suffix, jump, c)
    forward_fall(1, 2)
    send_fall(near, near_send, whole_fall, 4)

    for c in range(chunks):
        rows = pl.ds(c * width, width)
        for flag, dist, stage in ((far_recv, jump, 2), (near_recv, 4, near)):

            @pl.when(flag == 1)
            def _():
                state_copy(stage, outgoing.at[stage], c, me - dist).wait_recv()
                arrived = got[stage, rows].astype(jnp.float32)
                out_ref[rows] = out_fall[rows][:, None, :] * arrived + out_ref[rows]
                whole[rows] = whole_fall[rows][:, None, :] * arrived + whole[rows]

        if rounds > 3:
            send_chunk(3, ahead(8), whole, 8, c)

    for flag, dist, stage in ((far_recv, jump, 2), (near_recv, 4, near)):

        @pl.when(flag == 1)
        def _():
            fall_copy(stage, outgoing_fall.at[stage], me - dist).wait_recv()
            arrived = got_fall[stage]
            out_fall[...] = arrived * out_fall[...]
            whole_fall[...] = arrived * whole_fall[...]

    if rounds > 3:
        send_fall(3, ahead(8), whole_fall, 8)

    def attention():
        for dist in range(1, reach + 1):

            @pl.when(behind(dist) == 1)
            def _():
                kv_copy(dist, me - dist).wait_recv()

            @pl.when(behind(dist) == 0)
            def _():
                kv_got[dist - 1] = jnp.zeros_like(kv_got.at[dist - 1])

            @pl.when(ahead(dist) == 1)
            def _():
                kv_copy(dist, me + dist).wait_send()

        tokens, groups, group = q_ref.shape[0], q_ref.shape[1], q_ref.shape[2]
        scale = float(q_ref.shape[3]) ** (-0.5)
        for g in range(groups):
            q = q_ref[:, g].astype(jnp.float32).reshape(tokens * group, -1).astype(jnp.bfloat16)
            keys = [kv_got[slot, 0, g] for slot in range(reach - 1, -1, -1)] + [kv_ref[0, g]]
            values = [kv_got[slot, 1, g] for slot in range(reach - 1, -1, -1)] + [kv_ref[1, g]]
            logits = jnp.concatenate(
                [
                    lax.dot_general(q, k, (((1,), (1,)), ((), ())), preferred_element_type=jnp.float32)
                    for k in keys
                ],
                axis=1,
            )
            masked = (logits * scale).reshape(tokens, group, -1) + bias_ref[...][:, None, :]
            top = jnp.max(masked, axis=-1, keepdims=True)
            exps = jnp.exp(masked - top)
            total = jnp.sum(exps, axis=-1, keepdims=True)
            probs = exps.reshape(tokens * group, -1).astype(jnp.bfloat16)
            summed = jnp.dot(probs, jnp.concatenate(values, axis=0), preferred_element_type=jnp.float32)
            soft_ref[:, g] = (summed.reshape(tokens, group, -1) / total).astype(soft_ref.dtype)

    for k in range(3, rounds):
        shift, last = 2**k, k == rounds - 1
        if last:
            attention()
        for c in range(chunks):
            forward_chunk(k, shift, c, update_whole=not last)
            if not last:
                rows = pl.ds(c * width, width)

                @pl.when(ahead(2 * shift) == 1)
                def _():
                    outgoing[k + 1, rows] = whole[rows].astype(jnp.bfloat16)
                    state_copy(k + 1, outgoing.at[k + 1], c, me + 2 * shift).start()

        @pl.when(behind(shift) == 1)
        def _():
            fall_copy(k, outgoing_fall.at[k], me - shift).wait_recv()
            arrived = got_fall[k]
            out_fall[...] = arrived * out_fall[...]
            if not last:
                whole_fall[...] = arrived * whole_fall[...]

        if not last:

            @pl.when(ahead(2 * shift) == 1)
            def _():
                outgoing_fall[k + 1] = whole_fall[...]
                fall_copy(k + 1, outgoing_fall.at[k + 1], me + 2 * shift).start()

    sends = [(0, 1, ahead(1)), (back0, -1, behind(1)), (1, 2, ahead(2)), (back1, -2, behind(2))]
    sends += [(2, jump, ahead(jump)), (near, 4, near_send)]
    sends += [(k, 2**k, ahead(2**k)) for k in range(3, rounds)]
    for stage, dist, flag in sends:

        @pl.when(flag == 1)
        def _():
            fall_copy(stage, outgoing_fall.at[stage], me + dist).wait_send()
            for c in range(chunks):
                state_copy(stage, outgoing.at[stage], c, me + dist).wait_send()

    prior = out_ref[...]
    upper = prior.astype(jnp.bfloat16)
    lower = (prior - upper.astype(jnp.float32)).astype(jnp.bfloat16)
    queries = lq_ref[...]
    carried = jnp.einsum("hti,hij->htj", queries, upper, preferred_element_type=jnp.float32)
    carried = carried + jnp.einsum("hti,hij->htj", queries, lower, preferred_element_type=jnp.float32)
    grow = jnp.transpose(grow_ref[...])
    mixed = local_ref[...] + jnp.stack([grow[:, h : h + 1] for h in range(grow.shape[1])]) * carried
    column = jnp.sum(jnp.sum(mixed * mixed, axis=0), axis=1, keepdims=True)
    head_slots[head] = jnp.transpose(jnp.broadcast_to(column, (column.shape[0], 128)))[0:1, :]

    def head_copy(other, slot):
        return pltpu.make_async_remote_copy(
            src_ref=head_slots.at[head],
            dst_ref=head_slots.at[slot],
            send_sem=head_send.at[other],
            recv_sem=head_recv.at[slot],
            device_id=(me, other),
            device_id_type=MESH,
        )

    for other in range(head_count):

        @pl.when(other != head)
        def _():
            head_copy(other, head).start()

    for other in range(head_count):

        @pl.when(other != head)
        def _():
            head_copy(other, other).wait_recv()
            head_copy(other, head).wait_send()

    total = head_slots[0]
    for other in range(1, head_count):
        total = total + head_slots[other]
    heads_all, width_all = lq_ref.shape[0] * head_count, lq_ref.shape[2]
    scale_row = lax.rsqrt(total / (heads_all * width_all) + 1e-06)
    scale = jnp.transpose(jnp.broadcast_to(scale_row, (128, scale_row.shape[1])))[:, 0:1]
    gain = gain_ref[...].astype(jnp.float32)
    lin_ref[...] = (mixed * scale[None] * gain[:, None, :]).astype(lin_ref.dtype)


def exclusive_scan(falling, state, kv, queries, bias, lq, local, grow, gain, axis):
    length = lax.axis_size(axis)
    rounds = length.bit_length() - 1
    stages = rounds + 3
    chunks = 4
    heads, rows, columns = state.shape
    fall_rows = jnp.broadcast_to(falling[:, None], (heads, columns))
    vmem = pl.BlockSpec(memory_space=pltpu.VMEM)
    return pl.pallas_call(
        functools.partial(scan_kernel, rounds, chunks, REACH),
        out_shape=(
            jax.ShapeDtypeStruct(state.shape, jnp.float32),
            jax.ShapeDtypeStruct(queries.shape, queries.dtype),
            jax.ShapeDtypeStruct(lq.shape, jnp.bfloat16),
        ),
        in_specs=[vmem] * 10,
        out_specs=(vmem, vmem, vmem),
        scratch_shapes=[
            pltpu.VMEM(state.shape, jnp.float32),
            pltpu.VMEM((heads, columns), jnp.float32),
            pltpu.VMEM((heads, columns), jnp.float32),
            pltpu.VMEM(state.shape, jnp.float32),
            pltpu.VMEM((heads, columns), jnp.float32),
            pltpu.VMEM((stages,) + state.shape, jnp.bfloat16),
            pltpu.VMEM((stages, heads, columns), jnp.float32),
            pltpu.VMEM((stages,) + state.shape, jnp.bfloat16),
            pltpu.VMEM((stages, heads, columns), jnp.float32),
            pltpu.SemaphoreType.DMA((stages, chunks)),
            pltpu.SemaphoreType.DMA((stages, chunks)),
            pltpu.SemaphoreType.DMA((stages,)),
            pltpu.SemaphoreType.DMA((stages,)),
            pltpu.VMEM((REACH,) + kv.shape, kv.dtype),
            pltpu.SemaphoreType.DMA((REACH,)),
            pltpu.SemaphoreType.DMA((REACH,)),
            pltpu.VMEM((lax.axis_size("head"), 1, columns), jnp.float32),
            pltpu.SemaphoreType.DMA((lax.axis_size("head"),)),
            pltpu.SemaphoreType.DMA((lax.axis_size("head"),)),
        ],
        compiler_params=pltpu.CompilerParams(collective_id=0, has_side_effects=True),
    )(fall_rows, state, state.astype(jnp.bfloat16), kv, queries, bias, lq, local, grow, gain)


def head_sum_kernel(count, value_ref, out_ref, slots, send_sem, recv_sem):
    me = lax.axis_index("seq")
    head = lax.axis_index("head")
    barrier = pltpu.get_barrier_semaphore()
    for other in range(count):

        @pl.when(other != head)
        def _():
            pl.semaphore_signal(barrier, inc=1, device_id=(me, other), device_id_type=MESH)

    pl.semaphore_wait(barrier, count - 1)
    slots[head] = value_ref[...]

    def copy(other, slot):
        return pltpu.make_async_remote_copy(
            src_ref=value_ref,
            dst_ref=slots.at[slot],
            send_sem=send_sem.at[other],
            recv_sem=recv_sem.at[slot],
            device_id=(me, other),
            device_id_type=MESH,
        )

    for other in range(count):

        @pl.when(other != head)
        def _():
            copy(other, head).start()

    for other in range(count):

        @pl.when(other != head)
        def _():
            copy(other, other).wait_recv()
            copy(other, head).wait_send()

    total = slots[0]
    for other in range(1, count):
        total = total + slots[other]
    out_ref[...] = total


def head_sum(value, axis):
    count = lax.axis_size(axis)
    vmem = pl.BlockSpec(memory_space=pltpu.VMEM)
    row = value.reshape(1, -1)
    return pl.pallas_call(
        functools.partial(head_sum_kernel, count),
        out_shape=jax.ShapeDtypeStruct(row.shape, row.dtype),
        in_specs=[vmem],
        out_specs=vmem,
        scratch_shapes=[
            pltpu.VMEM((count,) + row.shape, row.dtype),
            pltpu.SemaphoreType.DMA((count,)),
            pltpu.SemaphoreType.DMA((count,)),
        ],
        compiler_params=pltpu.CompilerParams(collective_id=1, has_side_effects=True),
    )(row).reshape(value.shape)


def from_behind(value, axis, steps):
    count = lax.axis_size(axis)
    first, last = (max(0, -steps), min(count, count - steps))
    return lax.ppermute(value, axis, [(source, source + steps) for source in range(first, last)])


def combine_states(earlier, later):
    return (earlier[0] * later[0], later[0][:, None, None] * earlier[1] + later[1])


def split_parts(matrix):
    upper = matrix.astype(jnp.bfloat16)
    lower = (matrix - upper.astype(jnp.float32)).astype(jnp.bfloat16)
    return (upper, lower)


def attend(carried_over_state, query_rows, key_rows, value_rows, visible, score_scale):
    running_max, running_sum, accumulated = carried_over_state
    attention_logits = (
        jnp.einsum("cphm,npm->phcn", query_rows, key_rows, preferred_element_type=jnp.float32)
        * score_scale
    )
    masked = jnp.where(visible, attention_logits, -jnp.inf)
    new_max = jnp.maximum(running_max, jnp.max(masked, axis=-1))
    power_exponent = jnp.exp(masked - new_max[..., None])
    fading = jnp.exp(running_max - new_max)
    new_sum = running_sum * fading + jnp.sum(power_exponent, axis=-1)
    product = jnp.einsum(
        "qyjl,lqu->qyju",
        power_exponent.astype(jnp.bfloat16),
        value_rows,
        preferred_element_type=jnp.float32,
    )
    return (new_max, new_sum, accumulated * fading[..., None] + product)


def body(
    linear_query_rows,
    lin_keys,
    linear_value_rows,
    log_decay,
    norm_gain,
    soft_queries,
    soft_keys,
    soft_values,
    window_start,
):
    row_count, heads_here, head_width = linear_query_rows.shape
    cumulated = jnp.cumsum(log_decay, axis=1)
    token_locations = jnp.arange(row_count, dtype=jnp.int32)
    lower_mask = token_locations[:, None] >= token_locations[None, :]
    tail = jnp.exp(cumulated[:, -1:] - cumulated)
    key_product = lin_keys.astype(jnp.float32) * tail.T[:, :, None]
    key_product_upper, key_product_lower = split_parts(key_product)
    recurrent_state = jnp.einsum(
        "egz,egc->gzc", key_product_upper, linear_value_rows, preferred_element_type=jnp.float32
    )
    recurrent_state = recurrent_state + jnp.einsum(
        "egz,egc->gzc", key_product_lower, linear_value_rows, preferred_element_type=jnp.float32
    )
    falling = jnp.exp(cumulated[:, -1])
    kv_here = soft_keys.shape[1]
    group = heads_here // kv_here
    block_index = lax.axis_index("seq")
    key_index = jnp.arange((REACH + 1) * row_count, dtype=jnp.int32)
    key_block = block_index - REACH + key_index // row_count
    causal = (key_index % row_count)[None, :] <= token_locations[:, None]
    visible = ((key_block[None, :] < block_index) | causal) & (key_block[None, :] >= window_start[0])
    lin_scores = jnp.einsum(
        "thd,shd->hts", linear_query_rows, lin_keys, preferred_element_type=jnp.float32
    )
    gap = jnp.where(lower_mask[None], cumulated[:, :, None] - cumulated[:, None, :], -jnp.inf)
    lin_weights = (lin_scores * jnp.exp(gap)).astype(jnp.bfloat16)
    local_part = jnp.einsum(
        "hts,shd->htd", lin_weights, linear_value_rows, preferred_element_type=jnp.float32
    )
    normed, soft_out, lin_out = exclusive_scan(
        falling,
        recurrent_state,
        jnp.stack([soft_keys, soft_values]).transpose(0, 2, 1, 3),
        soft_queries.reshape(row_count, kv_here, group, head_width),
        jnp.where(visible, 0.0, -jnp.inf).astype(jnp.float32),
        linear_query_rows.transpose(1, 0, 2),
        local_part,
        jnp.exp(cumulated),
        norm_gain,
        "seq",
    )
    lin_out = lin_out.transpose(1, 0, 2)
    soft_out = soft_out.reshape(row_count, heads_here, head_width)
    return (lin_out, soft_out)


def solution(mesh):
    placed = (
        P("seq", "head", None),
        P("seq", "head", None),
        P("seq", "head", None),
        P("head", "seq"),
        P("head", None),
        P("seq", "head", None),
        P("seq", "head", None),
        P("seq", "head", None),
        P("seq"),
    )
    return jax.shard_map(
        body,
        mesh=mesh,
        in_specs=placed,
        out_specs=(P("seq", "head", None), P("seq", "head", None)),
        check_vma=False,
    )
```

```python
import functools

import jax
import jax.numpy as jnp
from jax import lax
from jax.experimental import pallas as pl
from jax.experimental.pallas import tpu as pltpu
from jax.sharding import PartitionSpec as P

MESH = pl.DeviceIdType.MESH

DH = 128
HEADS = 64
REACH = 3


def scan_kernel(
    rounds,
    chunks,
    reach,
    fall_ref,
    state_ref,
    sent0_ref,
    kv_ref,
    q_ref,
    bias_ref,
    lq_ref,
    local_ref,
    grow_ref,
    gain_ref,
    out_ref,
    soft_ref,
    lin_ref,
    whole,
    whole_fall,
    out_fall,
    suffix,
    suffix_fall,
    got,
    got_fall,
    outgoing,
    outgoing_fall,
    send_sem,
    recv_sem,
    fsend_sem,
    frecv_sem,
    kv_got,
    kv_send,
    kv_recv,
    head_slots,
    head_send,
    head_recv,
):
    me = lax.axis_index("seq")
    head = lax.axis_index("head")
    length = 2**rounds
    width = state_ref.shape[0] // chunks
    jump = 7
    back0, back1, near = rounds, rounds + 1, rounds + 2

    def ahead(dist):
        return 1 - (me + dist) // length

    def behind(dist):
        return (me - dist + length) // length

    far_recv = behind(jump)
    near_recv = behind(4) * (1 - far_recv)
    near_send = 1 - (me + length - 3) // length

    barrier = pltpu.get_barrier_semaphore()
    partners = 0
    distances = [2**k for k in range(rounds)] + list(range(1, reach + 1)) + [jump]
    for dist in sorted(set(distances)):
        partners = partners + ahead(dist) + behind(dist)

        @pl.when(ahead(dist) == 1)
        def _():
            pl.semaphore_signal(barrier, inc=1, device_id=(me + dist, head), device_id_type=MESH)

        @pl.when(behind(dist) == 1)
        def _():
            pl.semaphore_signal(barrier, inc=1, device_id=(me - dist, head), device_id_type=MESH)

    head_count = head_slots.shape[0]
    for other in range(head_count):

        @pl.when(other != head)
        def _():
            pl.semaphore_signal(barrier, inc=1, device_id=(me, other), device_id_type=MESH)

    pl.semaphore_wait(barrier, partners + head_count - 1)

    def kv_copy(dist, device):
        return pltpu.make_async_remote_copy(
            src_ref=kv_ref,
            dst_ref=kv_got.at[dist - 1],
            send_sem=kv_send.at[dist - 1],
            recv_sem=kv_recv.at[dist - 1],
            device_id=(device, head),
            device_id_type=MESH,
        )

    for dist in range(1, reach + 1):

        @pl.when(ahead(dist) == 1)
        def _():
            kv_copy(dist, me + dist).start()

    def state_copy(stage, source, c, device):
        rows = pl.ds(c * width, width)
        return pltpu.make_async_remote_copy(
            src_ref=source.at[rows],
            dst_ref=got.at[stage, rows],
            send_sem=send_sem.at[stage, c],
            recv_sem=recv_sem.at[stage, c],
            device_id=(device, head),
            device_id_type=MESH,
        )

    def fall_copy(stage, source, device):
        return pltpu.make_async_remote_copy(
            src_ref=source,
            dst_ref=got_fall.at[stage],
            send_sem=fsend_sem.at[stage],
            recv_sem=frecv_sem.at[stage],
            device_id=(device, head),
            device_id_type=MESH,
        )

    fall = jnp.broadcast_to(fall_ref[...], whole_fall.shape)
    outgoing_fall[0] = fall

    @pl.when(ahead(1) == 1)
    def _():
        fall_copy(0, outgoing_fall.at[0], me + 1).start()
        for c in range(chunks):
            state_copy(0, sent0_ref, c, me + 1).start()

    @pl.when(behind(1) == 1)
    def _():
        fall_copy(back0, outgoing_fall.at[0], me - 1).start()
        for c in range(chunks):
            state_copy(back0, sent0_ref, c, me - 1).start()

    whole[...] = state_ref[...]
    whole_fall[...] = fall
    suffix[...] = state_ref[...]
    suffix_fall[...] = fall
    out_ref[...] = jnp.zeros_like(out_ref)
    out_fall[...] = jnp.ones_like(out_fall)

    def forward_fall(stage, shift):
        @pl.when(behind(shift) == 1)
        def _():
            fall_copy(stage, outgoing_fall.at[stage], me - shift).wait_recv()
            arrived = got_fall[stage]
            out_fall[...] = arrived * out_fall[...]
            whole_fall[...] = arrived * whole_fall[...]

    def forward_chunk(stage, shift, c, update_whole=True):
        rows = pl.ds(c * width, width)

        @pl.when(behind(shift) == 1)
        def _():
            state_copy(stage, outgoing.at[stage], c, me - shift).wait_recv()
            arrived = got[stage, rows].astype(jnp.float32)
            out_ref[rows] = out_fall[rows][:, None, :] * arrived + out_ref[rows]
            if update_whole:
                whole[rows] = whole_fall[rows][:, None, :] * arrived + whole[rows]

    def backward_fall(stage, shift):
        @pl.when(ahead(shift) == 1)
        def _():
            fall_copy(stage, outgoing_fall.at[stage], me + shift).wait_recv()
            suffix_fall[...] = suffix_fall[...] * got_fall[stage]

    def backward_chunk(stage, shift, c):
        rows = pl.ds(c * width, width)

        @pl.when(ahead(shift) == 1)
        def _():
            state_copy(stage, outgoing.at[stage], c, me + shift).wait_recv()
            arrived = got[stage, rows].astype(jnp.float32)
            suffix[rows] = got_fall[stage][rows][:, None, :] * suffix[rows] + arrived

    def send_chunk(stage, flag, buffer, dist, c):
        rows = pl.ds(c * width, width)

        @pl.when(flag == 1)
        def _():
            outgoing[stage, rows] = buffer[rows].astype(jnp.bfloat16)
            state_copy(stage, outgoing.at[stage], c, me + dist).start()

    def send_fall(stage, flag, buffer_fall, dist):
        @pl.when(flag == 1)
        def _():
            outgoing_fall[stage] = buffer_fall[...]
            fall_copy(stage, outgoing_fall.at[stage], me + dist).start()

    backward_fall(back0, 1)
    send_fall(back1, behind(2), suffix_fall, -2)
    for c in range(chunks):
        forward_chunk(0, 1, c)
        send_chunk(1, ahead(2), whole, 2, c)
        backward_chunk(back0, 1, c)
        send_chunk(back1, behind(2), suffix, -2, c)
    forward_fall(0, 1)
    send_fall(1, ahead(2), whole_fall, 2)

    backward_fall(back1, 2)
    send_fall(2, ahead(jump), suffix_fall, jump)
    for c in range(chunks):
        forward_chunk(1, 2, c)
        send_chunk(near, near_send, whole, 4, c)
        backward_chunk(back1, 2, c)
        send_chunk(2, ahead(jump), suffix, jump, c)
    forward_fall(1, 2)
    send_fall(near, near_send, whole_fall, 4)

    for c in range(chunks):
        rows = pl.ds(c * width, width)
        for flag, dist, stage in ((far_recv, jump, 2), (near_recv, 4, near)):

            @pl.when(flag == 1)
            def _():
                state_copy(stage, outgoing.at[stage], c, me - dist).wait_recv()
                arrived = got[stage, rows].astype(jnp.float32)
                out_ref[rows] = out_fall[rows][:, None, :] * arrived + out_ref[rows]
                whole[rows] = whole_fall[rows][:, None, :] * arrived + whole[rows]

        if rounds > 3:
            send_chunk(3, ahead(8), whole, 8, c)

    for flag, dist, stage in ((far_recv, jump, 2), (near_recv, 4, near)):

        @pl.when(flag == 1)
        def _():
            fall_copy(stage, outgoing_fall.at[stage], me - dist).wait_recv()
            arrived = got_fall[stage]
            out_fall[...] = arrived * out_fall[...]
            whole_fall[...] = arrived * whole_fall[...]

    if rounds > 3:
        send_fall(3, ahead(8), whole_fall, 8)

    def attention():
        for dist in range(1, reach + 1):

            @pl.when(behind(dist) == 1)
            def _():
                kv_copy(dist, me - dist).wait_recv()

            @pl.when(behind(dist) == 0)
            def _():
                kv_got[dist - 1] = jnp.zeros_like(kv_got.at[dist - 1])

            @pl.when(ahead(dist) == 1)
            def _():
                kv_copy(dist, me + dist).wait_send()

        tokens, groups, group = q_ref.shape[0], q_ref.shape[1], q_ref.shape[2]
        scale = float(q_ref.shape[3]) ** (-0.5)
        for g in range(groups):
            q = q_ref[:, g].astype(jnp.float32).reshape(tokens * group, -1).astype(jnp.bfloat16)
            keys = [kv_got[slot, 0, g] for slot in range(reach - 1, -1, -1)] + [kv_ref[0, g]]
            values = [kv_got[slot, 1, g] for slot in range(reach - 1, -1, -1)] + [kv_ref[1, g]]
            logits = jnp.concatenate(
                [
                    lax.dot_general(q, k, (((1,), (1,)), ((), ())), preferred_element_type=jnp.float32)
                    for k in keys
                ],
                axis=1,
            )
            masked = (logits * scale).reshape(tokens, group, -1) + bias_ref[...][:, None, :]
            top = jnp.max(masked, axis=-1, keepdims=True)
            exps = jnp.exp(masked - top)
            total = jnp.sum(exps, axis=-1, keepdims=True)
            probs = exps.reshape(tokens * group, -1).astype(jnp.bfloat16)
            summed = jnp.dot(probs, jnp.concatenate(values, axis=0), preferred_element_type=jnp.float32)
            soft_ref[:, g] = (summed.reshape(tokens, group, -1) / total).astype(soft_ref.dtype)

    for k in range(3, rounds):
        shift, last = 2**k, k == rounds - 1
        if last:
            attention()
        for c in range(chunks):
            forward_chunk(k, shift, c, update_whole=not last)
            if not last:
                rows = pl.ds(c * width, width)

                @pl.when(ahead(2 * shift) == 1)
                def _():
                    outgoing[k + 1, rows] = whole[rows].astype(jnp.bfloat16)
                    state_copy(k + 1, outgoing.at[k + 1], c, me + 2 * shift).start()

        @pl.when(behind(shift) == 1)
        def _():
            fall_copy(k, outgoing_fall.at[k], me - shift).wait_recv()
            arrived = got_fall[k]
            out_fall[...] = arrived * out_fall[...]
            if not last:
                whole_fall[...] = arrived * whole_fall[...]

        if not last:

            @pl.when(ahead(2 * shift) == 1)
            def _():
                outgoing_fall[k + 1] = whole_fall[...]
                fall_copy(k + 1, outgoing_fall.at[k + 1], me + 2 * shift).start()

    sends = [(0, 1, ahead(1)), (back0, -1, behind(1)), (1, 2, ahead(2)), (back1, -2, behind(2))]
    sends += [(2, jump, ahead(jump)), (near, 4, near_send)]
    sends += [(k, 2**k, ahead(2**k)) for k in range(3, rounds)]
    for stage, dist, flag in sends:

        @pl.when(flag == 1)
        def _():
            fall_copy(stage, outgoing_fall.at[stage], me + dist).wait_send()
            for c in range(chunks):
                state_copy(stage, outgoing.at[stage], c, me + dist).wait_send()

    prior = out_ref[...]
    upper = prior.astype(jnp.bfloat16)
    lower = (prior - upper.astype(jnp.float32)).astype(jnp.bfloat16)
    queries = lq_ref[...]
    carried = jnp.einsum("hti,hij->htj", queries, upper, preferred_element_type=jnp.float32)
    carried = carried + jnp.einsum("hti,hij->htj", queries, lower, preferred_element_type=jnp.float32)
    grow = jnp.transpose(grow_ref[...])
    mixed = local_ref[...] + jnp.stack([grow[:, h : h + 1] for h in range(grow.shape[1])]) * carried
    column = jnp.sum(jnp.sum(mixed * mixed, axis=0), axis=1, keepdims=True)
    head_slots[head] = jnp.transpose(jnp.broadcast_to(column, (column.shape[0], 128)))[0:1, :]

    def head_copy(other, slot):
        return pltpu.make_async_remote_copy(
            src_ref=head_slots.at[head],
            dst_ref=head_slots.at[slot],
            send_sem=head_send.at[other],
            recv_sem=head_recv.at[slot],
            device_id=(me, other),
            device_id_type=MESH,
        )

    for other in range(head_count):

        @pl.when(other != head)
        def _():
            head_copy(other, head).start()

    for other in range(head_count):

        @pl.when(other != head)
        def _():
            head_copy(other, other).wait_recv()
            head_copy(other, head).wait_send()

    total = head_slots[0]
    for other in range(1, head_count):
        total = total + head_slots[other]
    heads_all, width_all = lq_ref.shape[0] * head_count, lq_ref.shape[2]
    scale_row = lax.rsqrt(total / (heads_all * width_all) + 1e-06)
    scale = jnp.transpose(jnp.broadcast_to(scale_row, (128, scale_row.shape[1])))[:, 0:1]
    gain = gain_ref[...].astype(jnp.float32)
    lin_ref[...] = (mixed * scale[None] * gain[:, None, :]).astype(lin_ref.dtype)


def exclusive_scan(falling, state, kv, queries, bias, lq, local, grow, gain, axis):
    length = lax.axis_size(axis)
    rounds = length.bit_length() - 1
    stages = rounds + 3
    chunks = 8
    heads, rows, columns = state.shape
    fall_rows = falling[:, None]
    vmem = pl.BlockSpec(memory_space=pltpu.VMEM)
    return pl.pallas_call(
        functools.partial(scan_kernel, rounds, chunks, REACH),
        out_shape=(
            jax.ShapeDtypeStruct(state.shape, jnp.float32),
            jax.ShapeDtypeStruct(queries.shape, queries.dtype),
            jax.ShapeDtypeStruct(lq.shape, jnp.bfloat16),
        ),
        in_specs=[vmem] * 10,
        out_specs=(vmem, vmem, vmem),
        scratch_shapes=[
            pltpu.VMEM(state.shape, jnp.float32),
            pltpu.VMEM((heads, columns), jnp.float32),
            pltpu.VMEM((heads, columns), jnp.float32),
            pltpu.VMEM(state.shape, jnp.float32),
            pltpu.VMEM((heads, columns), jnp.float32),
            pltpu.VMEM((stages,) + state.shape, jnp.bfloat16),
            pltpu.VMEM((stages, heads, columns), jnp.float32),
            pltpu.VMEM((stages,) + state.shape, jnp.bfloat16),
            pltpu.VMEM((stages, heads, columns), jnp.float32),
            pltpu.SemaphoreType.DMA((stages, chunks)),
            pltpu.SemaphoreType.DMA((stages, chunks)),
            pltpu.SemaphoreType.DMA((stages,)),
            pltpu.SemaphoreType.DMA((stages,)),
            pltpu.VMEM((REACH,) + kv.shape, kv.dtype),
            pltpu.SemaphoreType.DMA((REACH,)),
            pltpu.SemaphoreType.DMA((REACH,)),
            pltpu.VMEM((lax.axis_size("head"), 1, columns), jnp.float32),
            pltpu.SemaphoreType.DMA((lax.axis_size("head"),)),
            pltpu.SemaphoreType.DMA((lax.axis_size("head"),)),
        ],
        compiler_params=pltpu.CompilerParams(collective_id=0, has_side_effects=True),
    )(fall_rows, state, state.astype(jnp.bfloat16), kv, queries, bias, lq, local, grow, gain)


def head_sum_kernel(count, value_ref, out_ref, slots, send_sem, recv_sem):
    me = lax.axis_index("seq")
    head = lax.axis_index("head")
    barrier = pltpu.get_barrier_semaphore()
    for other in range(count):

        @pl.when(other != head)
        def _():
            pl.semaphore_signal(barrier, inc=1, device_id=(me, other), device_id_type=MESH)

    pl.semaphore_wait(barrier, count - 1)
    slots[head] = value_ref[...]

    def copy(other, slot):
        return pltpu.make_async_remote_copy(
            src_ref=value_ref,
            dst_ref=slots.at[slot],
            send_sem=send_sem.at[other],
            recv_sem=recv_sem.at[slot],
            device_id=(me, other),
            device_id_type=MESH,
        )

    for other in range(count):

        @pl.when(other != head)
        def _():
            copy(other, head).start()

    for other in range(count):

        @pl.when(other != head)
        def _():
            copy(other, other).wait_recv()
            copy(other, head).wait_send()

    total = slots[0]
    for other in range(1, count):
        total = total + slots[other]
    out_ref[...] = total


def head_sum(value, axis):
    count = lax.axis_size(axis)
    vmem = pl.BlockSpec(memory_space=pltpu.VMEM)
    row = value.reshape(1, -1)
    return pl.pallas_call(
        functools.partial(head_sum_kernel, count),
        out_shape=jax.ShapeDtypeStruct(row.shape, row.dtype),
        in_specs=[vmem],
        out_specs=vmem,
        scratch_shapes=[
            pltpu.VMEM((count,) + row.shape, row.dtype),
            pltpu.SemaphoreType.DMA((count,)),
            pltpu.SemaphoreType.DMA((count,)),
        ],
        compiler_params=pltpu.CompilerParams(collective_id=1, has_side_effects=True),
    )(row).reshape(value.shape)


def from_behind(value, axis, steps):
    count = lax.axis_size(axis)
    first, last = (max(0, -steps), min(count, count - steps))
    return lax.ppermute(value, axis, [(source, source + steps) for source in range(first, last)])


def combine_states(earlier, later):
    return (earlier[0] * later[0], later[0][:, None, None] * earlier[1] + later[1])


def split_parts(matrix):
    upper = matrix.astype(jnp.bfloat16)
    lower = (matrix - upper.astype(jnp.float32)).astype(jnp.bfloat16)
    return (upper, lower)


def attend(carried_over_state, query_rows, key_rows, value_rows, visible, score_scale):
    running_max, running_sum, accumulated = carried_over_state
    attention_logits = (
        jnp.einsum("cphm,npm->phcn", query_rows, key_rows, preferred_element_type=jnp.float32)
        * score_scale
    )
    masked = jnp.where(visible, attention_logits, -jnp.inf)
    new_max = jnp.maximum(running_max, jnp.max(masked, axis=-1))
    power_exponent = jnp.exp(masked - new_max[..., None])
    fading = jnp.exp(running_max - new_max)
    new_sum = running_sum * fading + jnp.sum(power_exponent, axis=-1)
    product = jnp.einsum(
        "qyjl,lqu->qyju",
        power_exponent.astype(jnp.bfloat16),
        value_rows,
        preferred_element_type=jnp.float32,
    )
    return (new_max, new_sum, accumulated * fading[..., None] + product)


def body(
    linear_query_rows,
    lin_keys,
    linear_value_rows,
    log_decay,
    norm_gain,
    soft_queries,
    soft_keys,
    soft_values,
    window_start,
):
    row_count, heads_here, head_width = linear_query_rows.shape
    cumulated = jnp.cumsum(log_decay, axis=1)
    token_locations = jnp.arange(row_count, dtype=jnp.int32)
    lower_mask = token_locations[:, None] >= token_locations[None, :]
    tail = jnp.exp(cumulated[:, -1:] - cumulated)
    key_product = lin_keys.astype(jnp.float32) * tail.T[:, :, None]
    key_product_upper, key_product_lower = split_parts(key_product)
    recurrent_state = jnp.einsum(
        "egz,egc->gzc", key_product_upper, linear_value_rows, preferred_element_type=jnp.float32
    )
    recurrent_state = recurrent_state + jnp.einsum(
        "egz,egc->gzc", key_product_lower, linear_value_rows, preferred_element_type=jnp.float32
    )
    falling = jnp.exp(cumulated[:, -1])
    kv_here = soft_keys.shape[1]
    group = heads_here // kv_here
    block_index = lax.axis_index("seq")
    key_index = jnp.arange((REACH + 1) * row_count, dtype=jnp.int32)
    key_block = block_index - REACH + key_index // row_count
    causal = (key_index % row_count)[None, :] <= token_locations[:, None]
    visible = ((key_block[None, :] < block_index) | causal) & (key_block[None, :] >= window_start[0])
    lin_scores = jnp.einsum(
        "thd,shd->hts", linear_query_rows, lin_keys, preferred_element_type=jnp.float32
    )
    gap = jnp.where(lower_mask[None], cumulated[:, :, None] - cumulated[:, None, :], -jnp.inf)
    lin_weights = (lin_scores * jnp.exp(gap)).astype(jnp.bfloat16)
    local_part = jnp.einsum(
        "hts,shd->htd", lin_weights, linear_value_rows, preferred_element_type=jnp.float32
    )
    normed, soft_out, lin_out = exclusive_scan(
        falling,
        recurrent_state,
        jnp.stack([soft_keys, soft_values]).transpose(0, 2, 1, 3),
        soft_queries.reshape(row_count, kv_here, group, head_width),
        jnp.where(visible, 0.0, -jnp.inf).astype(jnp.float32),
        linear_query_rows.transpose(1, 0, 2),
        local_part,
        jnp.exp(cumulated),
        norm_gain,
        "seq",
    )
    lin_out = lin_out.transpose(1, 0, 2)
    soft_out = soft_out.reshape(row_count, heads_here, head_width)
    return (lin_out, soft_out)


def solution(mesh):
    placed = (
        P("seq", "head", None),
        P("seq", "head", None),
        P("seq", "head", None),
        P("head", "seq"),
        P("head", None),
        P("seq", "head", None),
        P("seq", "head", None),
        P("seq", "head", None),
        P("seq"),
    )
    return jax.shard_map(
        body,
        mesh=mesh,
        in_specs=placed,
        out_specs=(P("seq", "head", None), P("seq", "head", None)),
        check_vma=False,
    )
```

```python
import functools

import jax
import jax.numpy as jnp
from jax import lax
from jax.experimental import pallas as pl
from jax.experimental.pallas import tpu as pltpu
from jax.sharding import PartitionSpec as P

MESH = pl.DeviceIdType.MESH

DH = 128
HEADS = 64
REACH = 3


def scan_kernel(
    rounds,
    chunks,
    reach,
    fall_ref,
    state_ref,
    sent0_ref,
    kv_ref,
    q_ref,
    bias_ref,
    lq_ref,
    local_ref,
    grow_ref,
    gain_ref,
    out_ref,
    soft_ref,
    lin_ref,
    whole,
    whole_fall,
    out_fall,
    suffix,
    suffix_fall,
    got,
    got_fall,
    outgoing,
    outgoing_fall,
    send_sem,
    recv_sem,
    fsend_sem,
    frecv_sem,
    kv_got,
    kv_send,
    kv_recv,
    head_slots,
    head_send,
    head_recv,
):
    me = lax.axis_index("seq")
    head = lax.axis_index("head")
    length = 2**rounds
    width = state_ref.shape[0] // chunks
    jump = 7
    back0, back1, near = rounds, rounds + 1, rounds + 2

    def ahead(dist):
        return 1 - (me + dist) // length

    def behind(dist):
        return (me - dist + length) // length

    far_recv = behind(jump)
    near_recv = behind(4) * (1 - far_recv)
    near_send = 1 - (me + length - 3) // length

    barrier = pltpu.get_barrier_semaphore()
    partners = 0
    distances = [2**k for k in range(rounds)] + list(range(1, reach + 1)) + [jump]
    for dist in sorted(set(distances)):
        partners = partners + ahead(dist) + behind(dist)

        @pl.when(ahead(dist) == 1)
        def _():
            pl.semaphore_signal(barrier, inc=1, device_id=(me + dist, head), device_id_type=MESH)

        @pl.when(behind(dist) == 1)
        def _():
            pl.semaphore_signal(barrier, inc=1, device_id=(me - dist, head), device_id_type=MESH)

    head_count = head_slots.shape[0]
    for other in range(head_count):

        @pl.when(other != head)
        def _():
            pl.semaphore_signal(barrier, inc=1, device_id=(me, other), device_id_type=MESH)

    pl.semaphore_wait(barrier, partners + head_count - 1)

    def kv_copy(dist, device):
        return pltpu.make_async_remote_copy(
            src_ref=kv_ref,
            dst_ref=kv_got.at[dist - 1],
            send_sem=kv_send.at[dist - 1],
            recv_sem=kv_recv.at[dist - 1],
            device_id=(device, head),
            device_id_type=MESH,
        )

    for dist in range(1, reach + 1):

        @pl.when(ahead(dist) == 1)
        def _():
            kv_copy(dist, me + dist).start()

    def state_copy(stage, source, c, device):
        rows = pl.ds(c * width, width)
        return pltpu.make_async_remote_copy(
            src_ref=source.at[rows],
            dst_ref=got.at[stage, rows],
            send_sem=send_sem.at[stage, c],
            recv_sem=recv_sem.at[stage, c],
            device_id=(device, head),
            device_id_type=MESH,
        )

    def fall_copy(stage, source, device):
        return pltpu.make_async_remote_copy(
            src_ref=source,
            dst_ref=got_fall.at[stage],
            send_sem=fsend_sem.at[stage],
            recv_sem=frecv_sem.at[stage],
            device_id=(device, head),
            device_id_type=MESH,
        )

    fall = jnp.broadcast_to(fall_ref[...], whole_fall.shape)
    outgoing_fall[0] = fall

    @pl.when(ahead(1) == 1)
    def _():
        fall_copy(0, outgoing_fall.at[0], me + 1).start()
        for c in range(chunks):
            state_copy(0, sent0_ref, c, me + 1).start()

    @pl.when(behind(1) == 1)
    def _():
        fall_copy(back0, outgoing_fall.at[0], me - 1).start()
        for c in range(chunks):
            state_copy(back0, sent0_ref, c, me - 1).start()

    whole[...] = state_ref[...]
    whole_fall[...] = fall
    suffix[...] = state_ref[...]
    suffix_fall[...] = fall
    out_ref[...] = jnp.zeros_like(out_ref)
    out_fall[...] = jnp.ones_like(out_fall)

    def forward_fall(stage, shift):
        @pl.when(behind(shift) == 1)
        def _():
            fall_copy(stage, outgoing_fall.at[stage], me - shift).wait_recv()
            arrived = got_fall[stage]
            out_fall[...] = arrived * out_fall[...]
            whole_fall[...] = arrived * whole_fall[...]

    def forward_chunk(stage, shift, c, update_whole=True):
        rows = pl.ds(c * width, width)

        @pl.when(behind(shift) == 1)
        def _():
            state_copy(stage, outgoing.at[stage], c, me - shift).wait_recv()
            arrived = got[stage, rows].astype(jnp.float32)
            out_ref[rows] = out_fall[rows][:, None, :] * arrived + out_ref[rows]
            if update_whole:
                whole[rows] = whole_fall[rows][:, None, :] * arrived + whole[rows]

    def backward_fall(stage, shift):
        @pl.when(ahead(shift) == 1)
        def _():
            fall_copy(stage, outgoing_fall.at[stage], me + shift).wait_recv()
            suffix_fall[...] = suffix_fall[...] * got_fall[stage]

    def backward_chunk(stage, shift, c):
        rows = pl.ds(c * width, width)

        @pl.when(ahead(shift) == 1)
        def _():
            state_copy(stage, outgoing.at[stage], c, me + shift).wait_recv()
            arrived = got[stage, rows].astype(jnp.float32)
            suffix[rows] = got_fall[stage][rows][:, None, :] * suffix[rows] + arrived

    def send_chunk(stage, flag, buffer, dist, c):
        rows = pl.ds(c * width, width)

        @pl.when(flag == 1)
        def _():
            outgoing[stage, rows] = buffer[rows].astype(jnp.bfloat16)
            state_copy(stage, outgoing.at[stage], c, me + dist).start()

    def send_fall(stage, flag, buffer_fall, dist):
        @pl.when(flag == 1)
        def _():
            outgoing_fall[stage] = buffer_fall[...]
            fall_copy(stage, outgoing_fall.at[stage], me + dist).start()

    backward_fall(back0, 1)
    send_fall(back1, behind(2), suffix_fall, -2)
    for c in range(chunks):
        forward_chunk(0, 1, c)
        send_chunk(1, ahead(2), whole, 2, c)
        backward_chunk(back0, 1, c)
        send_chunk(back1, behind(2), suffix, -2, c)
    forward_fall(0, 1)
    send_fall(1, ahead(2), whole_fall, 2)

    backward_fall(back1, 2)
    send_fall(2, ahead(jump), suffix_fall, jump)
    for c in range(chunks):
        forward_chunk(1, 2, c)
        send_chunk(near, near_send, whole, 4, c)
        backward_chunk(back1, 2, c)
        send_chunk(2, ahead(jump), suffix, jump, c)
    forward_fall(1, 2)
    send_fall(near, near_send, whole_fall, 4)

    for c in range(chunks):
        rows = pl.ds(c * width, width)
        for flag, dist, stage in ((far_recv, jump, 2), (near_recv, 4, near)):

            @pl.when(flag == 1)
            def _():
                state_copy(stage, outgoing.at[stage], c, me - dist).wait_recv()
                arrived = got[stage, rows].astype(jnp.float32)
                out_ref[rows] = out_fall[rows][:, None, :] * arrived + out_ref[rows]
                whole[rows] = whole_fall[rows][:, None, :] * arrived + whole[rows]

        if rounds > 3:
            send_chunk(3, ahead(8), whole, 8, c)

    for flag, dist, stage in ((far_recv, jump, 2), (near_recv, 4, near)):

        @pl.when(flag == 1)
        def _():
            fall_copy(stage, outgoing_fall.at[stage], me - dist).wait_recv()
            arrived = got_fall[stage]
            out_fall[...] = arrived * out_fall[...]
            whole_fall[...] = arrived * whole_fall[...]

    if rounds > 3:
        send_fall(3, ahead(8), whole_fall, 8)

    def attention():
        for dist in range(1, reach + 1):

            @pl.when(behind(dist) == 1)
            def _():
                kv_copy(dist, me - dist).wait_recv()

            @pl.when(behind(dist) == 0)
            def _():
                kv_got[dist - 1] = jnp.zeros_like(kv_got.at[dist - 1])

            @pl.when(ahead(dist) == 1)
            def _():
                kv_copy(dist, me + dist).wait_send()

        tokens, groups, group = q_ref.shape[0], q_ref.shape[1], q_ref.shape[2]
        scale = float(q_ref.shape[3]) ** (-0.5)
        for g in range(groups):
            q = q_ref[:, g].astype(jnp.float32).reshape(tokens * group, -1).astype(jnp.bfloat16)
            keys = [kv_got[slot, 0, g] for slot in range(reach - 1, -1, -1)] + [kv_ref[0, g]]
            values = [kv_got[slot, 1, g] for slot in range(reach - 1, -1, -1)] + [kv_ref[1, g]]
            logits = jnp.concatenate(
                [
                    lax.dot_general(q, k, (((1,), (1,)), ((), ())), preferred_element_type=jnp.float32)
                    for k in keys
                ],
                axis=1,
            )
            masked = (logits * scale).reshape(tokens, group, -1) + bias_ref[...][:, None, :]
            top = jnp.max(masked, axis=-1, keepdims=True)
            exps = jnp.exp(masked - top)
            total = jnp.sum(exps, axis=-1, keepdims=True)
            probs = exps.reshape(tokens * group, -1).astype(jnp.bfloat16)
            summed = jnp.dot(probs, jnp.concatenate(values, axis=0), preferred_element_type=jnp.float32)
            soft_ref[:, g] = (summed.reshape(tokens, group, -1) / total).astype(soft_ref.dtype)

    for k in range(3, rounds):
        shift, last = 2**k, k == rounds - 1
        if last:
            attention()
        for c in range(chunks):
            forward_chunk(k, shift, c, update_whole=not last)
            if not last:
                rows = pl.ds(c * width, width)

                @pl.when(ahead(2 * shift) == 1)
                def _():
                    outgoing[k + 1, rows] = whole[rows].astype(jnp.bfloat16)
                    state_copy(k + 1, outgoing.at[k + 1], c, me + 2 * shift).start()

        @pl.when(behind(shift) == 1)
        def _():
            fall_copy(k, outgoing_fall.at[k], me - shift).wait_recv()
            arrived = got_fall[k]
            out_fall[...] = arrived * out_fall[...]
            if not last:
                whole_fall[...] = arrived * whole_fall[...]

        if not last:

            @pl.when(ahead(2 * shift) == 1)
            def _():
                outgoing_fall[k + 1] = whole_fall[...]
                fall_copy(k + 1, outgoing_fall.at[k + 1], me + 2 * shift).start()

    sends = [(0, 1, ahead(1)), (back0, -1, behind(1)), (1, 2, ahead(2)), (back1, -2, behind(2))]
    sends += [(2, jump, ahead(jump)), (near, 4, near_send)]
    sends += [(k, 2**k, ahead(2**k)) for k in range(3, rounds)]
    for stage, dist, flag in sends:

        @pl.when(flag == 1)
        def _():
            fall_copy(stage, outgoing_fall.at[stage], me + dist).wait_send()
            for c in range(chunks):
                state_copy(stage, outgoing.at[stage], c, me + dist).wait_send()

    prior = out_ref[...]
    upper = prior.astype(jnp.bfloat16)
    lower = (prior - upper.astype(jnp.float32)).astype(jnp.bfloat16)
    parts = []
    for h in range(prior.shape[0]):
        query = lq_ref[:, h, :]
        part = jnp.dot(query, upper[h], preferred_element_type=jnp.float32)
        parts.append(part + jnp.dot(query, lower[h], preferred_element_type=jnp.float32))
    carried = jnp.stack(parts)
    grow = jnp.transpose(grow_ref[...])
    mixed = local_ref[...] + jnp.stack([grow[:, h : h + 1] for h in range(grow.shape[1])]) * carried
    column = jnp.sum(jnp.sum(mixed * mixed, axis=0), axis=1, keepdims=True)
    head_slots[head] = jnp.transpose(jnp.broadcast_to(column, (column.shape[0], 128)))[0:1, :]

    def head_copy(other, slot):
        return pltpu.make_async_remote_copy(
            src_ref=head_slots.at[head],
            dst_ref=head_slots.at[slot],
            send_sem=head_send.at[other],
            recv_sem=head_recv.at[slot],
            device_id=(me, other),
            device_id_type=MESH,
        )

    for other in range(head_count):

        @pl.when(other != head)
        def _():
            head_copy(other, head).start()

    for other in range(head_count):

        @pl.when(other != head)
        def _():
            head_copy(other, other).wait_recv()
            head_copy(other, head).wait_send()

    total = head_slots[0]
    for other in range(1, head_count):
        total = total + head_slots[other]
    heads_all, width_all = lq_ref.shape[1] * head_count, lq_ref.shape[2]
    scale_row = lax.rsqrt(total / (heads_all * width_all) + 1e-06)
    scale = jnp.transpose(jnp.broadcast_to(scale_row, (128, scale_row.shape[1])))[:, 0:1]
    gain = gain_ref[...].astype(jnp.float32)
    lin_ref[...] = (mixed * scale[None] * gain[:, None, :]).astype(lin_ref.dtype)


def exclusive_scan(falling, state, kv, queries, bias, lq, local, grow, gain, axis):
    length = lax.axis_size(axis)
    rounds = length.bit_length() - 1
    stages = rounds + 3
    chunks = 8
    heads, rows, columns = state.shape
    fall_rows = falling[:, None]
    vmem = pl.BlockSpec(memory_space=pltpu.VMEM)
    return pl.pallas_call(
        functools.partial(scan_kernel, rounds, chunks, REACH),
        out_shape=(
            jax.ShapeDtypeStruct(state.shape, jnp.float32),
            jax.ShapeDtypeStruct(queries.shape, queries.dtype),
            jax.ShapeDtypeStruct(state.shape, jnp.bfloat16),
        ),
        in_specs=[vmem] * 10,
        out_specs=(vmem, vmem, vmem),
        scratch_shapes=[
            pltpu.VMEM(state.shape, jnp.float32),
            pltpu.VMEM((heads, columns), jnp.float32),
            pltpu.VMEM((heads, columns), jnp.float32),
            pltpu.VMEM(state.shape, jnp.float32),
            pltpu.VMEM((heads, columns), jnp.float32),
            pltpu.VMEM((stages,) + state.shape, jnp.bfloat16),
            pltpu.VMEM((stages, heads, columns), jnp.float32),
            pltpu.VMEM((stages,) + state.shape, jnp.bfloat16),
            pltpu.VMEM((stages, heads, columns), jnp.float32),
            pltpu.SemaphoreType.DMA((stages, chunks)),
            pltpu.SemaphoreType.DMA((stages, chunks)),
            pltpu.SemaphoreType.DMA((stages,)),
            pltpu.SemaphoreType.DMA((stages,)),
            pltpu.VMEM((REACH,) + kv.shape, kv.dtype),
            pltpu.SemaphoreType.DMA((REACH,)),
            pltpu.SemaphoreType.DMA((REACH,)),
            pltpu.VMEM((lax.axis_size("head"), 1, columns), jnp.float32),
            pltpu.SemaphoreType.DMA((lax.axis_size("head"),)),
            pltpu.SemaphoreType.DMA((lax.axis_size("head"),)),
        ],
        compiler_params=pltpu.CompilerParams(collective_id=0, has_side_effects=True),
    )(fall_rows, state, state.astype(jnp.bfloat16), kv, queries, bias, lq, local, grow, gain)


def head_sum_kernel(count, value_ref, out_ref, slots, send_sem, recv_sem):
    me = lax.axis_index("seq")
    head = lax.axis_index("head")
    barrier = pltpu.get_barrier_semaphore()
    for other in range(count):

        @pl.when(other != head)
        def _():
            pl.semaphore_signal(barrier, inc=1, device_id=(me, other), device_id_type=MESH)

    pl.semaphore_wait(barrier, count - 1)
    slots[head] = value_ref[...]

    def copy(other, slot):
        return pltpu.make_async_remote_copy(
            src_ref=value_ref,
            dst_ref=slots.at[slot],
            send_sem=send_sem.at[other],
            recv_sem=recv_sem.at[slot],
            device_id=(me, other),
            device_id_type=MESH,
        )

    for other in range(count):

        @pl.when(other != head)
        def _():
            copy(other, head).start()

    for other in range(count):

        @pl.when(other != head)
        def _():
            copy(other, other).wait_recv()
            copy(other, head).wait_send()

    total = slots[0]
    for other in range(1, count):
        total = total + slots[other]
    out_ref[...] = total


def head_sum(value, axis):
    count = lax.axis_size(axis)
    vmem = pl.BlockSpec(memory_space=pltpu.VMEM)
    row = value.reshape(1, -1)
    return pl.pallas_call(
        functools.partial(head_sum_kernel, count),
        out_shape=jax.ShapeDtypeStruct(row.shape, row.dtype),
        in_specs=[vmem],
        out_specs=vmem,
        scratch_shapes=[
            pltpu.VMEM((count,) + row.shape, row.dtype),
            pltpu.SemaphoreType.DMA((count,)),
            pltpu.SemaphoreType.DMA((count,)),
        ],
        compiler_params=pltpu.CompilerParams(collective_id=1, has_side_effects=True),
    )(row).reshape(value.shape)


def from_behind(value, axis, steps):
    count = lax.axis_size(axis)
    first, last = (max(0, -steps), min(count, count - steps))
    return lax.ppermute(value, axis, [(source, source + steps) for source in range(first, last)])


def combine_states(earlier, later):
    return (earlier[0] * later[0], later[0][:, None, None] * earlier[1] + later[1])


def split_parts(matrix):
    upper = matrix.astype(jnp.bfloat16)
    lower = (matrix - upper.astype(jnp.float32)).astype(jnp.bfloat16)
    return (upper, lower)


def attend(carried_over_state, query_rows, key_rows, value_rows, visible, score_scale):
    running_max, running_sum, accumulated = carried_over_state
    attention_logits = (
        jnp.einsum("cphm,npm->phcn", query_rows, key_rows, preferred_element_type=jnp.float32)
        * score_scale
    )
    masked = jnp.where(visible, attention_logits, -jnp.inf)
    new_max = jnp.maximum(running_max, jnp.max(masked, axis=-1))
    power_exponent = jnp.exp(masked - new_max[..., None])
    fading = jnp.exp(running_max - new_max)
    new_sum = running_sum * fading + jnp.sum(power_exponent, axis=-1)
    product = jnp.einsum(
        "qyjl,lqu->qyju",
        power_exponent.astype(jnp.bfloat16),
        value_rows,
        preferred_element_type=jnp.float32,
    )
    return (new_max, new_sum, accumulated * fading[..., None] + product)


def body(
    linear_query_rows,
    lin_keys,
    linear_value_rows,
    log_decay,
    norm_gain,
    soft_queries,
    soft_keys,
    soft_values,
    window_start,
):
    row_count, heads_here, head_width = linear_query_rows.shape
    cumulated = jnp.cumsum(log_decay, axis=1)
    token_locations = jnp.arange(row_count, dtype=jnp.int32)
    lower_mask = token_locations[:, None] >= token_locations[None, :]
    tail = jnp.exp(cumulated[:, -1:] - cumulated)
    key_product = lin_keys.astype(jnp.float32) * tail.T[:, :, None]
    key_product_upper, key_product_lower = split_parts(key_product)
    recurrent_state = jnp.einsum(
        "egz,egc->gzc", key_product_upper, linear_value_rows, preferred_element_type=jnp.float32
    )
    recurrent_state = recurrent_state + jnp.einsum(
        "egz,egc->gzc", key_product_lower, linear_value_rows, preferred_element_type=jnp.float32
    )
    falling = jnp.exp(cumulated[:, -1])
    kv_here = soft_keys.shape[1]
    group = heads_here // kv_here
    block_index = lax.axis_index("seq")
    key_index = jnp.arange((REACH + 1) * row_count, dtype=jnp.int32)
    key_block = block_index - REACH + key_index // row_count
    causal = (key_index % row_count)[None, :] <= token_locations[:, None]
    visible = ((key_block[None, :] < block_index) | causal) & (key_block[None, :] >= window_start[0])
    lin_scores = jnp.einsum(
        "thd,shd->hts", linear_query_rows, lin_keys, preferred_element_type=jnp.float32
    )
    gap = jnp.where(lower_mask[None], cumulated[:, :, None] - cumulated[:, None, :], -jnp.inf)
    lin_weights = (lin_scores * jnp.exp(gap)).astype(jnp.bfloat16)
    local_part = jnp.einsum(
        "hts,shd->htd", lin_weights, linear_value_rows, preferred_element_type=jnp.float32
    )
    normed, soft_out, lin_out = exclusive_scan(
        falling,
        recurrent_state,
        jnp.stack([soft_keys, soft_values]).transpose(0, 2, 1, 3),
        soft_queries.reshape(row_count, kv_here, group, head_width),
        jnp.where(visible, 0.0, -jnp.inf).astype(jnp.float32),
        linear_query_rows,
        local_part,
        jnp.exp(cumulated),
        norm_gain,
        "seq",
    )
    lin_out = lin_out.transpose(1, 0, 2)
    soft_out = soft_out.reshape(row_count, heads_here, head_width)
    return (lin_out, soft_out)


def solution(mesh):
    placed = (
        P("seq", "head", None),
        P("seq", "head", None),
        P("seq", "head", None),
        P("head", "seq"),
        P("head", None),
        P("seq", "head", None),
        P("seq", "head", None),
        P("seq", "head", None),
        P("seq"),
    )
    return jax.shard_map(
        body,
        mesh=mesh,
        in_specs=placed,
        out_specs=(P("seq", "head", None), P("seq", "head", None)),
        check_vma=False,
    )
```

```python
import functools

import jax
import jax.numpy as jnp
from jax import lax
from jax.experimental import pallas as pl
from jax.experimental.pallas import tpu as pltpu
from jax.sharding import PartitionSpec as P

MESH = pl.DeviceIdType.MESH

DH = 128
HEADS = 64
REACH = 3


def scan_kernel(
    rounds,
    chunks,
    reach,
    fall_ref,
    state_ref,
    sent0_ref,
    kv_ref,
    q_ref,
    bias_ref,
    lq_ref,
    lk_ref,
    lv_ref,
    cum_ref,
    grow_ref,
    gain_ref,
    out_ref,
    soft_ref,
    lin_ref,
    whole,
    whole_fall,
    out_fall,
    suffix,
    suffix_fall,
    got,
    got_fall,
    outgoing,
    outgoing_fall,
    send_sem,
    recv_sem,
    fsend_sem,
    frecv_sem,
    kv_got,
    kv_send,
    kv_recv,
    head_slots,
    head_send,
    head_recv,
    local_ref,
):
    me = lax.axis_index("seq")
    head = lax.axis_index("head")
    length = 2**rounds
    width = state_ref.shape[0] // chunks
    jump = 7
    back0, back1, near = rounds, rounds + 1, rounds + 2

    def ahead(dist):
        return 1 - (me + dist) // length

    def behind(dist):
        return (me - dist + length) // length

    far_recv = behind(jump)
    near_recv = behind(4) * (1 - far_recv)
    near_send = 1 - (me + length - 3) // length

    barrier = pltpu.get_barrier_semaphore()
    partners = 0
    distances = [2**k for k in range(rounds)] + list(range(1, reach + 1)) + [jump]
    for dist in sorted(set(distances)):
        partners = partners + ahead(dist) + behind(dist)

        @pl.when(ahead(dist) == 1)
        def _():
            pl.semaphore_signal(barrier, inc=1, device_id=(me + dist, head), device_id_type=MESH)

        @pl.when(behind(dist) == 1)
        def _():
            pl.semaphore_signal(barrier, inc=1, device_id=(me - dist, head), device_id_type=MESH)

    head_count = head_slots.shape[0]
    for other in range(head_count):

        @pl.when(other != head)
        def _():
            pl.semaphore_signal(barrier, inc=1, device_id=(me, other), device_id_type=MESH)

    pl.semaphore_wait(barrier, partners + head_count - 1)

    def kv_copy(dist, device):
        return pltpu.make_async_remote_copy(
            src_ref=kv_ref,
            dst_ref=kv_got.at[dist - 1],
            send_sem=kv_send.at[dist - 1],
            recv_sem=kv_recv.at[dist - 1],
            device_id=(device, head),
            device_id_type=MESH,
        )

    for dist in range(1, reach + 1):

        @pl.when(ahead(dist) == 1)
        def _():
            kv_copy(dist, me + dist).start()

    def state_copy(stage, source, c, device):
        rows = pl.ds(c * width, width)
        return pltpu.make_async_remote_copy(
            src_ref=source.at[rows],
            dst_ref=got.at[stage, rows],
            send_sem=send_sem.at[stage, c],
            recv_sem=recv_sem.at[stage, c],
            device_id=(device, head),
            device_id_type=MESH,
        )

    def fall_copy(stage, source, device):
        return pltpu.make_async_remote_copy(
            src_ref=source,
            dst_ref=got_fall.at[stage],
            send_sem=fsend_sem.at[stage],
            recv_sem=frecv_sem.at[stage],
            device_id=(device, head),
            device_id_type=MESH,
        )

    fall = jnp.broadcast_to(fall_ref[...], whole_fall.shape)
    outgoing_fall[0] = fall

    @pl.when(ahead(1) == 1)
    def _():
        fall_copy(0, outgoing_fall.at[0], me + 1).start()
        for c in range(chunks):
            state_copy(0, sent0_ref, c, me + 1).start()

    @pl.when(behind(1) == 1)
    def _():
        fall_copy(back0, outgoing_fall.at[0], me - 1).start()
        for c in range(chunks):
            state_copy(back0, sent0_ref, c, me - 1).start()

    whole[...] = state_ref[...]
    whole_fall[...] = fall
    suffix[...] = state_ref[...]
    suffix_fall[...] = fall
    out_ref[...] = jnp.zeros_like(out_ref)
    out_fall[...] = jnp.ones_like(out_fall)

    def forward_fall(stage, shift):
        @pl.when(behind(shift) == 1)
        def _():
            fall_copy(stage, outgoing_fall.at[stage], me - shift).wait_recv()
            arrived = got_fall[stage]
            out_fall[...] = arrived * out_fall[...]
            whole_fall[...] = arrived * whole_fall[...]

    def forward_chunk(stage, shift, c, update_whole=True):
        rows = pl.ds(c * width, width)

        @pl.when(behind(shift) == 1)
        def _():
            state_copy(stage, outgoing.at[stage], c, me - shift).wait_recv()
            arrived = got[stage, rows].astype(jnp.float32)
            out_ref[rows] = out_fall[rows][:, None, :] * arrived + out_ref[rows]
            if update_whole:
                whole[rows] = whole_fall[rows][:, None, :] * arrived + whole[rows]

    def backward_fall(stage, shift):
        @pl.when(ahead(shift) == 1)
        def _():
            fall_copy(stage, outgoing_fall.at[stage], me + shift).wait_recv()
            suffix_fall[...] = suffix_fall[...] * got_fall[stage]

    def backward_chunk(stage, shift, c):
        rows = pl.ds(c * width, width)

        @pl.when(ahead(shift) == 1)
        def _():
            state_copy(stage, outgoing.at[stage], c, me + shift).wait_recv()
            arrived = got[stage, rows].astype(jnp.float32)
            suffix[rows] = got_fall[stage][rows][:, None, :] * suffix[rows] + arrived

    def send_chunk(stage, flag, buffer, dist, c):
        rows = pl.ds(c * width, width)

        @pl.when(flag == 1)
        def _():
            outgoing[stage, rows] = buffer[rows].astype(jnp.bfloat16)
            state_copy(stage, outgoing.at[stage], c, me + dist).start()

    def send_fall(stage, flag, buffer_fall, dist):
        @pl.when(flag == 1)
        def _():
            outgoing_fall[stage] = buffer_fall[...]
            fall_copy(stage, outgoing_fall.at[stage], me + dist).start()

    backward_fall(back0, 1)
    send_fall(back1, behind(2), suffix_fall, -2)
    for c in range(chunks):
        forward_chunk(0, 1, c)
        send_chunk(1, ahead(2), whole, 2, c)
        backward_chunk(back0, 1, c)
        send_chunk(back1, behind(2), suffix, -2, c)
    forward_fall(0, 1)
    send_fall(1, ahead(2), whole_fall, 2)

    backward_fall(back1, 2)
    send_fall(2, ahead(jump), suffix_fall, jump)
    for c in range(chunks):
        forward_chunk(1, 2, c)
        send_chunk(near, near_send, whole, 4, c)
        backward_chunk(back1, 2, c)
        send_chunk(2, ahead(jump), suffix, jump, c)
    forward_fall(1, 2)
    send_fall(near, near_send, whole_fall, 4)

    for c in range(chunks):
        rows = pl.ds(c * width, width)
        for flag, dist, stage in ((far_recv, jump, 2), (near_recv, 4, near)):

            @pl.when(flag == 1)
            def _():
                state_copy(stage, outgoing.at[stage], c, me - dist).wait_recv()
                arrived = got[stage, rows].astype(jnp.float32)
                out_ref[rows] = out_fall[rows][:, None, :] * arrived + out_ref[rows]
                whole[rows] = whole_fall[rows][:, None, :] * arrived + whole[rows]

        if rounds > 3:
            send_chunk(3, ahead(8), whole, 8, c)

    for flag, dist, stage in ((far_recv, jump, 2), (near_recv, 4, near)):

        @pl.when(flag == 1)
        def _():
            fall_copy(stage, outgoing_fall.at[stage], me - dist).wait_recv()
            arrived = got_fall[stage]
            out_fall[...] = arrived * out_fall[...]
            whole_fall[...] = arrived * whole_fall[...]

    if rounds > 3:
        send_fall(3, ahead(8), whole_fall, 8)

    def local_part():
        cum = cum_ref[...]
        cum_col = jnp.transpose(cum)
        tokens = cum.shape[1]
        rows_at = lax.broadcasted_iota(jnp.int32, (tokens, tokens), 0)
        cols_at = lax.broadcasted_iota(jnp.int32, (tokens, tokens), 1)
        for h in range(cum.shape[0]):
            scores = lax.dot_general(
                lq_ref[:, h, :], lk_ref[:, h, :], (((1,), (1,)), ((), ())), preferred_element_type=jnp.float32
            )
            gap = jnp.where(rows_at >= cols_at, cum_col[:, h : h + 1] - cum[h : h + 1, :], -jnp.inf)
            weights = (scores * jnp.exp(gap)).astype(jnp.bfloat16)
            local_ref[h] = jnp.dot(weights, lv_ref[:, h, :], preferred_element_type=jnp.float32)

    def attention():
        for dist in range(1, reach + 1):

            @pl.when(behind(dist) == 1)
            def _():
                kv_copy(dist, me - dist).wait_recv()

            @pl.when(behind(dist) == 0)
            def _():
                kv_got[dist - 1] = jnp.zeros_like(kv_got.at[dist - 1])

            @pl.when(ahead(dist) == 1)
            def _():
                kv_copy(dist, me + dist).wait_send()

        tokens, groups, group = q_ref.shape[0], q_ref.shape[1], q_ref.shape[2]
        scale = float(q_ref.shape[3]) ** (-0.5)
        for g in range(groups):
            q = q_ref[:, g].astype(jnp.float32).reshape(tokens * group, -1).astype(jnp.bfloat16)
            keys = [kv_got[slot, 0, g] for slot in range(reach - 1, -1, -1)] + [kv_ref[0, g]]
            values = [kv_got[slot, 1, g] for slot in range(reach - 1, -1, -1)] + [kv_ref[1, g]]
            logits = jnp.concatenate(
                [
                    lax.dot_general(q, k, (((1,), (1,)), ((), ())), preferred_element_type=jnp.float32)
                    for k in keys
                ],
                axis=1,
            )
            masked = (logits * scale).reshape(tokens, group, -1) + bias_ref[...][:, None, :]
            top = jnp.max(masked, axis=-1, keepdims=True)
            exps = jnp.exp(masked - top)
            total = jnp.sum(exps, axis=-1, keepdims=True)
            probs = exps.reshape(tokens * group, -1).astype(jnp.bfloat16)
            summed = jnp.dot(probs, jnp.concatenate(values, axis=0), preferred_element_type=jnp.float32)
            soft_ref[:, g] = (summed.reshape(tokens, group, -1) / total).astype(soft_ref.dtype)

    for k in range(3, rounds):
        shift, last = 2**k, k == rounds - 1
        if last:
            attention()
            local_part()
        for c in range(chunks):
            forward_chunk(k, shift, c, update_whole=not last)
            if not last:
                rows = pl.ds(c * width, width)

                @pl.when(ahead(2 * shift) == 1)
                def _():
                    outgoing[k + 1, rows] = whole[rows].astype(jnp.bfloat16)
                    state_copy(k + 1, outgoing.at[k + 1], c, me + 2 * shift).start()

        @pl.when(behind(shift) == 1)
        def _():
            fall_copy(k, outgoing_fall.at[k], me - shift).wait_recv()
            arrived = got_fall[k]
            out_fall[...] = arrived * out_fall[...]
            if not last:
                whole_fall[...] = arrived * whole_fall[...]

        if not last:

            @pl.when(ahead(2 * shift) == 1)
            def _():
                outgoing_fall[k + 1] = whole_fall[...]
                fall_copy(k + 1, outgoing_fall.at[k + 1], me + 2 * shift).start()

    sends = [(0, 1, ahead(1)), (back0, -1, behind(1)), (1, 2, ahead(2)), (back1, -2, behind(2))]
    sends += [(2, jump, ahead(jump)), (near, 4, near_send)]
    sends += [(k, 2**k, ahead(2**k)) for k in range(3, rounds)]
    for stage, dist, flag in sends:

        @pl.when(flag == 1)
        def _():
            fall_copy(stage, outgoing_fall.at[stage], me + dist).wait_send()
            for c in range(chunks):
                state_copy(stage, outgoing.at[stage], c, me + dist).wait_send()

    prior = out_ref[...]
    upper = prior.astype(jnp.bfloat16)
    lower = (prior - upper.astype(jnp.float32)).astype(jnp.bfloat16)
    parts = []
    for h in range(prior.shape[0]):
        query = lq_ref[:, h, :]
        part = jnp.dot(query, upper[h], preferred_element_type=jnp.float32)
        parts.append(part + jnp.dot(query, lower[h], preferred_element_type=jnp.float32))
    carried = jnp.stack(parts)
    grow = jnp.transpose(grow_ref[...])
    mixed = local_ref[...] + jnp.stack([grow[:, h : h + 1] for h in range(grow.shape[1])]) * carried
    column = jnp.sum(jnp.sum(mixed * mixed, axis=0), axis=1, keepdims=True)
    head_slots[head] = jnp.transpose(jnp.broadcast_to(column, (column.shape[0], 128)))[0:1, :]

    def head_copy(other, slot):
        return pltpu.make_async_remote_copy(
            src_ref=head_slots.at[head],
            dst_ref=head_slots.at[slot],
            send_sem=head_send.at[other],
            recv_sem=head_recv.at[slot],
            device_id=(me, other),
            device_id_type=MESH,
        )

    for other in range(head_count):

        @pl.when(other != head)
        def _():
            head_copy(other, head).start()

    for other in range(head_count):

        @pl.when(other != head)
        def _():
            head_copy(other, other).wait_recv()
            head_copy(other, head).wait_send()

    total = head_slots[0]
    for other in range(1, head_count):
        total = total + head_slots[other]
    heads_all, width_all = lq_ref.shape[1] * head_count, lq_ref.shape[2]
    scale_row = lax.rsqrt(total / (heads_all * width_all) + 1e-06)
    scale = jnp.transpose(jnp.broadcast_to(scale_row, (128, scale_row.shape[1])))[:, 0:1]
    gain = gain_ref[...].astype(jnp.float32)
    lin_ref[...] = (mixed * scale[None] * gain[:, None, :]).astype(lin_ref.dtype)


def exclusive_scan(falling, state, kv, queries, bias, lq, lk, lv, cum, grow, gain, axis):
    length = lax.axis_size(axis)
    rounds = length.bit_length() - 1
    stages = rounds + 3
    chunks = 8
    heads, rows, columns = state.shape
    fall_rows = falling[:, None]
    vmem = pl.BlockSpec(memory_space=pltpu.VMEM)
    return pl.pallas_call(
        functools.partial(scan_kernel, rounds, chunks, REACH),
        out_shape=(
            jax.ShapeDtypeStruct(state.shape, jnp.float32),
            jax.ShapeDtypeStruct(queries.shape, queries.dtype),
            jax.ShapeDtypeStruct(state.shape, jnp.bfloat16),
        ),
        in_specs=[vmem] * 12,
        out_specs=(vmem, vmem, vmem),
        scratch_shapes=[
            pltpu.VMEM(state.shape, jnp.float32),
            pltpu.VMEM((heads, columns), jnp.float32),
            pltpu.VMEM((heads, columns), jnp.float32),
            pltpu.VMEM(state.shape, jnp.float32),
            pltpu.VMEM((heads, columns), jnp.float32),
            pltpu.VMEM((stages,) + state.shape, jnp.bfloat16),
            pltpu.VMEM((stages, heads, columns), jnp.float32),
            pltpu.VMEM((stages,) + state.shape, jnp.bfloat16),
            pltpu.VMEM((stages, heads, columns), jnp.float32),
            pltpu.SemaphoreType.DMA((stages, chunks)),
            pltpu.SemaphoreType.DMA((stages, chunks)),
            pltpu.SemaphoreType.DMA((stages,)),
            pltpu.SemaphoreType.DMA((stages,)),
            pltpu.VMEM((REACH,) + kv.shape, kv.dtype),
            pltpu.SemaphoreType.DMA((REACH,)),
            pltpu.SemaphoreType.DMA((REACH,)),
            pltpu.VMEM((lax.axis_size("head"), 1, columns), jnp.float32),
            pltpu.SemaphoreType.DMA((lax.axis_size("head"),)),
            pltpu.SemaphoreType.DMA((lax.axis_size("head"),)),
            pltpu.VMEM(state.shape, jnp.float32),
        ],
        compiler_params=pltpu.CompilerParams(collective_id=0, has_side_effects=True),
    )(fall_rows, state, state.astype(jnp.bfloat16), kv, queries, bias, lq, lk, lv, cum, grow, gain)


def head_sum_kernel(count, value_ref, out_ref, slots, send_sem, recv_sem):
    me = lax.axis_index("seq")
    head = lax.axis_index("head")
    barrier = pltpu.get_barrier_semaphore()
    for other in range(count):

        @pl.when(other != head)
        def _():
            pl.semaphore_signal(barrier, inc=1, device_id=(me, other), device_id_type=MESH)

    pl.semaphore_wait(barrier, count - 1)
    slots[head] = value_ref[...]

    def copy(other, slot):
        return pltpu.make_async_remote_copy(
            src_ref=value_ref,
            dst_ref=slots.at[slot],
            send_sem=send_sem.at[other],
            recv_sem=recv_sem.at[slot],
            device_id=(me, other),
            device_id_type=MESH,
        )

    for other in range(count):

        @pl.when(other != head)
        def _():
            copy(other, head).start()

    for other in range(count):

        @pl.when(other != head)
        def _():
            copy(other, other).wait_recv()
            copy(other, head).wait_send()

    total = slots[0]
    for other in range(1, count):
        total = total + slots[other]
    out_ref[...] = total


def head_sum(value, axis):
    count = lax.axis_size(axis)
    vmem = pl.BlockSpec(memory_space=pltpu.VMEM)
    row = value.reshape(1, -1)
    return pl.pallas_call(
        functools.partial(head_sum_kernel, count),
        out_shape=jax.ShapeDtypeStruct(row.shape, row.dtype),
        in_specs=[vmem],
        out_specs=vmem,
        scratch_shapes=[
            pltpu.VMEM((count,) + row.shape, row.dtype),
            pltpu.SemaphoreType.DMA((count,)),
            pltpu.SemaphoreType.DMA((count,)),
        ],
        compiler_params=pltpu.CompilerParams(collective_id=1, has_side_effects=True),
    )(row).reshape(value.shape)


def from_behind(value, axis, steps):
    count = lax.axis_size(axis)
    first, last = (max(0, -steps), min(count, count - steps))
    return lax.ppermute(value, axis, [(source, source + steps) for source in range(first, last)])


def combine_states(earlier, later):
    return (earlier[0] * later[0], later[0][:, None, None] * earlier[1] + later[1])


def split_parts(matrix):
    upper = matrix.astype(jnp.bfloat16)
    lower = (matrix - upper.astype(jnp.float32)).astype(jnp.bfloat16)
    return (upper, lower)


def attend(carried_over_state, query_rows, key_rows, value_rows, visible, score_scale):
    running_max, running_sum, accumulated = carried_over_state
    attention_logits = (
        jnp.einsum("cphm,npm->phcn", query_rows, key_rows, preferred_element_type=jnp.float32)
        * score_scale
    )
    masked = jnp.where(visible, attention_logits, -jnp.inf)
    new_max = jnp.maximum(running_max, jnp.max(masked, axis=-1))
    power_exponent = jnp.exp(masked - new_max[..., None])
    fading = jnp.exp(running_max - new_max)
    new_sum = running_sum * fading + jnp.sum(power_exponent, axis=-1)
    product = jnp.einsum(
        "qyjl,lqu->qyju",
        power_exponent.astype(jnp.bfloat16),
        value_rows,
        preferred_element_type=jnp.float32,
    )
    return (new_max, new_sum, accumulated * fading[..., None] + product)


def body(
    linear_query_rows,
    lin_keys,
    linear_value_rows,
    log_decay,
    norm_gain,
    soft_queries,
    soft_keys,
    soft_values,
    window_start,
):
    row_count, heads_here, head_width = linear_query_rows.shape
    cumulated = jnp.cumsum(log_decay, axis=1)
    token_locations = jnp.arange(row_count, dtype=jnp.int32)
    lower_mask = token_locations[:, None] >= token_locations[None, :]
    tail = jnp.exp(cumulated[:, -1:] - cumulated)
    key_product = lin_keys.astype(jnp.float32) * tail.T[:, :, None]
    key_product_upper, key_product_lower = split_parts(key_product)
    recurrent_state = jnp.einsum(
        "egz,egc->gzc", key_product_upper, linear_value_rows, preferred_element_type=jnp.float32
    )
    recurrent_state = recurrent_state + jnp.einsum(
        "egz,egc->gzc", key_product_lower, linear_value_rows, preferred_element_type=jnp.float32
    )
    falling = jnp.exp(cumulated[:, -1])
    kv_here = soft_keys.shape[1]
    group = heads_here // kv_here
    block_index = lax.axis_index("seq")
    key_index = jnp.arange((REACH + 1) * row_count, dtype=jnp.int32)
    key_block = block_index - REACH + key_index // row_count
    causal = (key_index % row_count)[None, :] <= token_locations[:, None]
    visible = ((key_block[None, :] < block_index) | causal) & (key_block[None, :] >= window_start[0])
    normed, soft_out, lin_out = exclusive_scan(
        falling,
        recurrent_state,
        jnp.stack([soft_keys, soft_values]).transpose(0, 2, 1, 3),
        soft_queries.reshape(row_count, kv_here, group, head_width),
        jnp.where(visible, 0.0, -jnp.inf).astype(jnp.float32),
        linear_query_rows,
        lin_keys,
        linear_value_rows,
        cumulated,
        jnp.exp(cumulated),
        norm_gain,
        "seq",
    )
    lin_out = lin_out.transpose(1, 0, 2)
    soft_out = soft_out.reshape(row_count, heads_here, head_width)
    return (lin_out, soft_out)


def solution(mesh):
    placed = (
        P("seq", "head", None),
        P("seq", "head", None),
        P("seq", "head", None),
        P("head", "seq"),
        P("head", None),
        P("seq", "head", None),
        P("seq", "head", None),
        P("seq", "head", None),
        P("seq"),
    )
    return jax.shard_map(
        body,
        mesh=mesh,
        in_specs=placed,
        out_specs=(P("seq", "head", None), P("seq", "head", None)),
        check_vma=False,
    )
```

```python
import functools

import jax
import jax.numpy as jnp
from jax import lax
from jax.experimental import pallas as pl
from jax.experimental.pallas import tpu as pltpu
from jax.sharding import PartitionSpec as P

MESH = pl.DeviceIdType.MESH

DH = 128
HEADS = 64
REACH = 3


def scan_kernel(
    rounds,
    chunks,
    reach,
    fall_ref,
    state_ref,
    sent0_ref,
    kv_ref,
    q_ref,
    bias_ref,
    lq_ref,
    lk_ref,
    lv_ref,
    cum_ref,
    gain_ref,
    out_ref,
    soft_ref,
    lin_ref,
    whole,
    whole_fall,
    out_fall,
    suffix,
    suffix_fall,
    got,
    got_fall,
    outgoing,
    outgoing_fall,
    send_sem,
    recv_sem,
    fsend_sem,
    frecv_sem,
    kv_got,
    kv_send,
    kv_recv,
    head_slots,
    head_send,
    head_recv,
    local_ref,
):
    me = lax.axis_index("seq")
    head = lax.axis_index("head")
    length = 2**rounds
    width = state_ref.shape[0] // chunks
    jump = 7
    back0, back1, near = rounds, rounds + 1, rounds + 2

    def ahead(dist):
        return 1 - (me + dist) // length

    def behind(dist):
        return (me - dist + length) // length

    far_recv = behind(jump)
    near_recv = behind(4) * (1 - far_recv)
    near_send = 1 - (me + length - 3) // length

    barrier = pltpu.get_barrier_semaphore()
    partners = 0
    distances = [2**k for k in range(rounds)] + list(range(1, reach + 1)) + [jump]
    for dist in sorted(set(distances)):
        partners = partners + ahead(dist) + behind(dist)

        @pl.when(ahead(dist) == 1)
        def _():
            pl.semaphore_signal(barrier, inc=1, device_id=(me + dist, head), device_id_type=MESH)

        @pl.when(behind(dist) == 1)
        def _():
            pl.semaphore_signal(barrier, inc=1, device_id=(me - dist, head), device_id_type=MESH)

    head_count = head_slots.shape[0]
    for other in range(head_count):

        @pl.when(other != head)
        def _():
            pl.semaphore_signal(barrier, inc=1, device_id=(me, other), device_id_type=MESH)

    pl.semaphore_wait(barrier, partners + head_count - 1)

    def kv_copy(dist, device):
        return pltpu.make_async_remote_copy(
            src_ref=kv_ref,
            dst_ref=kv_got.at[dist - 1],
            send_sem=kv_send.at[dist - 1],
            recv_sem=kv_recv.at[dist - 1],
            device_id=(device, head),
            device_id_type=MESH,
        )

    for dist in range(1, reach + 1):

        @pl.when(ahead(dist) == 1)
        def _():
            kv_copy(dist, me + dist).start()

    def state_copy(stage, source, c, device):
        rows = pl.ds(c * width, width)
        return pltpu.make_async_remote_copy(
            src_ref=source.at[rows],
            dst_ref=got.at[stage, rows],
            send_sem=send_sem.at[stage, c],
            recv_sem=recv_sem.at[stage, c],
            device_id=(device, head),
            device_id_type=MESH,
        )

    def fall_copy(stage, source, device):
        return pltpu.make_async_remote_copy(
            src_ref=source,
            dst_ref=got_fall.at[stage],
            send_sem=fsend_sem.at[stage],
            recv_sem=frecv_sem.at[stage],
            device_id=(device, head),
            device_id_type=MESH,
        )

    fall = jnp.broadcast_to(fall_ref[...], whole_fall.shape)
    outgoing_fall[0] = fall

    @pl.when(ahead(1) == 1)
    def _():
        fall_copy(0, outgoing_fall.at[0], me + 1).start()
        for c in range(chunks):
            state_copy(0, sent0_ref, c, me + 1).start()

    @pl.when(behind(1) == 1)
    def _():
        fall_copy(back0, outgoing_fall.at[0], me - 1).start()
        for c in range(chunks):
            state_copy(back0, sent0_ref, c, me - 1).start()

    whole[...] = state_ref[...]
    whole_fall[...] = fall
    suffix[...] = state_ref[...]
    suffix_fall[...] = fall
    out_ref[...] = jnp.zeros_like(out_ref)
    out_fall[...] = jnp.ones_like(out_fall)

    def forward_fall(stage, shift):
        @pl.when(behind(shift) == 1)
        def _():
            fall_copy(stage, outgoing_fall.at[stage], me - shift).wait_recv()
            arrived = got_fall[stage]
            out_fall[...] = arrived * out_fall[...]
            whole_fall[...] = arrived * whole_fall[...]

    def forward_chunk(stage, shift, c, update_whole=True):
        rows = pl.ds(c * width, width)

        @pl.when(behind(shift) == 1)
        def _():
            state_copy(stage, outgoing.at[stage], c, me - shift).wait_recv()
            arrived = got[stage, rows].astype(jnp.float32)
            out_ref[rows] = out_fall[rows][:, None, :] * arrived + out_ref[rows]
            if update_whole:
                whole[rows] = whole_fall[rows][:, None, :] * arrived + whole[rows]

    def backward_fall(stage, shift):
        @pl.when(ahead(shift) == 1)
        def _():
            fall_copy(stage, outgoing_fall.at[stage], me + shift).wait_recv()
            suffix_fall[...] = suffix_fall[...] * got_fall[stage]

    def backward_chunk(stage, shift, c):
        rows = pl.ds(c * width, width)

        @pl.when(ahead(shift) == 1)
        def _():
            state_copy(stage, outgoing.at[stage], c, me + shift).wait_recv()
            arrived = got[stage, rows].astype(jnp.float32)
            suffix[rows] = got_fall[stage][rows][:, None, :] * suffix[rows] + arrived

    def send_chunk(stage, flag, buffer, dist, c):
        rows = pl.ds(c * width, width)

        @pl.when(flag == 1)
        def _():
            outgoing[stage, rows] = buffer[rows].astype(jnp.bfloat16)
            state_copy(stage, outgoing.at[stage], c, me + dist).start()

    def send_fall(stage, flag, buffer_fall, dist):
        @pl.when(flag == 1)
        def _():
            outgoing_fall[stage] = buffer_fall[...]
            fall_copy(stage, outgoing_fall.at[stage], me + dist).start()

    backward_fall(back0, 1)
    send_fall(back1, behind(2), suffix_fall, -2)
    for c in range(chunks):
        forward_chunk(0, 1, c)
        send_chunk(1, ahead(2), whole, 2, c)
        backward_chunk(back0, 1, c)
        send_chunk(back1, behind(2), suffix, -2, c)
    forward_fall(0, 1)
    send_fall(1, ahead(2), whole_fall, 2)

    backward_fall(back1, 2)
    send_fall(2, ahead(jump), suffix_fall, jump)
    for c in range(chunks):
        forward_chunk(1, 2, c)
        send_chunk(near, near_send, whole, 4, c)
        backward_chunk(back1, 2, c)
        send_chunk(2, ahead(jump), suffix, jump, c)
    forward_fall(1, 2)
    send_fall(near, near_send, whole_fall, 4)

    for c in range(chunks):
        rows = pl.ds(c * width, width)
        for flag, dist, stage in ((far_recv, jump, 2), (near_recv, 4, near)):

            @pl.when(flag == 1)
            def _():
                state_copy(stage, outgoing.at[stage], c, me - dist).wait_recv()
                arrived = got[stage, rows].astype(jnp.float32)
                out_ref[rows] = out_fall[rows][:, None, :] * arrived + out_ref[rows]
                whole[rows] = whole_fall[rows][:, None, :] * arrived + whole[rows]

        if rounds > 3:
            send_chunk(3, ahead(8), whole, 8, c)

    for flag, dist, stage in ((far_recv, jump, 2), (near_recv, 4, near)):

        @pl.when(flag == 1)
        def _():
            fall_copy(stage, outgoing_fall.at[stage], me - dist).wait_recv()
            arrived = got_fall[stage]
            out_fall[...] = arrived * out_fall[...]
            whole_fall[...] = arrived * whole_fall[...]

    if rounds > 3:
        send_fall(3, ahead(8), whole_fall, 8)

    def local_part():
        cum = cum_ref[...]
        cum_col = jnp.transpose(cum)
        tokens = cum.shape[1]
        rows_at = lax.broadcasted_iota(jnp.int32, (tokens, tokens), 0)
        cols_at = lax.broadcasted_iota(jnp.int32, (tokens, tokens), 1)
        for h in range(cum.shape[0]):
            scores = lax.dot_general(
                lq_ref[:, h, :], lk_ref[:, h, :], (((1,), (1,)), ((), ())), preferred_element_type=jnp.float32
            )
            gap = jnp.where(rows_at >= cols_at, cum_col[:, h : h + 1] - cum[h : h + 1, :], -jnp.inf)
            weights = (scores * jnp.exp(gap)).astype(jnp.bfloat16)
            local_ref[h] = jnp.dot(weights, lv_ref[:, h, :], preferred_element_type=jnp.float32)

    def attention():
        for dist in range(1, reach + 1):

            @pl.when(behind(dist) == 1)
            def _():
                kv_copy(dist, me - dist).wait_recv()

            @pl.when(behind(dist) == 0)
            def _():
                kv_got[dist - 1] = jnp.zeros_like(kv_got.at[dist - 1])

            @pl.when(ahead(dist) == 1)
            def _():
                kv_copy(dist, me + dist).wait_send()

        tokens, groups, group = q_ref.shape[0], q_ref.shape[1], q_ref.shape[2]
        scale = float(q_ref.shape[3]) ** (-0.5)
        for g in range(groups):
            q = q_ref[:, g].astype(jnp.float32).reshape(tokens * group, -1).astype(jnp.bfloat16)
            keys = [kv_got[slot, 0, g] for slot in range(reach - 1, -1, -1)] + [kv_ref[0, g]]
            values = [kv_got[slot, 1, g] for slot in range(reach - 1, -1, -1)] + [kv_ref[1, g]]
            logits = jnp.concatenate(
                [
                    lax.dot_general(q, k, (((1,), (1,)), ((), ())), preferred_element_type=jnp.float32)
                    for k in keys
                ],
                axis=1,
            )
            masked = (logits * scale).reshape(tokens, group, -1) + bias_ref[...][:, None, :]
            top = jnp.max(masked, axis=-1, keepdims=True)
            exps = jnp.exp(masked - top)
            total = jnp.sum(exps, axis=-1, keepdims=True)
            probs = exps.reshape(tokens * group, -1).astype(jnp.bfloat16)
            summed = jnp.dot(probs, jnp.concatenate(values, axis=0), preferred_element_type=jnp.float32)
            soft_ref[:, g] = (summed.reshape(tokens, group, -1) / total).astype(soft_ref.dtype)

    for k in range(3, rounds):
        shift, last = 2**k, k == rounds - 1
        if last:
            attention()
            local_part()
        for c in range(chunks):
            forward_chunk(k, shift, c, update_whole=not last)
            if not last:
                rows = pl.ds(c * width, width)

                @pl.when(ahead(2 * shift) == 1)
                def _():
                    outgoing[k + 1, rows] = whole[rows].astype(jnp.bfloat16)
                    state_copy(k + 1, outgoing.at[k + 1], c, me + 2 * shift).start()

        @pl.when(behind(shift) == 1)
        def _():
            fall_copy(k, outgoing_fall.at[k], me - shift).wait_recv()
            arrived = got_fall[k]
            out_fall[...] = arrived * out_fall[...]
            if not last:
                whole_fall[...] = arrived * whole_fall[...]

        if not last:

            @pl.when(ahead(2 * shift) == 1)
            def _():
                outgoing_fall[k + 1] = whole_fall[...]
                fall_copy(k + 1, outgoing_fall.at[k + 1], me + 2 * shift).start()

    sends = [(0, 1, ahead(1)), (back0, -1, behind(1)), (1, 2, ahead(2)), (back1, -2, behind(2))]
    sends += [(2, jump, ahead(jump)), (near, 4, near_send)]
    sends += [(k, 2**k, ahead(2**k)) for k in range(3, rounds)]
    for stage, dist, flag in sends:

        @pl.when(flag == 1)
        def _():
            fall_copy(stage, outgoing_fall.at[stage], me + dist).wait_send()
            for c in range(chunks):
                state_copy(stage, outgoing.at[stage], c, me + dist).wait_send()

    prior = out_ref[...]
    upper = prior.astype(jnp.bfloat16)
    lower = (prior - upper.astype(jnp.float32)).astype(jnp.bfloat16)
    parts = []
    for h in range(prior.shape[0]):
        query = lq_ref[:, h, :]
        part = jnp.dot(query, upper[h], preferred_element_type=jnp.float32)
        parts.append(part + jnp.dot(query, lower[h], preferred_element_type=jnp.float32))
    carried = jnp.stack(parts)
    grow = jnp.transpose(jnp.exp(cum_ref[...]))
    mixed = local_ref[...] + jnp.stack([grow[:, h : h + 1] for h in range(grow.shape[1])]) * carried
    column = jnp.sum(jnp.sum(mixed * mixed, axis=0), axis=1, keepdims=True)
    head_slots[head] = jnp.transpose(jnp.broadcast_to(column, (column.shape[0], 128)))[0:1, :]

    def head_copy(other, slot):
        return pltpu.make_async_remote_copy(
            src_ref=head_slots.at[head],
            dst_ref=head_slots.at[slot],
            send_sem=head_send.at[other],
            recv_sem=head_recv.at[slot],
            device_id=(me, other),
            device_id_type=MESH,
        )

    for other in range(head_count):

        @pl.when(other != head)
        def _():
            head_copy(other, head).start()

    for other in range(head_count):

        @pl.when(other != head)
        def _():
            head_copy(other, other).wait_recv()
            head_copy(other, head).wait_send()

    total = head_slots[0]
    for other in range(1, head_count):
        total = total + head_slots[other]
    heads_all, width_all = lq_ref.shape[1] * head_count, lq_ref.shape[2]
    scale_row = lax.rsqrt(total / (heads_all * width_all) + 1e-06)
    scale = jnp.transpose(jnp.broadcast_to(scale_row, (128, scale_row.shape[1])))[:, 0:1]
    gain = gain_ref[...].astype(jnp.float32)
    lin_ref[...] = (mixed * scale[None] * gain[:, None, :]).astype(lin_ref.dtype)


def exclusive_scan(falling, state, kv, queries, bias, lq, lk, lv, cum, gain, axis):
    length = lax.axis_size(axis)
    rounds = length.bit_length() - 1
    stages = rounds + 3
    chunks = 8
    heads, rows, columns = state.shape
    fall_rows = falling[:, None]
    vmem = pl.BlockSpec(memory_space=pltpu.VMEM)
    return pl.pallas_call(
        functools.partial(scan_kernel, rounds, chunks, REACH),
        out_shape=(
            jax.ShapeDtypeStruct(state.shape, jnp.float32),
            jax.ShapeDtypeStruct(queries.shape, queries.dtype),
            jax.ShapeDtypeStruct(state.shape, jnp.bfloat16),
        ),
        in_specs=[vmem] * 11,
        out_specs=(vmem, vmem, vmem),
        scratch_shapes=[
            pltpu.VMEM(state.shape, jnp.float32),
            pltpu.VMEM((heads, columns), jnp.float32),
            pltpu.VMEM((heads, columns), jnp.float32),
            pltpu.VMEM(state.shape, jnp.float32),
            pltpu.VMEM((heads, columns), jnp.float32),
            pltpu.VMEM((stages,) + state.shape, jnp.bfloat16),
            pltpu.VMEM((stages, heads, columns), jnp.float32),
            pltpu.VMEM((stages,) + state.shape, jnp.bfloat16),
            pltpu.VMEM((stages, heads, columns), jnp.float32),
            pltpu.SemaphoreType.DMA((stages, chunks)),
            pltpu.SemaphoreType.DMA((stages, chunks)),
            pltpu.SemaphoreType.DMA((stages,)),
            pltpu.SemaphoreType.DMA((stages,)),
            pltpu.VMEM((REACH,) + kv.shape, kv.dtype),
            pltpu.SemaphoreType.DMA((REACH,)),
            pltpu.SemaphoreType.DMA((REACH,)),
            pltpu.VMEM((lax.axis_size("head"), 1, columns), jnp.float32),
            pltpu.SemaphoreType.DMA((lax.axis_size("head"),)),
            pltpu.SemaphoreType.DMA((lax.axis_size("head"),)),
            pltpu.VMEM(state.shape, jnp.float32),
        ],
        compiler_params=pltpu.CompilerParams(collective_id=0, has_side_effects=True),
    )(fall_rows, state, state.astype(jnp.bfloat16), kv, queries, bias, lq, lk, lv, cum, gain)


def head_sum_kernel(count, value_ref, out_ref, slots, send_sem, recv_sem):
    me = lax.axis_index("seq")
    head = lax.axis_index("head")
    barrier = pltpu.get_barrier_semaphore()
    for other in range(count):

        @pl.when(other != head)
        def _():
            pl.semaphore_signal(barrier, inc=1, device_id=(me, other), device_id_type=MESH)

    pl.semaphore_wait(barrier, count - 1)
    slots[head] = value_ref[...]

    def copy(other, slot):
        return pltpu.make_async_remote_copy(
            src_ref=value_ref,
            dst_ref=slots.at[slot],
            send_sem=send_sem.at[other],
            recv_sem=recv_sem.at[slot],
            device_id=(me, other),
            device_id_type=MESH,
        )

    for other in range(count):

        @pl.when(other != head)
        def _():
            copy(other, head).start()

    for other in range(count):

        @pl.when(other != head)
        def _():
            copy(other, other).wait_recv()
            copy(other, head).wait_send()

    total = slots[0]
    for other in range(1, count):
        total = total + slots[other]
    out_ref[...] = total


def head_sum(value, axis):
    count = lax.axis_size(axis)
    vmem = pl.BlockSpec(memory_space=pltpu.VMEM)
    row = value.reshape(1, -1)
    return pl.pallas_call(
        functools.partial(head_sum_kernel, count),
        out_shape=jax.ShapeDtypeStruct(row.shape, row.dtype),
        in_specs=[vmem],
        out_specs=vmem,
        scratch_shapes=[
            pltpu.VMEM((count,) + row.shape, row.dtype),
            pltpu.SemaphoreType.DMA((count,)),
            pltpu.SemaphoreType.DMA((count,)),
        ],
        compiler_params=pltpu.CompilerParams(collective_id=1, has_side_effects=True),
    )(row).reshape(value.shape)


def from_behind(value, axis, steps):
    count = lax.axis_size(axis)
    first, last = (max(0, -steps), min(count, count - steps))
    return lax.ppermute(value, axis, [(source, source + steps) for source in range(first, last)])


def combine_states(earlier, later):
    return (earlier[0] * later[0], later[0][:, None, None] * earlier[1] + later[1])


def split_parts(matrix):
    upper = matrix.astype(jnp.bfloat16)
    lower = (matrix - upper.astype(jnp.float32)).astype(jnp.bfloat16)
    return (upper, lower)


def attend(carried_over_state, query_rows, key_rows, value_rows, visible, score_scale):
    running_max, running_sum, accumulated = carried_over_state
    attention_logits = (
        jnp.einsum("cphm,npm->phcn", query_rows, key_rows, preferred_element_type=jnp.float32)
        * score_scale
    )
    masked = jnp.where(visible, attention_logits, -jnp.inf)
    new_max = jnp.maximum(running_max, jnp.max(masked, axis=-1))
    power_exponent = jnp.exp(masked - new_max[..., None])
    fading = jnp.exp(running_max - new_max)
    new_sum = running_sum * fading + jnp.sum(power_exponent, axis=-1)
    product = jnp.einsum(
        "qyjl,lqu->qyju",
        power_exponent.astype(jnp.bfloat16),
        value_rows,
        preferred_element_type=jnp.float32,
    )
    return (new_max, new_sum, accumulated * fading[..., None] + product)


def body(
    linear_query_rows,
    lin_keys,
    linear_value_rows,
    log_decay,
    norm_gain,
    soft_queries,
    soft_keys,
    soft_values,
    window_start,
):
    row_count, heads_here, head_width = linear_query_rows.shape
    cumulated = jnp.cumsum(log_decay, axis=1)
    token_locations = jnp.arange(row_count, dtype=jnp.int32)
    lower_mask = token_locations[:, None] >= token_locations[None, :]
    tail = jnp.exp(cumulated[:, -1:] - cumulated)
    key_product = lin_keys.astype(jnp.float32) * tail.T[:, :, None]
    key_product_upper, key_product_lower = split_parts(key_product)
    recurrent_state = jnp.einsum(
        "egz,egc->gzc", key_product_upper, linear_value_rows, preferred_element_type=jnp.float32
    )
    recurrent_state = recurrent_state + jnp.einsum(
        "egz,egc->gzc", key_product_lower, linear_value_rows, preferred_element_type=jnp.float32
    )
    falling = jnp.exp(cumulated[:, -1])
    kv_here = soft_keys.shape[1]
    group = heads_here // kv_here
    block_index = lax.axis_index("seq")
    key_index = jnp.arange((REACH + 1) * row_count, dtype=jnp.int32)
    key_block = block_index - REACH + key_index // row_count
    causal = (key_index % row_count)[None, :] <= token_locations[:, None]
    visible = ((key_block[None, :] < block_index) | causal) & (key_block[None, :] >= window_start[0])
    normed, soft_out, lin_out = exclusive_scan(
        falling,
        recurrent_state,
        jnp.stack([soft_keys, soft_values]).transpose(0, 2, 1, 3),
        soft_queries.reshape(row_count, kv_here, group, head_width),
        jnp.where(visible, 0.0, -jnp.inf).astype(jnp.float32),
        linear_query_rows,
        lin_keys,
        linear_value_rows,
        cumulated,
        norm_gain,
        "seq",
    )
    lin_out = lin_out.transpose(1, 0, 2)
    soft_out = soft_out.reshape(row_count, heads_here, head_width)
    return (lin_out, soft_out)


def solution(mesh):
    placed = (
        P("seq", "head", None),
        P("seq", "head", None),
        P("seq", "head", None),
        P("head", "seq"),
        P("head", None),
        P("seq", "head", None),
        P("seq", "head", None),
        P("seq", "head", None),
        P("seq"),
    )
    return jax.shard_map(
        body,
        mesh=mesh,
        in_specs=placed,
        out_specs=(P("seq", "head", None), P("seq", "head", None)),
        check_vma=False,
    )
```

```python
import functools

import jax
import jax.numpy as jnp
from jax import lax
from jax.experimental import pallas as pl
from jax.experimental.pallas import tpu as pltpu
from jax.sharding import PartitionSpec as P

MESH = pl.DeviceIdType.MESH

DH = 128
HEADS = 64
REACH = 3


def scan_kernel(
    rounds,
    chunks,
    reach,
    fall_ref,
    state_ref,
    kv_ref,
    q_ref,
    bias_ref,
    lq_ref,
    lk_ref,
    lv_ref,
    cum_ref,
    gain_ref,
    out_ref,
    soft_ref,
    lin_ref,
    whole,
    whole_fall,
    out_fall,
    suffix,
    suffix_fall,
    got,
    got_fall,
    outgoing,
    outgoing_fall,
    send_sem,
    recv_sem,
    fsend_sem,
    frecv_sem,
    kv_got,
    kv_send,
    kv_recv,
    head_slots,
    head_send,
    head_recv,
    local_ref,
):
    me = lax.axis_index("seq")
    head = lax.axis_index("head")
    length = 2**rounds
    width = state_ref.shape[0] // chunks
    jump = 7
    back0, back1, near = rounds, rounds + 1, rounds + 2

    def ahead(dist):
        return 1 - (me + dist) // length

    def behind(dist):
        return (me - dist + length) // length

    far_recv = behind(jump)
    near_recv = behind(4) * (1 - far_recv)
    near_send = 1 - (me + length - 3) // length

    barrier = pltpu.get_barrier_semaphore()
    partners = 0
    distances = [2**k for k in range(rounds)] + list(range(1, reach + 1)) + [jump]
    for dist in sorted(set(distances)):
        partners = partners + ahead(dist) + behind(dist)

        @pl.when(ahead(dist) == 1)
        def _():
            pl.semaphore_signal(barrier, inc=1, device_id=(me + dist, head), device_id_type=MESH)

        @pl.when(behind(dist) == 1)
        def _():
            pl.semaphore_signal(barrier, inc=1, device_id=(me - dist, head), device_id_type=MESH)

    head_count = head_slots.shape[0]
    for other in range(head_count):

        @pl.when(other != head)
        def _():
            pl.semaphore_signal(barrier, inc=1, device_id=(me, other), device_id_type=MESH)

    pl.semaphore_wait(barrier, partners + head_count - 1)

    def kv_copy(dist, device):
        return pltpu.make_async_remote_copy(
            src_ref=kv_ref,
            dst_ref=kv_got.at[dist - 1],
            send_sem=kv_send.at[dist - 1],
            recv_sem=kv_recv.at[dist - 1],
            device_id=(device, head),
            device_id_type=MESH,
        )

    for dist in range(1, reach + 1):

        @pl.when(ahead(dist) == 1)
        def _():
            kv_copy(dist, me + dist).start()

    def state_copy(stage, source, c, device):
        rows = pl.ds(c * width, width)
        return pltpu.make_async_remote_copy(
            src_ref=source.at[rows],
            dst_ref=got.at[stage, rows],
            send_sem=send_sem.at[stage, c],
            recv_sem=recv_sem.at[stage, c],
            device_id=(device, head),
            device_id_type=MESH,
        )

    def fall_copy(stage, source, device):
        return pltpu.make_async_remote_copy(
            src_ref=source,
            dst_ref=got_fall.at[stage],
            send_sem=fsend_sem.at[stage],
            recv_sem=frecv_sem.at[stage],
            device_id=(device, head),
            device_id_type=MESH,
        )

    fall = jnp.broadcast_to(fall_ref[...], whole_fall.shape)
    outgoing_fall[0] = fall
    outgoing[0] = state_ref[...].astype(jnp.bfloat16)

    @pl.when(ahead(1) == 1)
    def _():
        fall_copy(0, outgoing_fall.at[0], me + 1).start()
        for c in range(chunks):
            state_copy(0, outgoing.at[0], c, me + 1).start()

    @pl.when(behind(1) == 1)
    def _():
        fall_copy(back0, outgoing_fall.at[0], me - 1).start()
        for c in range(chunks):
            state_copy(back0, outgoing.at[0], c, me - 1).start()

    whole[...] = state_ref[...]
    whole_fall[...] = fall
    suffix[...] = state_ref[...]
    suffix_fall[...] = fall
    out_ref[...] = jnp.zeros_like(out_ref)
    out_fall[...] = jnp.ones_like(out_fall)

    def forward_fall(stage, shift):
        @pl.when(behind(shift) == 1)
        def _():
            fall_copy(stage, outgoing_fall.at[stage], me - shift).wait_recv()
            arrived = got_fall[stage]
            out_fall[...] = arrived * out_fall[...]
            whole_fall[...] = arrived * whole_fall[...]

    def forward_chunk(stage, shift, c, update_whole=True):
        rows = pl.ds(c * width, width)

        @pl.when(behind(shift) == 1)
        def _():
            state_copy(stage, outgoing.at[stage], c, me - shift).wait_recv()
            arrived = got[stage, rows].astype(jnp.float32)
            out_ref[rows] = out_fall[rows][:, None, :] * arrived + out_ref[rows]
            if update_whole:
                whole[rows] = whole_fall[rows][:, None, :] * arrived + whole[rows]

    def backward_fall(stage, shift):
        @pl.when(ahead(shift) == 1)
        def _():
            fall_copy(stage, outgoing_fall.at[stage], me + shift).wait_recv()
            suffix_fall[...] = suffix_fall[...] * got_fall[stage]

    def backward_chunk(stage, shift, c):
        rows = pl.ds(c * width, width)

        @pl.when(ahead(shift) == 1)
        def _():
            state_copy(stage, outgoing.at[stage], c, me + shift).wait_recv()
            arrived = got[stage, rows].astype(jnp.float32)
            suffix[rows] = got_fall[stage][rows][:, None, :] * suffix[rows] + arrived

    def send_chunk(stage, flag, buffer, dist, c):
        rows = pl.ds(c * width, width)

        @pl.when(flag == 1)
        def _():
            outgoing[stage, rows] = buffer[rows].astype(jnp.bfloat16)
            state_copy(stage, outgoing.at[stage], c, me + dist).start()

    def send_fall(stage, flag, buffer_fall, dist):
        @pl.when(flag == 1)
        def _():
            outgoing_fall[stage] = buffer_fall[...]
            fall_copy(stage, outgoing_fall.at[stage], me + dist).start()

    backward_fall(back0, 1)
    send_fall(back1, behind(2), suffix_fall, -2)
    for c in range(chunks):
        forward_chunk(0, 1, c)
        send_chunk(1, ahead(2), whole, 2, c)
        backward_chunk(back0, 1, c)
        send_chunk(back1, behind(2), suffix, -2, c)
    forward_fall(0, 1)
    send_fall(1, ahead(2), whole_fall, 2)

    backward_fall(back1, 2)
    send_fall(2, ahead(jump), suffix_fall, jump)
    for c in range(chunks):
        forward_chunk(1, 2, c)
        send_chunk(near, near_send, whole, 4, c)
        backward_chunk(back1, 2, c)
        send_chunk(2, ahead(jump), suffix, jump, c)
    forward_fall(1, 2)
    send_fall(near, near_send, whole_fall, 4)

    for c in range(chunks):
        rows = pl.ds(c * width, width)
        for flag, dist, stage in ((far_recv, jump, 2), (near_recv, 4, near)):

            @pl.when(flag == 1)
            def _():
                state_copy(stage, outgoing.at[stage], c, me - dist).wait_recv()
                arrived = got[stage, rows].astype(jnp.float32)
                out_ref[rows] = out_fall[rows][:, None, :] * arrived + out_ref[rows]
                whole[rows] = whole_fall[rows][:, None, :] * arrived + whole[rows]

        if rounds > 3:
            send_chunk(3, ahead(8), whole, 8, c)

    for flag, dist, stage in ((far_recv, jump, 2), (near_recv, 4, near)):

        @pl.when(flag == 1)
        def _():
            fall_copy(stage, outgoing_fall.at[stage], me - dist).wait_recv()
            arrived = got_fall[stage]
            out_fall[...] = arrived * out_fall[...]
            whole_fall[...] = arrived * whole_fall[...]

    if rounds > 3:
        send_fall(3, ahead(8), whole_fall, 8)

    def local_part():
        cum = cum_ref[...]
        cum_col = jnp.transpose(cum)
        tokens = cum.shape[1]
        rows_at = lax.broadcasted_iota(jnp.int32, (tokens, tokens), 0)
        cols_at = lax.broadcasted_iota(jnp.int32, (tokens, tokens), 1)
        for h in range(cum.shape[0]):
            scores = lax.dot_general(
                lq_ref[:, h, :], lk_ref[:, h, :], (((1,), (1,)), ((), ())), preferred_element_type=jnp.float32
            )
            gap = jnp.where(rows_at >= cols_at, cum_col[:, h : h + 1] - cum[h : h + 1, :], -jnp.inf)
            weights = (scores * jnp.exp(gap)).astype(jnp.bfloat16)
            local_ref[h] = jnp.dot(weights, lv_ref[:, h, :], preferred_element_type=jnp.float32)

    def attention():
        for dist in range(1, reach + 1):

            @pl.when(behind(dist) == 1)
            def _():
                kv_copy(dist, me - dist).wait_recv()

            @pl.when(behind(dist) == 0)
            def _():
                kv_got[dist - 1] = jnp.zeros_like(kv_got.at[dist - 1])

            @pl.when(ahead(dist) == 1)
            def _():
                kv_copy(dist, me + dist).wait_send()

        tokens, groups, group = q_ref.shape[0], q_ref.shape[1], q_ref.shape[2]
        scale = float(q_ref.shape[3]) ** (-0.5)
        for g in range(groups):
            q = q_ref[:, g].astype(jnp.float32).reshape(tokens * group, -1).astype(jnp.bfloat16)
            keys = [kv_got[slot, 0, g] for slot in range(reach - 1, -1, -1)] + [kv_ref[0, g]]
            values = [kv_got[slot, 1, g] for slot in range(reach - 1, -1, -1)] + [kv_ref[1, g]]
            logits = jnp.concatenate(
                [
                    lax.dot_general(q, k, (((1,), (1,)), ((), ())), preferred_element_type=jnp.float32)
                    for k in keys
                ],
                axis=1,
            )
            masked = (logits * scale).reshape(tokens, group, -1) + bias_ref[...][:, None, :]
            top = jnp.max(masked, axis=-1, keepdims=True)
            exps = jnp.exp(masked - top)
            total = jnp.sum(exps, axis=-1, keepdims=True)
            probs = exps.reshape(tokens * group, -1).astype(jnp.bfloat16)
            summed = jnp.dot(probs, jnp.concatenate(values, axis=0), preferred_element_type=jnp.float32)
            soft_ref[:, g] = (summed.reshape(tokens, group, -1) / total).astype(soft_ref.dtype)

    for k in range(3, rounds):
        shift, last = 2**k, k == rounds - 1
        if last:
            attention()
            local_part()
        for c in range(chunks):
            forward_chunk(k, shift, c, update_whole=not last)
            if not last:
                rows = pl.ds(c * width, width)

                @pl.when(ahead(2 * shift) == 1)
                def _():
                    outgoing[k + 1, rows] = whole[rows].astype(jnp.bfloat16)
                    state_copy(k + 1, outgoing.at[k + 1], c, me + 2 * shift).start()

        @pl.when(behind(shift) == 1)
        def _():
            fall_copy(k, outgoing_fall.at[k], me - shift).wait_recv()
            arrived = got_fall[k]
            out_fall[...] = arrived * out_fall[...]
            if not last:
                whole_fall[...] = arrived * whole_fall[...]

        if not last:

            @pl.when(ahead(2 * shift) == 1)
            def _():
                outgoing_fall[k + 1] = whole_fall[...]
                fall_copy(k + 1, outgoing_fall.at[k + 1], me + 2 * shift).start()

    sends = [(0, 1, ahead(1)), (back0, -1, behind(1)), (1, 2, ahead(2)), (back1, -2, behind(2))]
    sends += [(2, jump, ahead(jump)), (near, 4, near_send)]
    sends += [(k, 2**k, ahead(2**k)) for k in range(3, rounds)]
    for stage, dist, flag in sends:

        @pl.when(flag == 1)
        def _():
            fall_copy(stage, outgoing_fall.at[stage], me + dist).wait_send()
            for c in range(chunks):
                state_copy(stage, outgoing.at[stage], c, me + dist).wait_send()

    prior = out_ref[...]
    upper = prior.astype(jnp.bfloat16)
    lower = (prior - upper.astype(jnp.float32)).astype(jnp.bfloat16)
    parts = []
    for h in range(prior.shape[0]):
        query = lq_ref[:, h, :]
        part = jnp.dot(query, upper[h], preferred_element_type=jnp.float32)
        parts.append(part + jnp.dot(query, lower[h], preferred_element_type=jnp.float32))
    carried = jnp.stack(parts)
    grow = jnp.transpose(jnp.exp(cum_ref[...]))
    mixed = local_ref[...] + jnp.stack([grow[:, h : h + 1] for h in range(grow.shape[1])]) * carried
    column = jnp.sum(jnp.sum(mixed * mixed, axis=0), axis=1, keepdims=True)
    head_slots[head] = jnp.transpose(jnp.broadcast_to(column, (column.shape[0], 128)))[0:1, :]

    def head_copy(other, slot):
        return pltpu.make_async_remote_copy(
            src_ref=head_slots.at[head],
            dst_ref=head_slots.at[slot],
            send_sem=head_send.at[other],
            recv_sem=head_recv.at[slot],
            device_id=(me, other),
            device_id_type=MESH,
        )

    for other in range(head_count):

        @pl.when(other != head)
        def _():
            head_copy(other, head).start()

    for other in range(head_count):

        @pl.when(other != head)
        def _():
            head_copy(other, other).wait_recv()
            head_copy(other, head).wait_send()

    total = head_slots[0]
    for other in range(1, head_count):
        total = total + head_slots[other]
    heads_all, width_all = lq_ref.shape[1] * head_count, lq_ref.shape[2]
    scale_row = lax.rsqrt(total / (heads_all * width_all) + 1e-06)
    scale = jnp.transpose(jnp.broadcast_to(scale_row, (128, scale_row.shape[1])))[:, 0:1]
    gain = gain_ref[...].astype(jnp.float32)
    lin_ref[...] = (mixed * scale[None] * gain[:, None, :]).astype(lin_ref.dtype)


def exclusive_scan(falling, state, kv, queries, bias, lq, lk, lv, cum, gain, axis):
    length = lax.axis_size(axis)
    rounds = length.bit_length() - 1
    stages = rounds + 3
    chunks = 8
    heads, rows, columns = state.shape
    fall_rows = falling[:, None]
    vmem = pl.BlockSpec(memory_space=pltpu.VMEM)
    return pl.pallas_call(
        functools.partial(scan_kernel, rounds, chunks, REACH),
        out_shape=(
            jax.ShapeDtypeStruct(state.shape, jnp.float32),
            jax.ShapeDtypeStruct(queries.shape, queries.dtype),
            jax.ShapeDtypeStruct(state.shape, jnp.bfloat16),
        ),
        in_specs=[vmem] * 10,
        out_specs=(vmem, vmem, vmem),
        scratch_shapes=[
            pltpu.VMEM(state.shape, jnp.float32),
            pltpu.VMEM((heads, columns), jnp.float32),
            pltpu.VMEM((heads, columns), jnp.float32),
            pltpu.VMEM(state.shape, jnp.float32),
            pltpu.VMEM((heads, columns), jnp.float32),
            pltpu.VMEM((stages,) + state.shape, jnp.bfloat16),
            pltpu.VMEM((stages, heads, columns), jnp.float32),
            pltpu.VMEM((stages,) + state.shape, jnp.bfloat16),
            pltpu.VMEM((stages, heads, columns), jnp.float32),
            pltpu.SemaphoreType.DMA((stages, chunks)),
            pltpu.SemaphoreType.DMA((stages, chunks)),
            pltpu.SemaphoreType.DMA((stages,)),
            pltpu.SemaphoreType.DMA((stages,)),
            pltpu.VMEM((REACH,) + kv.shape, kv.dtype),
            pltpu.SemaphoreType.DMA((REACH,)),
            pltpu.SemaphoreType.DMA((REACH,)),
            pltpu.VMEM((lax.axis_size("head"), 1, columns), jnp.float32),
            pltpu.SemaphoreType.DMA((lax.axis_size("head"),)),
            pltpu.SemaphoreType.DMA((lax.axis_size("head"),)),
            pltpu.VMEM(state.shape, jnp.float32),
        ],
        compiler_params=pltpu.CompilerParams(collective_id=0, has_side_effects=True),
    )(fall_rows, state, kv, queries, bias, lq, lk, lv, cum, gain)


def head_sum_kernel(count, value_ref, out_ref, slots, send_sem, recv_sem):
    me = lax.axis_index("seq")
    head = lax.axis_index("head")
    barrier = pltpu.get_barrier_semaphore()
    for other in range(count):

        @pl.when(other != head)
        def _():
            pl.semaphore_signal(barrier, inc=1, device_id=(me, other), device_id_type=MESH)

    pl.semaphore_wait(barrier, count - 1)
    slots[head] = value_ref[...]

    def copy(other, slot):
        return pltpu.make_async_remote_copy(
            src_ref=value_ref,
            dst_ref=slots.at[slot],
            send_sem=send_sem.at[other],
            recv_sem=recv_sem.at[slot],
            device_id=(me, other),
            device_id_type=MESH,
        )

    for other in range(count):

        @pl.when(other != head)
        def _():
            copy(other, head).start()

    for other in range(count):

        @pl.when(other != head)
        def _():
            copy(other, other).wait_recv()
            copy(other, head).wait_send()

    total = slots[0]
    for other in range(1, count):
        total = total + slots[other]
    out_ref[...] = total


def head_sum(value, axis):
    count = lax.axis_size(axis)
    vmem = pl.BlockSpec(memory_space=pltpu.VMEM)
    row = value.reshape(1, -1)
    return pl.pallas_call(
        functools.partial(head_sum_kernel, count),
        out_shape=jax.ShapeDtypeStruct(row.shape, row.dtype),
        in_specs=[vmem],
        out_specs=vmem,
        scratch_shapes=[
            pltpu.VMEM((count,) + row.shape, row.dtype),
            pltpu.SemaphoreType.DMA((count,)),
            pltpu.SemaphoreType.DMA((count,)),
        ],
        compiler_params=pltpu.CompilerParams(collective_id=1, has_side_effects=True),
    )(row).reshape(value.shape)


def from_behind(value, axis, steps):
    count = lax.axis_size(axis)
    first, last = (max(0, -steps), min(count, count - steps))
    return lax.ppermute(value, axis, [(source, source + steps) for source in range(first, last)])


def combine_states(earlier, later):
    return (earlier[0] * later[0], later[0][:, None, None] * earlier[1] + later[1])


def split_parts(matrix):
    upper = matrix.astype(jnp.bfloat16)
    lower = (matrix - upper.astype(jnp.float32)).astype(jnp.bfloat16)
    return (upper, lower)


def attend(carried_over_state, query_rows, key_rows, value_rows, visible, score_scale):
    running_max, running_sum, accumulated = carried_over_state
    attention_logits = (
        jnp.einsum("cphm,npm->phcn", query_rows, key_rows, preferred_element_type=jnp.float32)
        * score_scale
    )
    masked = jnp.where(visible, attention_logits, -jnp.inf)
    new_max = jnp.maximum(running_max, jnp.max(masked, axis=-1))
    power_exponent = jnp.exp(masked - new_max[..., None])
    fading = jnp.exp(running_max - new_max)
    new_sum = running_sum * fading + jnp.sum(power_exponent, axis=-1)
    product = jnp.einsum(
        "qyjl,lqu->qyju",
        power_exponent.astype(jnp.bfloat16),
        value_rows,
        preferred_element_type=jnp.float32,
    )
    return (new_max, new_sum, accumulated * fading[..., None] + product)


def body(
    linear_query_rows,
    lin_keys,
    linear_value_rows,
    log_decay,
    norm_gain,
    soft_queries,
    soft_keys,
    soft_values,
    window_start,
):
    row_count, heads_here, head_width = linear_query_rows.shape
    cumulated = jnp.cumsum(log_decay, axis=1)
    token_locations = jnp.arange(row_count, dtype=jnp.int32)
    lower_mask = token_locations[:, None] >= token_locations[None, :]
    tail = jnp.exp(cumulated[:, -1:] - cumulated)
    key_product = lin_keys.astype(jnp.float32) * tail.T[:, :, None]
    key_product_upper, key_product_lower = split_parts(key_product)
    recurrent_state = jnp.einsum(
        "egz,egc->gzc", key_product_upper, linear_value_rows, preferred_element_type=jnp.float32
    )
    recurrent_state = recurrent_state + jnp.einsum(
        "egz,egc->gzc", key_product_lower, linear_value_rows, preferred_element_type=jnp.float32
    )
    falling = jnp.exp(cumulated[:, -1])
    kv_here = soft_keys.shape[1]
    group = heads_here // kv_here
    block_index = lax.axis_index("seq")
    key_index = jnp.arange((REACH + 1) * row_count, dtype=jnp.int32)
    key_block = block_index - REACH + key_index // row_count
    causal = (key_index % row_count)[None, :] <= token_locations[:, None]
    visible = ((key_block[None, :] < block_index) | causal) & (key_block[None, :] >= window_start[0])
    normed, soft_out, lin_out = exclusive_scan(
        falling,
        recurrent_state,
        jnp.stack([soft_keys, soft_values]).transpose(0, 2, 1, 3),
        soft_queries.reshape(row_count, kv_here, group, head_width),
        jnp.where(visible, 0.0, -jnp.inf).astype(jnp.float32),
        linear_query_rows,
        lin_keys,
        linear_value_rows,
        cumulated,
        norm_gain,
        "seq",
    )
    lin_out = lin_out.transpose(1, 0, 2)
    soft_out = soft_out.reshape(row_count, heads_here, head_width)
    return (lin_out, soft_out)


def solution(mesh):
    placed = (
        P("seq", "head", None),
        P("seq", "head", None),
        P("seq", "head", None),
        P("head", "seq"),
        P("head", None),
        P("seq", "head", None),
        P("seq", "head", None),
        P("seq", "head", None),
        P("seq"),
    )
    return jax.shard_map(
        body,
        mesh=mesh,
        in_specs=placed,
        out_specs=(P("seq", "head", None), P("seq", "head", None)),
        check_vma=False,
    )
```
